256 devices in a mesh: tile: 32 (over z_hi, x, core), grp: 8 (over z_lo, y).
Axes of the slice: x: 4, y: 4, z: 8 (z_hi: 4, z_lo: 2; z = z_hi * 2 + z_lo), core: 2. Of those that a mesh axis runs over, the one named last changes fastest.
Arguments:
- traces: float32 [1024, 16, 1500], P(('tile', 'grp')), may hold values from -6 to 6
- validity: int32 [1024, 16], P(('tile', 'grp')), may hold values 0 or 1
- boundary_rows: int32 [256, 2, 4], P(('tile', 'grp')), may hold values from 0 to 3, as said below
- boundary_count: int32 [256, 2], P(('tile', 'grp')), may hold values from 1 to 4, as said below
- pair_mask: int32 [1024, 96], P(('tile', 'grp')), may hold values from 0 to 1, as said below
Outputs:
- correlations: bfloat16 [1024, 96, 2001], P(('tile', 'grp'))
The draws below stay inside these ranges and needn't reach their ends.
Inputs may be any that keep to these rules, and one draw needn't show every extreme that they name: `boundary_rows`: each device's list in each direction orders all of its 4 local stations, each once. `boundary_count`: in every draw some device sends all 4 of its stations in each direction. `pair_mask`: a station's column for itself is 0.
All inputs are finite; a program needn't handle non-finite values. No bound on the sum of `validity` on one device may be relied on, other than what follows from the above.
Results may differ from the reference program's by a relative error of at most 0.008.
Values may be sent and summed in bfloat16 or wider, within the bound.
A program may use at most 64 MiB of HBM per device.

```python
import math
import jax
import jax.numpy as jnp
from jax import lax

SG = 4
SEG = 16
SAMP = 1500
NBIN = 144
MAXLAG = 1000
LAGS = 2001
TILE_ST = 32
COLS = 96
STATIONS = 1024
N_TILE = 32
N_GRP = 8


def draw_boundary_rows(key, part):
    devices_all = N_TILE * N_GRP
    key_list = jax.random.split(key, devices_all * 2)
    orders = jax.vmap(lambda one_key: jax.random.permutation(one_key, SG))(key_list)
    return orders.reshape(devices_all, 2, SG).astype(jnp.int32)


def draw_boundary_count(key, part):
    devices_all = N_TILE * N_GRP
    counts_drawn = jax.random.randint(key, (devices_all, 2), 1, SG + 1)
    fullest = jax.random.randint(jax.random.fold_in(key, 7), (2,), 0, devices_all)
    device_number = jnp.arange(devices_all, dtype=jnp.int32)[:, None]
    return jnp.where(device_number == fullest[None, :], SG, counts_drawn).astype(jnp.int32)


def draw_pair_mask(key, part):
    flags = jax.random.randint(key, (STATIONS, COLS), 0, 4)
    station_number = jnp.arange(STATIONS, dtype=jnp.int32)[:, None]
    group_number = station_number % (SG * N_GRP) // SG
    self_column = group_number * 3 * SG + station_number % SG
    column_number = jnp.arange(COLS, dtype=jnp.int32)[None, :]
    keep = (flags > 0) & (column_number != self_column)
    return keep.astype(jnp.int32)


def set_ends(array, rng, smallest, top_value):
    dims = array.shape
    place = [jax.random.randint(jax.random.fold_in(rng, axis), (), 0, dims[axis]) for axis in range(len(dims))]
    array = array.at[tuple(place)].set(smallest)
    longest = dims.index(max(dims))
    place[longest] = (place[longest] + 1) % dims[longest]
    return array.at[tuple(place)].set(top_value)


def level_of(key, dims, cuts, smallest, largest):
    def one(axis_at, shards_of):
        steps = jax.random.uniform(jax.random.fold_in(jax.random.fold_in(key, 6), axis_at), (shards_of,), jnp.float32, smallest / len(cuts), largest / len(cuts))
        return jnp.repeat(jnp.exp(steps), dims[axis_at] // shards_of).reshape((-1,) + (1,) * (len(dims) - axis_at - 1))

    loudness = one(*cuts[0])
    for cut in cuts[1:]:
        loudness = loudness * one(*cut)
    return loudness


def normal_values(own_key, extent, deviation, most, pieces=(), kind=jnp.bfloat16):
    factor_of = level_of(own_key, extent, pieces, -0.22, 0.18) if pieces else 1.0
    values = jax.random.normal(own_key, extent, jnp.float32) * deviation * factor_of
    return jnp.minimum(jnp.maximum(values, -most), most).astype(kind)


def setup_inputs(seed: int = 0) -> dict:
    streams_of = jax.random.split(jax.random.key(seed), 6)
    return {
        "traces": normal_values(streams_of[0], (STATIONS, SEG, SAMP), 1.0, 6.0, ((0, 256),), jnp.float32),
        "validity": set_ends((jax.random.randint(streams_of[1], (STATIONS, SEG), 0, 5) < 3).astype(jnp.int32), jax.random.fold_in(streams_of[1], 1), 0, 1),
        "boundary_rows": draw_boundary_rows(jax.random.fold_in(streams_of[5], 71), 0),
        "boundary_count": draw_boundary_count(jax.random.fold_in(streams_of[5], 71), 0),
        "pair_mask": draw_pair_mask(jax.random.fold_in(streams_of[5], 71), 0),
    }


def whiten_all(traces, valid_float):
    sample_number = jnp.arange(SAMP, dtype=jnp.float32)
    hann_taper = 0.5 - 0.5 * jnp.cos(sample_number * (2.0 * jnp.pi / SAMP))
    spectrum = jnp.fft.rfft(traces * hann_taper, n=2 * SAMP, axis=-1)[..., 1:NBIN + 1]
    real_part = jnp.real(spectrum)
    imag_part = jnp.imag(spectrum)
    power_bins = real_part * real_part + imag_part * imag_part
    padded = jnp.pad(power_bins, ((0, 0), (0, 0), (4, 4)))
    smooth = sum((padded[:, :, offset:offset + NBIN] for offset in range(9))) / 9.0
    mean_power = lax.optimization_barrier(jnp.mean(power_bins, axis=2, keepdims=True))
    factor = valid_float[:, :, None] / jnp.sqrt(0.5 * smooth + 0.5 * mean_power + 1e-06)
    return jnp.stack([real_part * factor, imag_part * factor], axis=2).astype(jnp.bfloat16)

def reference(traces, validity, boundary_rows, boundary_count, pair_mask):
    valid_float = validity.astype(jnp.float32)
    spectra = whiten_all(traces, valid_float)
    spec_grid = spectra.reshape(N_TILE, N_GRP, SG, SEG, 2, NBIN)
    valid_grid = valid_float.reshape(N_TILE, N_GRP, SG, SEG)
    list_grid = boundary_rows.reshape(N_TILE, N_GRP, 2, SG).astype(jnp.int32)
    count_grid = boundary_count.reshape(N_TILE, N_GRP, 2)
    live_grid = (jnp.arange(SG, dtype=jnp.int32)[None, None, None, :] < count_grid[..., None]).astype(jnp.float32)

    def picked(direction):
        chosen = list_grid[:, :, direction]
        live_now = live_grid[:, :, direction]
        spec_sel = jnp.take_along_axis(spec_grid, chosen[:, :, :, None, None, None], axis=2)
        spec_sel = (spec_sel.astype(jnp.float32) * live_now[:, :, :, None, None, None]).astype(jnp.bfloat16)
        valid_sel = jnp.take_along_axis(valid_grid, chosen[:, :, :, None], axis=2) * live_now[:, :, :, None]
        return (spec_sel, valid_sel)
    sent_up, valid_up = picked(0)
    sent_down, valid_down = picked(1)
    below_spec = jnp.concatenate([jnp.zeros_like(sent_up[:1]), sent_up[:-1]], axis=0)
    below_valid = jnp.concatenate([jnp.zeros_like(valid_up[:1]), valid_up[:-1]], axis=0)
    above_spec = jnp.concatenate([sent_down[1:], jnp.zeros_like(sent_down[:1])], axis=0)
    above_valid = jnp.concatenate([valid_down[1:], jnp.zeros_like(valid_down[:1])], axis=0)
    column_spec = jnp.concatenate([spec_grid, below_spec, above_spec], axis=2).reshape(N_TILE, COLS, SEG, 2, NBIN)
    column_valid = jnp.concatenate([valid_grid, below_valid, above_valid], axis=2).reshape(N_TILE, COLS, SEG)
    own_spec = spectra.reshape(N_TILE, TILE_ST, SEG, 2, NBIN)
    own_valid = valid_float.reshape(N_TILE, TILE_ST, SEG)
    mask_grid = pair_mask.astype(jnp.float32).reshape(N_TILE, TILE_ST, COLS)
    lag_number = jnp.mod(jnp.arange(LAGS, dtype=jnp.int32) - MAXLAG, 2 * SAMP)

    def per_tile(inputs):
        left_spec, left_valid, right_spec, right_valid, mask_tile = inputs
        left_real = left_spec[:, :, 0].astype(jnp.float32)
        left_imag = left_spec[:, :, 1].astype(jnp.float32)
        right_real = right_spec[:, :, 0].astype(jnp.float32)
        right_imag = right_spec[:, :, 1].astype(jnp.float32)
        cross_real = jnp.einsum('iqf,jqf->ijf', left_real, right_real) + jnp.einsum('iqf,jqf->ijf', left_imag, right_imag)
        cross_imag = jnp.einsum('iqf,jqf->ijf', left_imag, right_real) - jnp.einsum('iqf,jqf->ijf', left_real, right_imag)
        pair_count = jnp.einsum('iq,jq->ij', left_valid, right_valid)
        divisor = jnp.maximum(pair_count, 1.0)[:, :, None]
        cross_real = (cross_real / divisor).astype(jnp.bfloat16).astype(jnp.float32)
        cross_imag = (cross_imag / divisor).astype(jnp.bfloat16).astype(jnp.float32)
        bins_full = cross_real + 1j * cross_imag
        bins_full = jnp.pad(bins_full, ((0, 0), (0, 0), (1, SAMP - NBIN)))
        series = jnp.fft.irfft(bins_full, n=2 * SAMP, axis=-1) * SAMP
        chosen_lags = jnp.take(series, lag_number, axis=-1)
        return (chosen_lags / math.sqrt(NBIN) * mask_tile[:, :, None]).astype(jnp.bfloat16)
    result = lax.map(per_tile, (own_spec, own_valid, column_spec, column_valid, mask_grid))
    return result.reshape(STATIONS, COLS, LAGS)
```

```python
import functools
import math

import jax
import jax.numpy as jnp
import ml_dtypes
import numpy as np
from jax import lax
from jax.experimental import pallas as pl
from jax.experimental.pallas import tpu as pltpu
from jax.sharding import PartitionSpec as P

SG = 4
SEG = 16
SAMP = 1500
NBIN = 144
MAXLAG = 1000
LAGS = 2001
NGRP = 8
MAIN = 128
ROWS = SG * SEG
BLK = ROWS + 16
CHUNK = 512
BF = jnp.bfloat16
F32 = jnp.float32
MESH = pl.DeviceIdType.MESH


def split_halves(table):
    high = table.astype(ml_dtypes.bfloat16)
    low = (table - high.astype(np.float64)).astype(ml_dtypes.bfloat16)
    return high, low


def dft_table():
    n = np.arange(SAMP, dtype=np.int64)[:, None]
    k = np.arange(1, NBIN + 1, dtype=np.int64)[None, :]
    angle = ((n * k) % (2 * SAMP)).astype(np.float64) * (2.0 * np.pi / (2 * SAMP))
    taper = 0.5 - 0.5 * np.cos(2.0 * np.pi * n / SAMP)
    cos, sin = taper * np.cos(angle), -taper * np.sin(angle)
    main = np.concatenate([cos[:, :MAIN], sin[:, :MAIN]], axis=1)
    rest = np.tile(np.concatenate([cos[:, MAIN:], sin[:, MAIN:]], axis=1), (1, 4))
    main_high, main_low = split_halves(main)
    rest_high, rest_low = split_halves(rest)
    return np.concatenate([main_high, main_low, rest_high, rest_low], axis=1)


def lag_table():
    k = np.arange(1, NBIN + 1, dtype=np.int64)[:, None]
    lag = np.arange(LAGS, dtype=np.int64)[None, :] - MAXLAG
    angle = ((k * lag) % (2 * SAMP)).astype(np.float64) * (2.0 * np.pi / (2 * SAMP))
    cos = np.cos(angle) / math.sqrt(NBIN)
    sin = -np.sin(angle) / math.sqrt(NBIN)
    table = np.concatenate([cos[:MAIN], sin[:MAIN], cos[MAIN:], sin[MAIN:]], axis=0)
    return table.astype(ml_dtypes.bfloat16)


def small_tables():
    lane = np.arange(256)
    bin_of = np.where(lane < MAIN, lane + 1, MAIN + 1 + (lane - MAIN) % 16)
    counted = lane < MAIN + 32
    near = np.abs(bin_of[:, None] - bin_of[None, :]) <= 4
    weights = np.where(counted[:, None], np.where(near, 17.0, 1.0), 0.0)
    order = np.zeros((BLK, 256))
    for s in range(SG):
        for q in range(SEG):
            order[q * SG + s, s * SEG + q] = 1.0
            order[ROWS + (q % 4) * SG + s, s * SEG + q] = 1.0
    spread = np.zeros((SG * BLK, 256))
    for s in range(SG):
        for row in range(BLK):
            spread[s * BLK + row, row // SG * SG + s] = 1.0
    return np.concatenate([weights, order, spread], axis=0).astype(ml_dtypes.bfloat16)


def iota(shape, axis):
    return lax.broadcasted_iota(jnp.int32, shape, axis)


def dot(a, b):
    return jnp.dot(a, b, preferred_element_type=F32)


def lane_fold(a, shifts):
    for shift in shifts:
        a = a + pltpu.roll(a, shift, 1)
    return a


def cross_kernel(
    n_tile, x_hbm, val_hbm, rows_hbm, cnt_hbm, dft_hbm, small_hbm, f_ref,
    x_v, val_v, rows_s, cnt_s, dft_v, small_v, blk, up_down, gath, nbin, role, turned,
    out2, in2, load_sem, send_g, send_n, send_p, recv_g, recv_n, recv_p,
):
    tile, me = lax.axis_index("tile"), lax.axis_index("grp")
    z_me, y_me = me // 4, lax.rem(me, 4)
    up = lax.rem(tile + 1, n_tile)
    down = lax.rem(tile + n_tile - 1, n_tile)

    loads = [
        pltpu.make_async_copy(src, dst, load_sem.at[i])
        for i, (src, dst) in enumerate(
            [(x_hbm, x_v), (dft_hbm, dft_v), (val_hbm, val_v), (small_hbm, small_v),
             (rows_hbm, rows_s), (cnt_hbm, cnt_s)]
        )
    ]
    for load in loads:
        load.start()

    def other(d):
        return lax.rem(z_me + d // 4, 2) * 4 + lax.rem(y_me + lax.rem(d, 4), 4)

    barrier = pltpu.get_barrier_semaphore()
    for d in range(1, NGRP):
        pl.semaphore_signal(barrier, inc=1, device_id=(tile, other(d)), device_id_type=MESH)
    pl.semaphore_signal(barrier, inc=1, device_id=(up, me), device_id_type=MESH)
    pl.semaphore_signal(barrier, inc=1, device_id=(down, me), device_id_type=MESH)

    loads[2].wait()
    lane_group = iota((ROWS, 128), 1) // 32
    same_group = lane_group == (lax.rem(iota((ROWS, 128), 0), SEG) // 4)
    valid_parts = []
    for s in range(SG):
        row = jnp.broadcast_to(val_v[s : s + 1, :].astype(F32), (SEG, SEG))
        diag = jnp.where(iota((SEG, SEG), 0) == iota((SEG, SEG), 1), row, 0.0)
        valid_parts.append(jnp.sum(diag, axis=1, keepdims=True))
    valid = jnp.broadcast_to(jnp.concatenate(valid_parts, axis=0), (ROWS, 128))

    loads[0].wait()
    x = x_v[...].reshape(ROWS, SAMP)
    x_high = x.astype(BF)
    x_low = (x - x_high.astype(F32)).astype(BF)
    loads[1].wait()
    both = dot(jnp.concatenate([x_high, x_low], axis=0), dft_v[...])
    main = both[:ROWS, :256] + (both[ROWS:, :256] + both[:ROWS, 256:512])
    rest = both[:ROWS, 512:640] + (both[ROWS:, 512:640] + both[:ROWS, 640:768])
    real, imag = main[:, :MAIN], main[:, MAIN:]
    power = jnp.concatenate([real * real + imag * imag, rest * rest], axis=1)
    power_high = power.astype(BF)
    power_low = (power - power_high.astype(F32)).astype(BF)
    loads[3].wait()
    level = dot(jnp.concatenate([power_high, power_low], axis=0), small_v[0:256, :])
    level = (level[:ROWS] + level[ROWS:]) * (1.0 / 288.0) + 1e-06
    factor = lax.rsqrt(level)
    factor_main = factor[:, :MAIN] * valid
    factor_rest = jnp.where(same_group, factor[:, MAIN:] * valid, 0.0)
    white = jnp.concatenate([real * factor_main, imag * factor_main], axis=1).astype(BF)
    white_rest = jnp.concatenate(
        [rest * factor_rest, jnp.where(same_group, valid, 0.0)], axis=1
    ).astype(BF)
    blk[0:ROWS, :] = dot(small_v[256 : 256 + ROWS, 0:ROWS], white).astype(BF)
    blk[ROWS:BLK, :] = dot(small_v[256 + ROWS : 256 + BLK, 0:ROWS], white_rest).astype(BF)

    pl.semaphore_wait(barrier, NGRP + 1)

    def gather_copy(d):
        return pltpu.make_async_remote_copy(
            src_ref=blk, dst_ref=gath.at[me], send_sem=send_g.at[d - 1], recv_sem=recv_g.at[me],
            device_id=(tile, other(d)), device_id_type=MESH,
        )

    for d in range(1, NGRP):
        gather_copy(d).start()

    own = blk[...]
    gath[me] = own
    loads[4].wait()
    loads[5].wait()
    within = lax.rem(iota((BLK, BLK), 0), SG)
    same_four = (iota((BLK, BLK), 0) // SG) == (iota((BLK, BLK), 1) // SG)
    column = lax.rem(iota((BLK, BLK), 1), SG)
    neighbour = (up, down)

    def edge_copy(direction):
        return pltpu.make_async_remote_copy(
            src_ref=up_down.at[direction], dst_ref=nbin.at[direction],
            send_sem=send_n.at[direction], recv_sem=recv_n.at[direction],
            device_id=(neighbour[direction], me), device_id_type=MESH,
        )

    for direction in range(2):
        wanted = jnp.full((BLK, BLK), rows_s[0, direction, SG - 1], jnp.int32)
        for h in range(SG - 1):
            wanted = jnp.where(within == h, rows_s[0, direction, h], wanted)
        live = within < cnt_s[0, direction]
        pick = jnp.where(same_four & live & (column == wanted), 1.0, 0.0).astype(BF)
        up_down[direction] = dot(pick, own).astype(BF)
        edge_copy(direction).start()

    spread = small_v[256 + BLK : 256 + BLK + SG * BLK, 0:BLK]
    lane = iota((16, 128), 1)
    first_half = lax.rem(lane, 32) < 16

    def set_role(first, block, keep):
        wide = dot(spread, block)
        if keep is not None:
            wide = wide * keep
        for s in range(SG):
            part = wide[s * BLK : (s + 1) * BLK]
            role[first + s] = part
            tail = part[ROWS:, :128]
            turned[first + s] = jnp.where(
                first_half, pltpu.roll(tail, 112, 1), -pltpu.roll(tail, 16, 1)
            )

    set_role(0, own, None)
    for direction in range(2):
        edge_copy(direction).wait_recv()
        inside = (tile > 0) if direction == 0 else (tile < n_tile - 1)
        set_role(SG + direction * SG, nbin[direction], jnp.where(inside, 1.0, 0.0))

    sub = iota((8, 128), 0)
    low_half = sub < 4
    rest_real = lax.rem(iota((8, 128), 1), 32) < 16

    def products(j, block):
        w_re, w_im = role[j, 0:ROWS, 0:128], role[j, 0:ROWS, 128:256]
        w_rest, w_val = role[j, ROWS:BLK, 0:128], role[j, ROWS:BLK, 128:256]
        v_re, v_im = block[0:ROWS, 0:128], block[0:ROWS, 128:256]
        v_rest, v_val = block[ROWS:BLK, 0:128], block[ROWS:BLK, 128:256]
        return [
            jnp.sum(a.reshape(-1, 8, 128), axis=0)
            for a in (
                w_re * v_re + w_im * v_im,
                w_im * v_re - w_re * v_im,
                w_rest * v_rest,
                turned[j] * v_rest,
                w_val * v_val,
            )
        ]

    def finish(sums, sign):
        re, im, rest_re, rest_im, count = sums
        count = lane_fold(count, (64, 32))
        inverse = 1.0 / jnp.maximum(count, 1.0)
        rest_re = lane_fold(rest_re, (64, 32, 16))
        rest_im = lane_fold(rest_im, (64, 32, 16)) * sign
        return re * inverse, im * (inverse * sign), jnp.where(rest_real, rest_re, rest_im) * inverse

    def result_copy(d):
        return pltpu.make_async_remote_copy(
            src_ref=out2.at[d], dst_ref=in2.at[me], send_sem=send_p.at[d],
            recv_sem=recv_p.at[me], device_id=(tile, other(d)), device_id_type=MESH,
        )

    def recv_wait(buffer, sems, g):
        pltpu.make_async_copy(buffer.at[g], buffer.at[g], sems.at[g]).wait()

    def boundary(d, carry):
        g = other(d)

        @pl.when(d > 0)
        def _():
            recv_wait(gath, recv_g, g)

        block = gath[g].astype(F32)
        for pair in range(4):
            a = products(SG + 2 * pair, block)
            b = products(SG + 2 * pair + 1, block)
            both = [
                jnp.where(low_half, p, q) + pltpu.roll(jnp.where(low_half, q, p), 4, 0)
                for p, q in zip(a, b)
            ]
            done = finish(both, -1.0)
            for i in range(3):
                out2[d, 8 * pair : 8 * pair + 8, 128 * i : 128 * i + 128] = done[i].astype(BF)

        @pl.when(d > 0)
        def _():
            result_copy(d).start()

        return carry

    lax.fori_loop(0, NGRP, boundary, 0)

    def inner(d, carry):
        g = other(d)
        block = gath[g].astype(F32)
        for s in range(SG):
            sums = [a + pltpu.roll(a, 4, 0) for a in products(s, block)]
            done = finish(sums, 1.0)
            for i in range(3):
                f_ref[i, pl.ds(g * 48 + s, 4, stride=4), :] = done[i][0:4]
        return carry

    lax.fori_loop(0, NGRP, inner, 0)

    def collect(d, carry):
        g = other(d)

        @pl.when(d > 0)
        def _():
            recv_wait(in2, recv_p, g)
            start = pl.multiple_of(g * 48 + 16, 8)
            for i in range(3):
                f_ref[i, pl.ds(start, 32), :] = in2[g, :, 128 * i : 128 * i + 128].astype(F32)

        return carry

    lax.fori_loop(0, NGRP, collect, 0)
    start = pl.multiple_of(me * 48 + 16, 8)
    for i in range(3):
        f_ref[i, pl.ds(start, 32), :] = out2[0, :, 128 * i : 128 * i + 128].astype(F32)
    for d in range(1, NGRP):
        gather_copy(d).wait_send()
        result_copy(d).wait_send()
    for direction in range(2):
        edge_copy(direction).wait_send()


def lag_kernel(f_ref, mask_ref, basis_ref, out_ref, left):
    @pl.when(pl.program_id(0) == 0)
    def _():
        for s in range(SG):
            row = jnp.broadcast_to(mask_ref[s : s + 1, :].astype(F32), (96, 96))
            diag = jnp.where(iota((96, 96), 0) == iota((96, 96), 1), row, 0.0)
            keep = jnp.sum(diag, axis=1, keepdims=True)
            for i in range(3):
                rows = f_ref[i, pl.ds(s, 96, stride=4), :] * keep
                left[s * 96 : (s + 1) * 96, 128 * i : 128 * i + 128] = rows.astype(BF)

    series = dot(left[:, 0 : 2 * NBIN], basis_ref[...])
    out_ref[...] = series.reshape(SG, 96, CHUNK).astype(BF)


def on_device(n_tile, traces, validity, boundary_rows, boundary_count, pair_mask):
    dft = jnp.asarray(dft_table())
    small = jnp.asarray(small_tables())
    anywhere = pl.BlockSpec(memory_space=pltpu.MemorySpace.HBM)
    dma = pltpu.SemaphoreType.DMA
    cross = pl.pallas_call(
        functools.partial(cross_kernel, n_tile),
        out_shape=jax.ShapeDtypeStruct((3, SG * 96, 128), F32),
        in_specs=[anywhere] * 6,
        out_specs=pl.BlockSpec(memory_space=pltpu.VMEM),
        scratch_shapes=[
            pltpu.VMEM((SG, SEG, SAMP), F32),
            pltpu.VMEM((SG, SEG), jnp.int32),
            pltpu.SMEM((1, 2, SG), jnp.int32),
            pltpu.SMEM((1, 2), jnp.int32),
            pltpu.VMEM(dft.shape, BF),
            pltpu.VMEM(small.shape, BF),
            pltpu.VMEM((BLK, 256), BF),
            pltpu.VMEM((2, BLK, 256), BF),
            pltpu.VMEM((NGRP, BLK, 256), BF),
            pltpu.VMEM((2, BLK, 256), BF),
            pltpu.VMEM((12, BLK, 256), F32),
            pltpu.VMEM((12, 16, 128), F32),
            pltpu.VMEM((NGRP, 32, 384), BF),
            pltpu.VMEM((NGRP, 32, 384), BF),
            dma((6,)), dma((7,)), dma((2,)), dma((8,)), dma((8,)), dma((2,)), dma((8,)),
        ],
        compiler_params=pltpu.CompilerParams(
            collective_id=0, has_side_effects=True, vmem_limit_bytes=24 << 20
        ),
        name="cross",
    )(*[
        pltpu.with_memory_space_constraint(array, pltpu.MemorySpace.HBM)
        for array in (traces, validity, boundary_rows, boundary_count, dft, small)
    ])
    basis = jnp.asarray(lag_table())
    return pl.pallas_call(
        lag_kernel,
        out_shape=jax.ShapeDtypeStruct((SG, 96, LAGS), BF),
        grid=(pl.cdiv(LAGS, CHUNK),),
        in_specs=[
            pl.BlockSpec((3, SG * 96, 128), lambda i: (0, 0, 0)),
            pl.BlockSpec((SG, 96), lambda i: (0, 0)),
            pl.BlockSpec((2 * NBIN, CHUNK), lambda i: (0, i)),
        ],
        out_specs=pl.BlockSpec((SG, 96, CHUNK), lambda i: (0, 0, i)),
        scratch_shapes=[pltpu.VMEM((SG * 96, 384), BF)],
        compiler_params=pltpu.CompilerParams(vmem_limit_bytes=24 << 20),
        name="lags",
    )(cross, pair_mask, basis)


def solution(mesh):
    three = P(("tile", "grp"), None, None)
    two = P(("tile", "grp"), None)
    return jax.shard_map(
        functools.partial(on_device, mesh.shape["tile"]),
        mesh=mesh,
        in_specs=(three, two, three, two, two),
        out_specs=three,
        check_vma=False,
    )
```

```python
import functools
import math

import jax
import jax.numpy as jnp
import ml_dtypes
import numpy as np
from jax import lax
from jax.experimental import pallas as pl
from jax.experimental.pallas import tpu as pltpu
from jax.sharding import PartitionSpec as P

SG = 4
SEG = 16
SAMP = 1500
NBIN = 144
MAXLAG = 1000
LAGS = 2001
NGRP = 8
MAIN = 128
ROWS = SG * SEG
BLK = ROWS + 16
CHUNK = 512
DFT_PARTS = ((0, 512), (512, 1024), (1024, SAMP))
FAR_FIRST = (6, 2, 5, 7, 1, 3, 4)
BF = jnp.bfloat16
F32 = jnp.float32
MESH = pl.DeviceIdType.MESH


def split_halves(table):
    high = table.astype(ml_dtypes.bfloat16)
    low = (table - high.astype(np.float64)).astype(ml_dtypes.bfloat16)
    return high, low


def dft_table():
    n = np.arange(SAMP, dtype=np.int64)[:, None]
    k = np.arange(1, NBIN + 1, dtype=np.int64)[None, :]
    angle = ((n * k) % (2 * SAMP)).astype(np.float64) * (2.0 * np.pi / (2 * SAMP))
    taper = 0.5 - 0.5 * np.cos(2.0 * np.pi * n / SAMP)
    cos, sin = taper * np.cos(angle), -taper * np.sin(angle)
    main = np.concatenate([cos[:, :MAIN], sin[:, :MAIN]], axis=1)
    rest = np.tile(np.concatenate([cos[:, MAIN:], sin[:, MAIN:]], axis=1), (1, 4))
    main_high, main_low = split_halves(main)
    rest_high, rest_low = split_halves(rest)
    return np.concatenate([main_high, main_low, rest_high, rest_low], axis=1)


def lag_table():
    k = np.arange(1, NBIN + 1, dtype=np.int64)[:, None]
    lag = np.arange(LAGS, dtype=np.int64)[None, :] - MAXLAG
    angle = ((k * lag) % (2 * SAMP)).astype(np.float64) * (2.0 * np.pi / (2 * SAMP))
    cos = np.cos(angle) / math.sqrt(NBIN)
    sin = -np.sin(angle) / math.sqrt(NBIN)
    table = np.concatenate([cos[:MAIN], sin[:MAIN], cos[MAIN:], sin[MAIN:]], axis=0)
    table = np.pad(table, ((0, 0), (0, -LAGS % CHUNK)))
    return table.astype(ml_dtypes.bfloat16)


def small_tables():
    lane = np.arange(256)
    bin_of = np.where(lane < MAIN, lane + 1, MAIN + 1 + (lane - MAIN) % 16)
    counted = lane < MAIN + 32
    near = np.abs(bin_of[:, None] - bin_of[None, :]) <= 4
    weights = np.where(counted[:, None], np.where(near, 17.0, 1.0), 0.0)
    order = np.zeros((BLK, 256))
    for s in range(SG):
        for q in range(SEG):
            order[q * SG + s, s * SEG + q] = 1.0
            order[ROWS + (q % 4) * SG + s, s * SEG + q] = 1.0
    spread = np.zeros((SG * BLK, 256))
    for s in range(SG):
        for row in range(BLK):
            spread[s * BLK + row, row // SG * SG + s] = 1.0
    return np.concatenate([weights, order, spread], axis=0).astype(ml_dtypes.bfloat16)


def arrival(step):
    return lax.rem(step, 2) * 4 + step // 2


def iota(shape, axis):
    return lax.broadcasted_iota(jnp.int32, shape, axis)


def dot(a, b):
    return jnp.dot(a, b, preferred_element_type=F32)


def lane_fold(a, shifts):
    for shift in shifts:
        a = a + pltpu.roll(a, shift, 1)
    return a


def cross_kernel(
    n_tile, x_hbm, val_hbm, rows_hbm, cnt_hbm, mask_hbm, dft_hbm, small_hbm, basis_hbm,
    left_ref, basis_ref,
    x_v, val_v, rows_s, cnt_s, mask_v, dft_v, small_v, blk, up_down, gath, nbin, role, turned,
    keep_v, f_ref, out2, in2, load_sem, dft_sem, send_g, send_n, send_p, recv_g, recv_n, recv_p,
):
    tile, me = lax.axis_index("tile"), lax.axis_index("grp")
    z_me, y_me = me // 4, lax.rem(me, 4)
    neighbour = (tile + 1, tile - 1)
    exists = (tile < n_tile - 1, tile > 0)

    loads = [
        pltpu.make_async_copy(src, dst, load_sem.at[i])
        for i, (src, dst) in enumerate(
            [(x_hbm, x_v), (val_hbm, val_v), (small_hbm, small_v), (rows_hbm, rows_s),
             (cnt_hbm, cnt_s), (mask_hbm, mask_v), (basis_hbm, basis_ref)]
        )
    ]
    dft_loads = [
        pltpu.make_async_copy(dft_hbm.at[a:b], dft_v.at[a:b], dft_sem.at[i])
        for i, (a, b) in enumerate(DFT_PARTS)
    ]
    loads[0].start()
    for load in dft_loads:
        load.start()
    for load in loads[1:6]:
        load.start()

    def other(d):
        return lax.rem(z_me + d // 4, 2) * 4 + lax.rem(y_me + lax.rem(d, 4), 4)

    barrier = pltpu.get_barrier_semaphore()
    for d in range(1, NGRP):
        pl.semaphore_signal(barrier, inc=1, device_id=(tile, other(d)), device_id_type=MESH)
    for direction in range(2):

        @pl.when(exists[direction])
        def _():
            pl.semaphore_signal(
                barrier, inc=1, device_id=(neighbour[direction], me), device_id_type=MESH
            )

    loads[1].wait()
    lane_group = iota((ROWS, 128), 1) // 32
    same_group = lane_group == (lax.rem(iota((ROWS, 128), 0), SEG) // 4)
    valid_parts = []
    for s in range(SG):
        row = jnp.broadcast_to(val_v[s : s + 1, :].astype(F32), (SEG, SEG))
        diag = jnp.where(iota((SEG, SEG), 0) == iota((SEG, SEG), 1), row, 0.0)
        valid_parts.append(jnp.sum(diag, axis=1, keepdims=True))
    valid = jnp.broadcast_to(jnp.concatenate(valid_parts, axis=0), (ROWS, 128))

    loads[0].wait()
    x = x_v[...].reshape(ROWS, SAMP)
    x_high = x.astype(BF)
    x_low = (x - x_high.astype(F32)).astype(BF)
    x_both = jnp.concatenate([x_high, x_low], axis=0)
    both = None
    for load, (a, b) in zip(dft_loads, DFT_PARTS):
        load.wait()
        part = dot(x_both[:, a:b], dft_v[a:b, :])
        both = part if both is None else both + part
    loads[6].start()
    main = both[:ROWS, :256] + (both[ROWS:, :256] + both[:ROWS, 256:512])
    rest = both[:ROWS, 512:640] + (both[ROWS:, 512:640] + both[:ROWS, 640:768])
    real, imag = main[:, :MAIN], main[:, MAIN:]
    power = jnp.concatenate([real * real + imag * imag, rest * rest], axis=1)
    power_high = power.astype(BF)
    power_low = (power - power_high.astype(F32)).astype(BF)
    loads[2].wait()
    level = dot(jnp.concatenate([power_high, power_low], axis=0), small_v[0:256, :])
    level = (level[:ROWS] + level[ROWS:]) * (1.0 / 288.0) + 1e-06
    factor = lax.rsqrt(level)
    factor_main = factor[:, :MAIN] * valid
    factor_rest = jnp.where(same_group, factor[:, MAIN:] * valid, 0.0)
    white = jnp.concatenate([real * factor_main, imag * factor_main], axis=1).astype(BF)
    white_rest = jnp.concatenate(
        [rest * factor_rest, jnp.where(same_group, valid, 0.0)], axis=1
    ).astype(BF)
    blk[0:ROWS, :] = dot(small_v[256 : 256 + ROWS, 0:ROWS], white).astype(BF)
    blk[ROWS:BLK, :] = dot(small_v[256 + ROWS : 256 + BLK, 0:ROWS], white_rest).astype(BF)

    edges = jnp.where(exists[0], 1, 0) + jnp.where(exists[1], 1, 0)
    pl.semaphore_wait(barrier, NGRP - 1 + edges)

    def gather_copy(d):
        return pltpu.make_async_remote_copy(
            src_ref=blk, dst_ref=gath.at[me], send_sem=send_g.at[d - 1], recv_sem=recv_g.at[me],
            device_id=(tile, other(d)), device_id_type=MESH,
        )

    for d in FAR_FIRST:
        gather_copy(d).start()

    own = blk[...]
    gath[me] = own
    loads[3].wait()
    loads[4].wait()
    within = lax.rem(iota((BLK, BLK), 0), SG)
    same_four = (iota((BLK, BLK), 0) // SG) == (iota((BLK, BLK), 1) // SG)
    column = lax.rem(iota((BLK, BLK), 1), SG)

    def edge_copy(direction):
        return pltpu.make_async_remote_copy(
            src_ref=up_down.at[direction], dst_ref=nbin.at[direction],
            send_sem=send_n.at[direction], recv_sem=recv_n.at[direction],
            device_id=(neighbour[direction], me), device_id_type=MESH,
        )

    for direction in range(2):
        wanted = jnp.full((BLK, BLK), rows_s[0, direction, SG - 1], jnp.int32)
        for h in range(SG - 1):
            wanted = jnp.where(within == h, rows_s[0, direction, h], wanted)
        live = within < cnt_s[0, direction]
        pick = jnp.where(same_four & live & (column == wanted), 1.0, 0.0).astype(BF)
        up_down[direction] = dot(pick, own).astype(BF)

        @pl.when(exists[direction])
        def _():
            edge_copy(direction).start()

    spread = small_v[256 + BLK : 256 + BLK + SG * BLK, 0:BLK]
    lane = iota((16, 128), 1)
    first_half = lax.rem(lane, 32) < 16

    def set_role(first, block):
        wide = dot(spread, block)
        for s in range(SG):
            part = wide[s * BLK : (s + 1) * BLK]
            role[first + s] = part
            tail = part[ROWS:, :128]
            turned[first + s] = jnp.where(
                first_half, pltpu.roll(tail, 112, 1), -pltpu.roll(tail, 16, 1)
            )

    set_role(0, own)
    loads[5].wait()
    pick = (lax.rem(iota((SG * 96, 96), 0), 96) == iota((SG * 96, 96), 1)).astype(F32)
    keep = lax.dot_general(
        pick.astype(BF), mask_v[...].astype(F32).astype(BF), (((1,), (1,)), ((), ())),
        preferred_element_type=F32,
    )
    keep = jnp.where(iota((SG * 96, SG), 0) // 96 == iota((SG * 96, SG), 1), keep, 0.0)
    keep_v[...] = dot(keep.astype(BF), jnp.ones((SG, 128), BF))
    for direction in range(2):
        source = 1 - direction

        @pl.when(exists[source])
        def _():
            edge_copy(direction).wait_recv()

        @pl.when(jnp.logical_not(exists[source]))
        def _():
            nbin[direction] = jnp.zeros((BLK, 256), BF)

        set_role(SG + direction * SG, nbin[direction])

    sub = iota((8, 128), 0)
    low_half = sub < 4
    rest_real = lax.rem(iota((8, 128), 1), 32) < 16

    def products(j, block):
        w_re, w_im = role[j, 0:ROWS, 0:128], role[j, 0:ROWS, 128:256]
        w_rest, w_val = role[j, ROWS:BLK, 0:128], role[j, ROWS:BLK, 128:256]
        v_re, v_im = block[0:ROWS, 0:128], block[0:ROWS, 128:256]
        v_rest, v_val = block[ROWS:BLK, 0:128], block[ROWS:BLK, 128:256]
        return [
            jnp.sum(a.reshape(-1, 8, 128), axis=0)
            for a in (
                w_re * v_re + w_im * v_im,
                w_im * v_re - w_re * v_im,
                w_rest * v_rest,
                turned[j] * v_rest,
                w_val * v_val,
            )
        ]

    def finish(sums, sign):
        re, im, rest_re, rest_im, count = sums
        count = lane_fold(count, (64, 32))
        inverse = 1.0 / jnp.maximum(count, 1.0)
        rest_re = lane_fold(rest_re, (64, 32, 16))
        rest_im = lane_fold(rest_im, (64, 32, 16)) * sign
        return re * inverse, im * (inverse * sign), jnp.where(rest_real, rest_re, rest_im) * inverse

    def result_copy(d):
        return pltpu.make_async_remote_copy(
            src_ref=out2.at[d], dst_ref=in2.at[me], send_sem=send_p.at[d],
            recv_sem=recv_p.at[me], device_id=(tile, other(d)), device_id_type=MESH,
        )

    def recv_wait(buffer, sems, g):
        pltpu.make_async_copy(buffer.at[g], buffer.at[g], sems.at[g]).wait()

    def boundary(step, carry):
        d = arrival(step)
        g = other(d)

        @pl.when(d > 0)
        def _():
            recv_wait(gath, recv_g, g)

        block = gath[g].astype(F32)
        for pair in range(4):
            a = products(SG + 2 * pair, block)
            b = products(SG + 2 * pair + 1, block)
            both = [
                jnp.where(low_half, p, q) + pltpu.roll(jnp.where(low_half, q, p), 4, 0)
                for p, q in zip(a, b)
            ]
            done = finish(both, -1.0)
            for i in range(3):
                out2[d, 8 * pair : 8 * pair + 8, 128 * i : 128 * i + 128] = done[i].astype(BF)

        @pl.when(d > 0)
        def _():
            result_copy(d).start()

        return carry

    lax.fori_loop(0, NGRP, boundary, 0)

    def inner(d, carry):
        g = other(d)
        block = gath[g].astype(F32)
        for s in range(SG):
            sums = [a + pltpu.roll(a, 4, 0) for a in products(s, block)]
            done = finish(sums, 1.0)
            for i in range(3):
                f_ref[i, pl.ds(g * 48 + s, 4, stride=4), :] = done[i][0:4]
        return carry

    lax.fori_loop(0, NGRP, inner, 0)

    def collect(d, carry):
        g = other(d)

        @pl.when(d > 0)
        def _():
            recv_wait(in2, recv_p, g)
            start = pl.multiple_of(g * 48 + 16, 8)
            for i in range(3):
                f_ref[i, pl.ds(start, 32), :] = in2[g, :, 128 * i : 128 * i + 128].astype(F32)

        return carry

    lax.fori_loop(0, NGRP, collect, 0)
    start = pl.multiple_of(me * 48 + 16, 8)
    for i in range(3):
        f_ref[i, pl.ds(start, 32), :] = out2[0, :, 128 * i : 128 * i + 128].astype(F32)
    for d in range(1, NGRP):
        gather_copy(d).wait_send()
        result_copy(d).wait_send()
    for direction in range(2):

        @pl.when(exists[direction])
        def _():
            edge_copy(direction).wait_send()

    for s in range(SG):
        keep = keep_v[s * 96 : (s + 1) * 96, :]
        for i in range(3):
            rows = f_ref[i, pl.ds(s, 96, stride=4), :] * keep
            left_ref[s * 96 : (s + 1) * 96, 128 * i : 128 * i + 128] = rows.astype(BF)
    loads[6].wait()


def lag_kernel(left_ref, basis_ref, out_ref):
    chunk = pl.ds(pl.multiple_of(pl.program_id(0) * CHUNK, CHUNK), CHUNK)
    series = dot(left_ref[:, 0 : 2 * NBIN], basis_ref[:, chunk])
    out_ref[...] = series.reshape(SG, 96, CHUNK).astype(BF)


def on_device(n_tile, traces, validity, boundary_rows, boundary_count, pair_mask):
    dft = jnp.asarray(dft_table())
    small = jnp.asarray(small_tables())
    anywhere = pl.BlockSpec(memory_space=pltpu.MemorySpace.HBM)
    dma = pltpu.SemaphoreType.DMA
    vmem = pl.BlockSpec(memory_space=pltpu.VMEM)
    basis = jnp.asarray(lag_table())
    left, basis = pl.pallas_call(
        functools.partial(cross_kernel, n_tile),
        out_shape=(
            jax.ShapeDtypeStruct((SG * 96, 384), BF),
            jax.ShapeDtypeStruct(basis.shape, BF),
        ),
        in_specs=[anywhere] * 8,
        out_specs=(vmem, vmem),
        scratch_shapes=[
            pltpu.VMEM((SG, SEG, SAMP), F32),
            pltpu.VMEM((SG, SEG), jnp.int32),
            pltpu.SMEM((1, 2, SG), jnp.int32),
            pltpu.SMEM((1, 2), jnp.int32),
            pltpu.VMEM((SG, 96), jnp.int32),
            pltpu.VMEM(dft.shape, BF),
            pltpu.VMEM(small.shape, BF),
            pltpu.VMEM((BLK, 256), BF),
            pltpu.VMEM((2, BLK, 256), BF),
            pltpu.VMEM((NGRP, BLK, 256), BF),
            pltpu.VMEM((2, BLK, 256), BF),
            pltpu.VMEM((12, BLK, 256), F32),
            pltpu.VMEM((12, 16, 128), F32),
            pltpu.VMEM((SG * 96, 128), F32),
            pltpu.VMEM((3, SG * 96, 128), F32),
            pltpu.VMEM((NGRP, 32, 384), BF),
            pltpu.VMEM((NGRP, 32, 384), BF),
            dma((7,)), dma((len(DFT_PARTS),)),
            dma((7,)), dma((2,)), dma((8,)), dma((8,)), dma((2,)), dma((8,)),
        ],
        compiler_params=pltpu.CompilerParams(
            collective_id=0, has_side_effects=True, vmem_limit_bytes=24 << 20
        ),
        name="cross",
    )(*[
        pltpu.with_memory_space_constraint(array, pltpu.MemorySpace.HBM)
        for array in (
            traces, validity, boundary_rows, boundary_count, pair_mask, dft, small, basis
        )
    ])
    return pl.pallas_call(
        lag_kernel,
        out_shape=jax.ShapeDtypeStruct((SG, 96, LAGS), BF),
        grid=(pl.cdiv(LAGS, CHUNK),),
        in_specs=[vmem, vmem],
        out_specs=pl.BlockSpec((SG, 96, CHUNK), lambda i: (0, 0, i)),
        compiler_params=pltpu.CompilerParams(vmem_limit_bytes=24 << 20),
        name="lags",
    )(left, basis)


def solution(mesh):
    three = P(("tile", "grp"), None, None)
    two = P(("tile", "grp"), None)
    return jax.shard_map(
        functools.partial(on_device, mesh.shape["tile"]),
        mesh=mesh,
        in_specs=(three, two, three, two, two),
        out_specs=three,
        check_vma=False,
    )
```

```python
import functools
import math

import jax
import jax.numpy as jnp
import ml_dtypes
import numpy as np
from jax import lax
from jax.experimental import pallas as pl
from jax.experimental.pallas import tpu as pltpu
from jax.sharding import PartitionSpec as P

SG = 4
SEG = 16
SAMP = 1500
NBIN = 144
MAXLAG = 1000
LAGS = 2001
NGRP = 8
MAIN = 128
ROWS = SG * SEG
BLK = ROWS + 16
CHUNK = 512
DFT_PARTS = ((0, 512), (512, 1024), (1024, SAMP))
BF = jnp.bfloat16
F32 = jnp.float32
MESH = pl.DeviceIdType.MESH


def split_halves(table):
    high = table.astype(ml_dtypes.bfloat16)
    low = (table - high.astype(np.float64)).astype(ml_dtypes.bfloat16)
    return high, low


def dft_table():
    n = np.arange(SAMP, dtype=np.int64)[:, None]
    k = np.arange(1, NBIN + 1, dtype=np.int64)[None, :]
    angle = ((n * k) % (2 * SAMP)).astype(np.float64) * (2.0 * np.pi / (2 * SAMP))
    taper = 0.5 - 0.5 * np.cos(2.0 * np.pi * n / SAMP)
    cos, sin = taper * np.cos(angle), -taper * np.sin(angle)
    main = np.concatenate([cos[:, :MAIN], sin[:, :MAIN]], axis=1)
    rest = np.concatenate([cos[:, MAIN:], sin[:, MAIN:]], axis=1)
    main_high, main_low = split_halves(main)
    rest_high, rest_low = split_halves(rest)
    unused = np.zeros((SAMP, 64), ml_dtypes.bfloat16)
    return np.concatenate([main_high, main_low, rest_high, rest_low, unused], axis=1)


def lag_table():
    k = np.arange(1, NBIN + 1, dtype=np.int64)[:, None]
    lag = np.arange(LAGS, dtype=np.int64)[None, :] - MAXLAG
    angle = ((k * lag) % (2 * SAMP)).astype(np.float64) * (2.0 * np.pi / (2 * SAMP))
    cos = np.cos(angle) / math.sqrt(NBIN)
    sin = -np.sin(angle) / math.sqrt(NBIN)
    table = np.concatenate([cos[:MAIN], sin[:MAIN], cos[MAIN:], sin[MAIN:]], axis=0)
    table = np.pad(table, ((0, 0), (0, -LAGS % CHUNK)))
    return table.astype(ml_dtypes.bfloat16)


def iota(shape, axis):
    return lax.broadcasted_iota(jnp.int32, shape, axis)


def dot(a, b):
    return jnp.dot(a, b, preferred_element_type=F32)


def lane_fold(a, shifts):
    for shift in shifts:
        a = a + pltpu.roll(a, shift, 1)
    return a


def bin_of(lane):
    return jnp.where(lane < MAIN, lane, MAIN + lax.rem(lane, 16))


def power_weights():
    shape = (256, 256)
    source, target = iota(shape, 0), iota(shape, 1)
    near = jnp.abs(bin_of(source) - bin_of(target)) <= 4
    return jnp.where(source < MAIN + 32, jnp.where(near, 17.0, 1.0), 0.0).astype(BF)


def cross_kernel(
    n_tile, x_hbm, val_hbm, rows_hbm, cnt_hbm, mask_hbm, dft_hbm, basis_hbm,
    left_ref, basis_ref,
    x_v, val_v, rows_s, cnt_s, mask_v, dft_v, blk, up_down, gath, nbin, role, turned,
    keep_v, f_ref, out2, in2, load_sem, dft_sem, send_g, send_n, send_p, recv_g, recv_n, recv_p,
):
    tile, me = lax.axis_index("tile"), lax.axis_index("grp")
    my_step = lax.rem(me, 4) * 2 + me // 4
    neighbour = (tile + 1, tile - 1)
    exists = (tile < n_tile - 1, tile > 0)

    def member(step):
        return lax.rem(step, 2) * 4 + step // 2

    def peer(j):
        return member(j + jnp.where(my_step <= j, 1, 0))

    loads = [
        pltpu.make_async_copy(src, dst, load_sem.at[i])
        for i, (src, dst) in enumerate(
            [(x_hbm, x_v), (val_hbm, val_v), (rows_hbm, rows_s), (cnt_hbm, cnt_s),
             (mask_hbm, mask_v), (basis_hbm, basis_ref)]
        )
    ]
    dft_loads = [
        pltpu.make_async_copy(dft_hbm.at[a:b], dft_v.at[a:b], dft_sem.at[i])
        for i, (a, b) in enumerate(DFT_PARTS)
    ]
    loads[0].start()
    loads[1].start()
    for load in dft_loads:
        load.start()
    for load in loads[2:5]:
        load.start()

    barrier = pltpu.get_barrier_semaphore()
    for j in range(NGRP - 1):
        pl.semaphore_signal(barrier, inc=1, device_id=(tile, peer(j)), device_id_type=MESH)
    for direction in range(2):

        @pl.when(exists[direction])
        def _():
            pl.semaphore_signal(
                barrier, inc=1, device_id=(neighbour[direction], me), device_id_type=MESH
            )

    row64, col64 = iota((ROWS, ROWS), 0), iota((ROWS, ROWS), 1)
    order = (col64 == lax.rem(row64, SG) * SEG + row64 // SG).astype(F32).astype(BF)
    weights = power_weights()
    loads[1].wait()
    same_group = iota((ROWS, 128), 1) // 32 == iota((ROWS, 128), 0) // 16
    lane128 = iota((ROWS, 128), 1)
    valid_parts = []
    for s in range(SG):
        row = jnp.broadcast_to(val_v[s : s + 1, :].astype(F32), (SEG, SEG))
        diag = jnp.where(iota((SEG, SEG), 0) == iota((SEG, SEG), 1), row, 0.0)
        valid_parts.append(jnp.sum(diag, axis=1, keepdims=True))
    valid = jnp.broadcast_to(jnp.concatenate(valid_parts, axis=0), (ROWS, 128))
    valid = dot(order, valid.astype(BF))
    valid_group = jnp.where(same_group, valid, 0.0)

    def stack_group(a):
        packed = (a[0:16] + a[16:32]) + (a[32:48] + a[48:64])
        return jnp.concatenate([packed[0:8], packed[8:16]], axis=1)

    loads[0].wait()
    x = x_v[...].reshape(ROWS, SAMP)
    x_high = x.astype(BF)
    x_low = (x - x_high.astype(F32)).astype(BF)
    x_both = jnp.concatenate(
        [dot(order, x_high).astype(BF), dot(order, x_low).astype(BF)], axis=0
    )
    both = None
    for load, (a, b) in zip(dft_loads, DFT_PARTS):
        load.wait()
        part = dot(x_both[:, a:b], dft_v[a:b, :])
        both = part if both is None else both + part
    loads[5].start()
    main = both[:ROWS, :256] + (both[ROWS:, :256] + both[:ROWS, 256:512])
    rest = both[:ROWS, 512:640] + jnp.where(lane128 < 32, both[ROWS:, 512:640], 0.0)
    rest = jnp.where(lane128 < 32, rest + pltpu.roll(rest, 96, 1), 0.0)
    rest = rest + pltpu.roll(rest, 32, 1)
    rest = rest + pltpu.roll(rest, 64, 1)
    real, imag = main[:, :MAIN], main[:, MAIN:]
    power = jnp.concatenate([real * real + imag * imag, rest * rest], axis=1)
    power_high = power.astype(BF)
    power_low = (power - power_high.astype(F32)).astype(BF)
    level = dot(jnp.concatenate([power_high, power_low], axis=0), weights)
    level = (level[:ROWS] + level[ROWS:]) * (1.0 / 288.0) + 1e-06
    factor = lax.rsqrt(level)
    factor_main = factor[:, :MAIN] * valid
    factor_rest = factor[:, MAIN:] * valid_group
    white = jnp.concatenate([real * factor_main, imag * factor_main], axis=1)
    own = jnp.concatenate(
        [white, stack_group(rest * factor_rest), stack_group(valid_group)], axis=0
    ).astype(BF)
    blk[...] = own

    edges = jnp.where(exists[0], 1, 0) + jnp.where(exists[1], 1, 0)
    pl.semaphore_wait(barrier, NGRP - 1 + edges)

    loads[2].wait()
    loads[3].wait()
    row, col = iota((BLK, BLK), 0), iota((BLK, BLK), 1)
    within, column = lax.rem(row, SG), lax.rem(col, SG)
    same_four = (row // SG) == (col // SG)

    def edge_copy(direction):
        return pltpu.make_async_remote_copy(
            src_ref=up_down.at[direction], dst_ref=nbin.at[direction],
            send_sem=send_n.at[direction], recv_sem=recv_n.at[direction],
            device_id=(neighbour[direction], me), device_id_type=MESH,
        )

    for direction in range(2):
        wanted = jnp.full((BLK, BLK), rows_s[0, direction, SG - 1], jnp.int32)
        for h in range(SG - 1):
            wanted = jnp.where(within == h, rows_s[0, direction, h], wanted)
        live = within < cnt_s[0, direction]
        pick = jnp.where(same_four & live & (column == wanted), 1.0, 0.0).astype(BF)
        up_down[direction] = dot(pick, own).astype(BF)

        @pl.when(exists[direction])
        def _():
            edge_copy(direction).start()

    def gather_copy(j):
        return pltpu.make_async_remote_copy(
            src_ref=blk, dst_ref=gath.at[me], send_sem=send_g.at[j], recv_sem=recv_g.at[me],
            device_id=(tile, peer(j)), device_id_type=MESH,
        )

    for j in range(NGRP - 1):
        gather_copy(j).start()
    gath[me] = own

    first_half = lax.rem(iota((8, 256), 1), 32) < 16

    def set_role(first, block):
        for s in range(SG):
            spread = (col == row // SG * SG + s).astype(F32).astype(BF)
            wide = dot(spread, block)
            role[first + s] = wide
            tail = wide[ROWS : ROWS + 8]
            ahead = jnp.concatenate(
                [pltpu.roll(tail[:, 0:128], 112, 1), pltpu.roll(tail[:, 128:], 112, 1)], axis=1
            )
            behind = jnp.concatenate(
                [pltpu.roll(tail[:, 0:128], 16, 1), pltpu.roll(tail[:, 128:], 16, 1)], axis=1
            )
            turned[first + s] = jnp.where(first_half, ahead, -behind)

    set_role(0, own)
    loads[4].wait()
    pick = (lax.rem(iota((SG * 96, 96), 0), 96) == iota((SG * 96, 96), 1)).astype(F32)
    keep = lax.dot_general(
        pick.astype(BF), mask_v[...].astype(F32).astype(BF), (((1,), (1,)), ((), ())),
        preferred_element_type=F32,
    )
    keep = jnp.where(iota((SG * 96, SG), 0) // 96 == iota((SG * 96, SG), 1), keep, 0.0)
    keep_v[...] = dot(keep.astype(BF), jnp.ones((SG, 128), BF))
    for direction in range(2):
        source = 1 - direction

        @pl.when(exists[source])
        def _():
            edge_copy(direction).wait_recv()

        @pl.when(jnp.logical_not(exists[source]))
        def _():
            nbin[direction] = jnp.zeros((BLK, 256), BF)

        set_role(SG + direction * SG, nbin[direction])

    low_half = iota((8, 128), 0) < 4
    lane = iota((8, 128), 1)
    rest_real = lax.rem(lane, 32) < 16

    def products(j, block):
        w_re, w_im = role[j, 0:ROWS, 0:128], role[j, 0:ROWS, 128:256]
        v_re, v_im = block[0:ROWS, 0:128], block[0:ROWS, 128:256]
        w_rest, v_rest = role[j, ROWS : ROWS + 8, :], block[ROWS : ROWS + 8]
        count = role[j, ROWS + 8 : BLK, :] * block[ROWS + 8 : BLK]
        rest_re = w_rest * v_rest
        rest_im = turned[j] * v_rest
        return [
            jnp.sum((w_re * v_re + w_im * v_im).reshape(-1, 8, 128), axis=0),
            jnp.sum((w_im * v_re - w_re * v_im).reshape(-1, 8, 128), axis=0),
            rest_re[:, 0:128] + rest_re[:, 128:],
            rest_im[:, 0:128] + rest_im[:, 128:],
            count[:, 0:128] + count[:, 128:],
        ]

    def finish(sums, sign):
        re, im, rest_re, rest_im, count = sums
        count = lane_fold(count, (64, 32))
        inverse = 1.0 / jnp.maximum(count, 1.0)
        rest_re = lane_fold(rest_re, (64, 32, 16))
        rest_im = lane_fold(rest_im, (64, 32, 16)) * sign
        return re * inverse, im * (inverse * sign), jnp.where(rest_real, rest_re, rest_im) * inverse

    def result_copy(g):
        return pltpu.make_async_remote_copy(
            src_ref=out2.at[g], dst_ref=in2.at[me], send_sem=send_p.at[g],
            recv_sem=recv_p.at[me], device_id=(tile, g), device_id_type=MESH,
        )

    def recv_wait(buffer, sems, g):
        pltpu.make_async_copy(buffer.at[g], buffer.at[g], sems.at[g]).wait()

    def boundary(step, carry):
        g = member(step)

        @pl.when(g != me)
        def _():
            recv_wait(gath, recv_g, g)

        block = gath[g].astype(F32)
        packed = jnp.zeros((8, 128), F32)
        for pair in range(4):
            a = products(SG + 2 * pair, block)
            b = products(SG + 2 * pair + 1, block)
            both = [
                jnp.where(low_half, p, q) + pltpu.roll(jnp.where(low_half, q, p), 4, 0)
                for p, q in zip(a, b)
            ]
            re, im, rest = finish(both, -1.0)
            out2[g, 8 * pair : 8 * pair + 8, :] = jnp.concatenate([re, im], axis=1).astype(BF)
            packed = jnp.where(lane // 32 == pair, rest, packed)
        out2[g, 32:40, :] = jnp.concatenate([packed, packed], axis=1).astype(BF)

        @pl.when(g != me)
        def _():
            result_copy(g).start()

        return carry

    lax.fori_loop(0, NGRP, boundary, 0)

    def inner(step, carry):
        g = member(step)
        block = gath[g].astype(F32)
        for s in range(SG):
            sums = [a + pltpu.roll(a, 4, 0) for a in products(s, block)]
            done = finish(sums, 1.0)
            for i in range(3):
                f_ref[i, pl.ds(g * 48 + s, 4, stride=4), :] = done[i][0:4]
        return carry

    lax.fori_loop(0, NGRP, inner, 0)

    def unpack(g, block):
        start = pl.multiple_of(g * 48 + 16, 8)
        block = block.astype(F32)
        for i in range(2):
            f_ref[i, pl.ds(start, 32), :] = block[0:32, 128 * i : 128 * i + 128]
        rest = block[32:40, 0:128]
        for pair in range(4):
            turned_rest = rest if pair == 0 else pltpu.roll(rest, 128 - 32 * pair, 1)
            f_ref[2, pl.ds(pl.multiple_of(start + 8 * pair, 8), 8), :] = turned_rest

    unpack(me, out2[me])

    def collect(step, carry):
        g = member(step)

        @pl.when(g != me)
        def _():
            recv_wait(in2, recv_p, g)
            unpack(g, in2[g])

        return carry

    lax.fori_loop(0, NGRP, collect, 0)
    for s in range(SG):
        keep = keep_v[s * 96 : (s + 1) * 96, :]
        for i in range(3):
            rows = f_ref[i, pl.ds(s, 96, stride=4), :] * keep
            left_ref[s * 96 : (s + 1) * 96, 128 * i : 128 * i + 128] = rows.astype(BF)

    for j in range(NGRP - 1):
        gather_copy(j).wait_send()
        result_copy(peer(j)).wait_send()
    for direction in range(2):

        @pl.when(exists[direction])
        def _():
            edge_copy(direction).wait_send()

    loads[5].wait()


def lag_kernel(left_ref, basis_ref, out_hbm, out_v, sems):
    copies = []
    for i, start in enumerate(range(0, LAGS, CHUNK)):
        series = dot(left_ref[:, 0 : 2 * NBIN], basis_ref[:, start : start + CHUNK])
        stop = min(start + CHUNK, LAGS)
        series = series[:, : stop - start].reshape(SG, 96, stop - start)
        out_v[:, :, start:stop] = series.astype(BF)
        copies.append(
            pltpu.make_async_copy(
                out_v.at[:, :, start:stop], out_hbm.at[:, :, start:stop], sems.at[i]
            )
        )
        copies[-1].start()
    for copy in copies:
        copy.wait()


def on_device(n_tile, traces, validity, boundary_rows, boundary_count, pair_mask):
    dft = jnp.asarray(dft_table())
    anywhere = pl.BlockSpec(memory_space=pltpu.MemorySpace.HBM)
    dma = pltpu.SemaphoreType.DMA
    vmem = pl.BlockSpec(memory_space=pltpu.VMEM)
    basis = jnp.asarray(lag_table())
    left, basis = pl.pallas_call(
        functools.partial(cross_kernel, n_tile),
        out_shape=(
            jax.ShapeDtypeStruct((SG * 96, 384), BF),
            jax.ShapeDtypeStruct(basis.shape, BF),
        ),
        in_specs=[anywhere] * 7,
        out_specs=(vmem, vmem),
        scratch_shapes=[
            pltpu.VMEM((SG, SEG, SAMP), F32),
            pltpu.VMEM((SG, SEG), jnp.int32),
            pltpu.SMEM((1, 2, SG), jnp.int32),
            pltpu.SMEM((1, 2), jnp.int32),
            pltpu.VMEM((SG, 96), jnp.int32),
            pltpu.VMEM(dft.shape, BF),
            pltpu.VMEM((BLK, 256), BF),
            pltpu.VMEM((2, BLK, 256), BF),
            pltpu.VMEM((NGRP, BLK, 256), BF),
            pltpu.VMEM((2, BLK, 256), BF),
            pltpu.VMEM((12, BLK, 256), F32),
            pltpu.VMEM((12, 8, 256), F32),
            pltpu.VMEM((SG * 96, 128), F32),
            pltpu.VMEM((3, SG * 96, 128), F32),
            pltpu.VMEM((NGRP, 40, 256), BF),
            pltpu.VMEM((NGRP, 40, 256), BF),
            dma((6,)), dma((len(DFT_PARTS),)),
            dma((7,)), dma((2,)), dma((8,)), dma((8,)), dma((2,)), dma((8,)),
        ],
        compiler_params=pltpu.CompilerParams(
            collective_id=0, has_side_effects=True, vmem_limit_bytes=24 << 20
        ),
        name="cross",
    )(*[
        pltpu.with_memory_space_constraint(array, pltpu.MemorySpace.HBM)
        for array in (
            traces, validity, boundary_rows, boundary_count, pair_mask, dft, basis
        )
    ])
    return pl.pallas_call(
        lag_kernel,
        out_shape=jax.ShapeDtypeStruct((SG, 96, LAGS), BF),
        in_specs=[vmem, vmem],
        out_specs=pl.BlockSpec(memory_space=pl.ANY),
        scratch_shapes=[
            pltpu.VMEM((SG, 96, LAGS), BF),
            pltpu.SemaphoreType.DMA((pl.cdiv(LAGS, CHUNK),)),
        ],
        compiler_params=pltpu.CompilerParams(vmem_limit_bytes=24 << 20),
        name="lags",
    )(left, basis)


def solution(mesh):
    three = P(("tile", "grp"), None, None)
    two = P(("tile", "grp"), None)
    return jax.shard_map(
        functools.partial(on_device, mesh.shape["tile"]),
        mesh=mesh,
        in_specs=(three, two, three, two, two),
        out_specs=three,
        check_vma=False,
    )
```

```python
import functools
import math

import jax
import jax.numpy as jnp
import ml_dtypes
import numpy as np
from jax import lax
from jax.experimental import pallas as pl
from jax.experimental.pallas import tpu as pltpu
from jax.sharding import PartitionSpec as P

SG = 4
SEG = 16
SAMP = 1500
NBIN = 144
MAXLAG = 1000
LAGS = 2001
NGRP = 8
MAIN = 128
ROWS = SG * SEG
BLK = ROWS + 16
CHUNK = 512
X_RUN = 8
DEAD = 15.0
DFT_PARTS = ((0, 512), (512, 1024), (1024, SAMP))
BF = jnp.bfloat16
F32 = jnp.float32
MESH = pl.DeviceIdType.MESH


def split_halves(table):
    high = table.astype(ml_dtypes.bfloat16)
    low = (table - high.astype(np.float64)).astype(ml_dtypes.bfloat16)
    return high, low


def dft_table():
    n = np.arange(SAMP, dtype=np.int64)[:, None]
    k = np.arange(1, NBIN + 1, dtype=np.int64)[None, :]
    angle = ((n * k) % (2 * SAMP)).astype(np.float64) * (2.0 * np.pi / (2 * SAMP))
    taper = 0.5 - 0.5 * np.cos(2.0 * np.pi * n / SAMP)
    cos, sin = taper * np.cos(angle), -taper * np.sin(angle)
    main = np.concatenate([cos[:, :MAIN], sin[:, :MAIN]], axis=1)
    rest = np.concatenate([cos[:, MAIN:], sin[:, MAIN:]], axis=1)
    main_high, main_low = split_halves(main)
    rest_high, rest_low = split_halves(rest)
    unused = np.zeros((SAMP, 64), ml_dtypes.bfloat16)
    return np.concatenate([main_high, main_low, rest_high, rest_low, unused], axis=1)


def lag_table():
    k = np.arange(1, NBIN + 1, dtype=np.int64)[:, None]
    lag = np.arange(LAGS, dtype=np.int64)[None, :] - MAXLAG
    angle = ((k * lag) % (2 * SAMP)).astype(np.float64) * (2.0 * np.pi / (2 * SAMP))
    cos = np.cos(angle) / math.sqrt(NBIN)
    sin = -np.sin(angle) / math.sqrt(NBIN)
    table = np.concatenate([cos[:MAIN], sin[:MAIN], cos[MAIN:], sin[MAIN:]], axis=0)
    table = np.pad(table, ((0, 0), (0, -LAGS % CHUNK)))
    return table.astype(ml_dtypes.bfloat16)


def iota(shape, axis):
    return lax.broadcasted_iota(jnp.int32, shape, axis)


def dot(a, b):
    return jnp.dot(a, b, preferred_element_type=F32)


def lane_fold(a, shifts):
    for shift in shifts:
        a = a + pltpu.roll(a, shift, 1)
    return a


def bin_of(lane):
    return jnp.where(lane < MAIN, lane, MAIN + lax.rem(lane, 16))


def power_weights():
    shape = (256, 256)
    source, target = iota(shape, 0), iota(shape, 1)
    near = jnp.abs(bin_of(source) - bin_of(target)) <= 4
    return jnp.where(source < MAIN + 32, jnp.where(near, 17.0, 1.0), 0.0).astype(BF)


def cross_kernel(
    n_tile, x_hbm, val_hbm, rows_hbm, cnt_hbm, mask_hbm, dft_hbm, basis_hbm,
    left_ref, basis_ref,
    x_v, val_v, rows_s, cnt_s, mask_v, dft_v, blk, gath, side, far, role, turned,
    keep_v, code_v, f_ref, load_sem, dft_sem, send_g, send_s, send_x, send_b,
    recv_g, recv_s, recv_x,
):
    tile, me = lax.axis_index("tile"), lax.axis_index("grp")
    my_step = lax.rem(me, 4) * 2 + me // 4
    neighbour = (tile + 1, tile - 1)
    exists = (tile < n_tile - 1, tile > 0)
    core = lax.rem(tile, 2)
    side_tile = tile + 1 - 2 * core
    far_tile = tile - 1 + 2 * core
    has_far = jnp.logical_and(far_tile >= 0, far_tile < n_tile)
    turn = jnp.logical_and(has_far, (far_tile + X_RUN) // X_RUN != (tile + X_RUN) // X_RUN)
    straight = jnp.logical_and(has_far, jnp.logical_not(turn))

    def member(step):
        return lax.rem(step, 2) * 4 + step // 2

    def peer(j):
        return member(j + jnp.where(my_step <= j, 1, 0))

    loads = [
        pltpu.make_async_copy(src, dst, load_sem.at[i])
        for i, (src, dst) in enumerate(
            [(x_hbm, x_v), (val_hbm, val_v), (rows_hbm, rows_s), (cnt_hbm, cnt_s),
             (mask_hbm, mask_v), (basis_hbm, basis_ref)]
        )
    ]
    dft_loads = [
        pltpu.make_async_copy(dft_hbm.at[a:b], dft_v.at[a:b], dft_sem.at[i])
        for i, (a, b) in enumerate(DFT_PARTS)
    ]
    loads[0].start()
    loads[1].start()
    for load in dft_loads:
        load.start()
    for load in loads[2:5]:
        load.start()

    barrier = pltpu.get_barrier_semaphore()
    for j in range(NGRP - 1):
        pl.semaphore_signal(barrier, inc=1, device_id=(tile, peer(j)), device_id_type=MESH)
    for direction in range(2):

        @pl.when(exists[direction])
        def _():
            pl.semaphore_signal(
                barrier, inc=1, device_id=(neighbour[direction], me), device_id_type=MESH
            )

    row64, col64 = iota((ROWS, ROWS), 0), iota((ROWS, ROWS), 1)
    order = (col64 == lax.rem(row64, SG) * SEG + row64 // SG).astype(F32).astype(BF)
    weights = power_weights()
    loads[1].wait()
    same_group = iota((ROWS, 128), 1) // 32 == iota((ROWS, 128), 0) // 16
    lane128 = iota((ROWS, 128), 1)
    valid_parts = []
    for s in range(SG):
        row = jnp.broadcast_to(val_v[s : s + 1, :].astype(F32), (SEG, SEG))
        diag = jnp.where(iota((SEG, SEG), 0) == iota((SEG, SEG), 1), row, 0.0)
        valid_parts.append(jnp.sum(diag, axis=1, keepdims=True))
    valid = jnp.broadcast_to(jnp.concatenate(valid_parts, axis=0), (ROWS, 128))
    valid = dot(order, valid.astype(BF))
    valid_group = jnp.where(same_group, valid, 0.0)
    loads[2].wait()
    loads[3].wait()

    def stack_group(a):
        packed = (a[0:16] + a[16:32]) + (a[32:48] + a[48:64])
        return jnp.concatenate([packed[0:8], packed[8:16]], axis=1)

    tail = stack_group(valid_group)
    tail_row, tail_lane = iota((8, 256), 0), iota((8, 256), 1)
    tail = jnp.where(lax.rem(tail_lane, 32) == 31, 0.0, tail)
    for direction in range(2):
        for h in range(SG):
            code = jnp.where(
                h < cnt_s[0, direction], rows_s[0, direction, h].astype(F32), DEAD
            )
            here = (tail_row == h) & (tail_lane == 31 + 32 * direction)
            tail = jnp.where(here, code, tail)

    loads[0].wait()
    x = x_v[...].reshape(ROWS, SAMP)
    x_high = x.astype(BF)
    x_low = (x - x_high.astype(F32)).astype(BF)
    x_both = jnp.concatenate(
        [dot(order, x_high).astype(BF), dot(order, x_low).astype(BF)], axis=0
    )
    both = None
    for load, (a, b) in zip(dft_loads, DFT_PARTS):
        load.wait()
        part = dot(x_both[:, a:b], dft_v[a:b, :])
        both = part if both is None else both + part
    loads[5].start()
    main = both[:ROWS, :256] + (both[ROWS:, :256] + both[:ROWS, 256:512])
    rest = both[:ROWS, 512:640] + jnp.where(lane128 < 32, both[ROWS:, 512:640], 0.0)
    rest = jnp.where(lane128 < 32, rest + pltpu.roll(rest, 96, 1), 0.0)
    rest = rest + pltpu.roll(rest, 32, 1)
    rest = rest + pltpu.roll(rest, 64, 1)
    real, imag = main[:, :MAIN], main[:, MAIN:]
    power = jnp.concatenate([real * real + imag * imag, rest * rest], axis=1)
    power_high = power.astype(BF)
    power_low = (power - power_high.astype(F32)).astype(BF)
    level = dot(jnp.concatenate([power_high, power_low], axis=0), weights)
    level = (level[:ROWS] + level[ROWS:]) * (1.0 / 288.0) + 1e-06
    factor = lax.rsqrt(level)
    factor_main = factor[:, :MAIN] * valid
    factor_rest = factor[:, MAIN:] * valid_group
    white = jnp.concatenate([real * factor_main, imag * factor_main], axis=1)
    own = jnp.concatenate([white, stack_group(rest * factor_rest), tail], axis=0).astype(BF)
    blk[...] = own
    gath[me] = own

    edges = jnp.where(exists[0], 1, 0) + jnp.where(exists[1], 1, 0)
    pl.semaphore_wait(barrier, NGRP - 1 + edges)

    def send(src, dst, send_sem, recv_sem, to_tile, to_member):
        return pltpu.make_async_remote_copy(
            src_ref=src, dst_ref=dst, send_sem=send_sem, recv_sem=recv_sem,
            device_id=(to_tile, to_member), device_id_type=MESH,
        )

    def gather_copy(j):
        return send(blk, gath.at[me], send_g.at[j], recv_g.at[me], tile, peer(j))

    def side_copy(g, src):
        return send(src, side.at[g], send_s.at[g], recv_s.at[g], side_tile, me)

    def far_copy(g, src):
        return send(src, far.at[g], send_x.at[g], recv_x.at[g], far_tile, me)

    def spread_copy(j):
        return send(far.at[me], far.at[me], send_b.at[j], recv_x.at[me], tile, peer(j))

    @pl.when(has_far)
    def _():
        far_copy(me, blk).start()

    for j in range(NGRP - 1):
        gather_copy(j).start()
    side_copy(me, blk).start()

    row, col = iota((BLK, BLK), 0), iota((BLK, BLK), 1)
    first_half = lax.rem(iota((8, 256), 1), 32) < 16

    def set_role(first, block):
        for s in range(SG):
            spread = (col == row // SG * SG + s).astype(F32).astype(BF)
            wide = dot(spread, block)
            role[first + s] = wide
            tail = wide[ROWS : ROWS + 8]
            ahead = jnp.concatenate(
                [pltpu.roll(tail[:, 0:128], 112, 1), pltpu.roll(tail[:, 128:], 112, 1)], axis=1
            )
            behind = jnp.concatenate(
                [pltpu.roll(tail[:, 0:128], 16, 1), pltpu.roll(tail[:, 128:], 16, 1)], axis=1
            )
            turned[first + s] = jnp.where(first_half, ahead, -behind)

    set_role(0, own)
    loads[4].wait()
    column, line = iota((96, 96), 0), iota((96, 96), 1)
    on_diagonal = column == line
    for s in range(SG):
        wanted = jnp.broadcast_to(mask_v[s : s + 1, :].astype(F32), (96, 96))
        kept = jnp.sum(jnp.where(on_diagonal, wanted, 0.0), axis=1, keepdims=True)
        keep_v[s] = jnp.broadcast_to(kept, (96, 128))

    lane = iota((8, 128), 1)
    last_lane = lax.rem(lane, 32) == 31
    rest_real = lax.rem(lane, 32) < 16

    def products(j, block):
        w_re, w_im = role[j, 0:ROWS, 0:128], role[j, 0:ROWS, 128:256]
        v_re, v_im = block[0:ROWS, 0:128], block[0:ROWS, 128:256]
        w_rest, v_rest = role[j, ROWS : ROWS + 8, :], block[ROWS : ROWS + 8]
        count = role[j, ROWS + 8 : BLK, :] * block[ROWS + 8 : BLK]
        rest_re = w_rest * v_rest
        rest_im = turned[j] * v_rest
        return [
            jnp.sum((w_re * v_re + w_im * v_im).reshape(-1, 8, 128), axis=0),
            jnp.sum((w_im * v_re - w_re * v_im).reshape(-1, 8, 128), axis=0),
            rest_re[:, 0:128] + rest_re[:, 128:],
            rest_im[:, 0:128] + rest_im[:, 128:],
            count[:, 0:128] + count[:, 128:],
        ]

    def finish(sums):
        re, im, rest_re, rest_im, count = sums
        count = lane_fold(count, (64, 32))
        count = jnp.where(last_lane, pltpu.roll(count, 1, 1), count)
        inverse = 1.0 / jnp.maximum(count, 1.0)
        rest_re = lane_fold(rest_re, (64, 32, 16))
        rest_im = lane_fold(rest_im, (64, 32, 16))
        return re * inverse, im * inverse, jnp.where(rest_real, rest_re, rest_im) * inverse

    def recv_wait(buffer, sems, g):
        pltpu.make_async_copy(buffer.at[g], buffer.at[g], sems.at[g]).wait()

    def columns(g, block, kind):
        block = block.astype(F32)
        for s in range(SG):
            sums = [a + pltpu.roll(a, 4, 0) for a in products(s, block)]
            done = finish(sums)
            for i in range(3):
                f_ref[i, pl.ds(g * 48 + kind * 16 + s, 4, stride=4), :] = done[i][0:4]

    @pl.when(jnp.logical_not(has_far))
    def _():
        far[...] = jnp.zeros(far.shape, BF)

    @pl.when(turn)
    def _():
        recv_wait(far, recv_x, me)
        for j in range(NGRP - 1):
            spread_copy(j).start()

    def own_columns(step, carry):
        g = member(step)

        @pl.when(g != me)
        def _():
            recv_wait(gath, recv_g, g)
            side_copy(g, gath.at[g]).start()

            @pl.when(straight)
            def _():
                far_copy(g, gath.at[g]).start()

        columns(g, gath[g], 0)
        return carry

    lax.fori_loop(0, NGRP, own_columns, 0)

    def outer_columns(step, carry):
        g = member(step)
        recv_wait(side, recv_s, g)
        columns(g, side[g], 2 - core)

        @pl.when(jnp.logical_or(straight, jnp.logical_and(turn, g != me)))
        def _():
            recv_wait(far, recv_x, g)

        columns(g, far[g], 1 + core)
        return carry

    lax.fori_loop(0, NGRP, outer_columns, 0)

    def codes(buffer, g, direction):
        rows = buffer[g, ROWS + 8 : BLK, 0:128].astype(F32)
        picked = jnp.where(lane == 31 + 32 * direction, rows, 0.0)
        return jnp.broadcast_to(jnp.sum(picked, axis=1, keepdims=True), (8, 128))

    even = core == 0
    for g in range(NGRP):
        side_code = codes(side, g, 1 - core)
        far_code = jnp.where(has_far, codes(far, g, core), DEAD)
        code_v[g * 12 : g * 12 + 4, :] = iota((4, 128), 0).astype(F32)
        code_v[g * 12 + 4 : g * 12 + 8, :] = jnp.where(even, far_code, side_code)[0:4]
        code_v[g * 12 + 8 : g * 12 + 12, :] = jnp.where(even, side_code, far_code)[0:4]
    same_list = column // SG == line // SG
    chosen = same_list & (lax.rem(line, SG).astype(F32) == code_v[:, 0:96])
    chosen = jnp.where(chosen, 1.0, 0.0)
    for s in range(SG):
        pick = (chosen * keep_v[s][:, 0:96]).astype(BF)
        rows = jnp.concatenate(
            [f_ref[i, pl.ds(s, 96, stride=4), :].astype(BF) for i in range(3)], axis=1
        )
        left_ref[s * 96 : (s + 1) * 96, :] = dot(pick, rows).astype(BF)

    for j in range(NGRP - 1):
        gather_copy(j).wait_send()
    side_copy(me, blk).wait_send()

    @pl.when(has_far)
    def _():
        far_copy(me, blk).wait_send()

    @pl.when(turn)
    def _():
        for j in range(NGRP - 1):
            spread_copy(j).wait_send()

    for j in range(NGRP - 1):
        g = peer(j)
        side_copy(g, gath.at[g]).wait_send()

        @pl.when(straight)
        def _():
            far_copy(g, gath.at[g]).wait_send()

    loads[5].wait()


def lag_kernel(left_ref, basis_ref, out_hbm, out_v, sems):
    copies = []
    for i, start in enumerate(range(0, LAGS, CHUNK)):
        series = dot(left_ref[:, 0 : 2 * NBIN], basis_ref[:, start : start + CHUNK])
        stop = min(start + CHUNK, LAGS)
        series = series[:, : stop - start].reshape(SG, 96, stop - start)
        out_v[:, :, start:stop] = series.astype(BF)
        copies.append(
            pltpu.make_async_copy(
                out_v.at[:, :, start:stop], out_hbm.at[:, :, start:stop], sems.at[i]
            )
        )
        copies[-1].start()
    for copy in copies:
        copy.wait()


def on_device(n_tile, traces, validity, boundary_rows, boundary_count, pair_mask):
    dft = jnp.asarray(dft_table())
    anywhere = pl.BlockSpec(memory_space=pltpu.MemorySpace.HBM)
    dma = pltpu.SemaphoreType.DMA
    vmem = pl.BlockSpec(memory_space=pltpu.VMEM)
    basis = jnp.asarray(lag_table())
    left, basis = pl.pallas_call(
        functools.partial(cross_kernel, n_tile),
        out_shape=(
            jax.ShapeDtypeStruct((SG * 96, 384), BF),
            jax.ShapeDtypeStruct(basis.shape, BF),
        ),
        in_specs=[anywhere] * 7,
        out_specs=(vmem, vmem),
        scratch_shapes=[
            pltpu.VMEM((SG, SEG, SAMP), F32),
            pltpu.VMEM((SG, SEG), jnp.int32),
            pltpu.SMEM((1, 2, SG), jnp.int32),
            pltpu.SMEM((1, 2), jnp.int32),
            pltpu.VMEM((SG, 96), jnp.int32),
            pltpu.VMEM(dft.shape, BF),
            pltpu.VMEM((BLK, 256), BF),
            pltpu.VMEM((NGRP, BLK, 256), BF),
            pltpu.VMEM((NGRP, BLK, 256), BF),
            pltpu.VMEM((NGRP, BLK, 256), BF),
            pltpu.VMEM((SG, BLK, 256), F32),
            pltpu.VMEM((SG, 8, 256), F32),
            pltpu.VMEM((SG, 96, 128), F32),
            pltpu.VMEM((96, 128), F32),
            pltpu.VMEM((3, SG * 96, 128), F32),
            dma((6,)), dma((len(DFT_PARTS),)),
            dma((7,)), dma((8,)), dma((8,)), dma((7,)), dma((8,)), dma((8,)), dma((8,)),
        ],
        compiler_params=pltpu.CompilerParams(
            collective_id=0, has_side_effects=True, vmem_limit_bytes=24 << 20
        ),
        name="cross",
    )(*[
        pltpu.with_memory_space_constraint(array, pltpu.MemorySpace.HBM)
        for array in (
            traces, validity, boundary_rows, boundary_count, pair_mask, dft, basis
        )
    ])
    return pl.pallas_call(
        lag_kernel,
        out_shape=jax.ShapeDtypeStruct((SG, 96, LAGS), BF),
        in_specs=[vmem, vmem],
        out_specs=pl.BlockSpec(memory_space=pl.ANY),
        scratch_shapes=[
            pltpu.VMEM((SG, 96, LAGS), BF),
            pltpu.SemaphoreType.DMA((pl.cdiv(LAGS, CHUNK),)),
        ],
        compiler_params=pltpu.CompilerParams(vmem_limit_bytes=24 << 20),
        name="lags",
    )(left, basis)


def solution(mesh):
    three = P(("tile", "grp"), None, None)
    two = P(("tile", "grp"), None)
    return jax.shard_map(
        functools.partial(on_device, mesh.shape["tile"]),
        mesh=mesh,
        in_specs=(three, two, three, two, two),
        out_specs=three,
        check_vma=False,
    )
```

```python
import functools
import math

import jax
import jax.numpy as jnp
import ml_dtypes
import numpy as np
from jax import lax
from jax.experimental import pallas as pl
from jax.experimental.pallas import tpu as pltpu
from jax.sharding import PartitionSpec as P

SG = 4
SEG = 16
SAMP = 1500
NBIN = 144
MAXLAG = 1000
LAGS = 2001
NGRP = 8
MAIN = 128
ROWS = SG * SEG
BLK = ROWS + 16
CHUNK = 512
X_RUN = 8
DEAD = 128.0
DFT_PARTS = ((0, 512), (512, 1024), (1024, SAMP))
BF = jnp.bfloat16
F32 = jnp.float32
MESH = pl.DeviceIdType.MESH


def split_halves(table):
    high = table.astype(ml_dtypes.bfloat16)
    low = (table - high.astype(np.float64)).astype(ml_dtypes.bfloat16)
    return high, low


def dft_table():
    n = np.arange(SAMP, dtype=np.int64)[:, None]
    k = np.arange(1, NBIN + 1, dtype=np.int64)[None, :]
    angle = ((n * k) % (2 * SAMP)).astype(np.float64) * (2.0 * np.pi / (2 * SAMP))
    taper = 0.5 - 0.5 * np.cos(2.0 * np.pi * n / SAMP)
    cos, sin = taper * np.cos(angle), -taper * np.sin(angle)
    main = np.concatenate([cos[:, :MAIN], sin[:, :MAIN]], axis=1)
    rest = np.concatenate([cos[:, MAIN:], sin[:, MAIN:]], axis=1)
    main_high, main_low = split_halves(main)
    rest_high, rest_low = split_halves(rest)
    unused = np.zeros((SAMP, 64), ml_dtypes.bfloat16)
    return np.concatenate([main_high, main_low, rest_high, rest_low, unused], axis=1)


def lag_table():
    k = np.arange(1, NBIN + 1, dtype=np.int64)[:, None]
    lag = np.arange(LAGS, dtype=np.int64)[None, :] - MAXLAG
    angle = ((k * lag) % (2 * SAMP)).astype(np.float64) * (2.0 * np.pi / (2 * SAMP))
    cos = np.cos(angle) / math.sqrt(NBIN)
    sin = -np.sin(angle) / math.sqrt(NBIN)
    table = np.concatenate([cos[:MAIN], sin[:MAIN], cos[MAIN:], sin[MAIN:]], axis=0)
    table = np.pad(table, ((0, 0), (0, -LAGS % CHUNK)))
    return table.astype(ml_dtypes.bfloat16)


def iota(shape, axis):
    return lax.broadcasted_iota(jnp.int32, shape, axis)


def dot(a, b):
    return jnp.dot(a, b, preferred_element_type=F32)


def lane_fold(a, shifts):
    for shift in shifts:
        a = a + pltpu.roll(a, shift, 1)
    return a


def bin_of(lane):
    return jnp.where(lane < MAIN, lane, MAIN + lax.rem(lane, 16))


def power_weights():
    shape = (256, 256)
    source, target = iota(shape, 0), iota(shape, 1)
    near = jnp.abs(bin_of(source) - bin_of(target)) <= 4
    return jnp.where(source < MAIN + 32, jnp.where(near, 17.0, 1.0), 0.0).astype(BF)


def cross_kernel(
    n_tile, x_hbm, val_hbm, rows_hbm, cnt_hbm, mask_hbm, dft_hbm, basis_hbm,
    left_ref, basis_ref,
    x_v, val_v, rows_s, cnt_s, mask_v, dft_v, blk, gath, side, far, role, turned,
    keep_v, code_v, raw, f_ref, load_sem, dft_sem, send_g, send_s, send_x, send_b,
    recv_g, recv_s, recv_x,
):
    tile, me = lax.axis_index("tile"), lax.axis_index("grp")
    my_step = lax.rem(me, 4) * 2 + me // 4
    neighbour = (tile + 1, tile - 1)
    exists = (tile < n_tile - 1, tile > 0)
    core = lax.rem(tile, 2)
    side_tile = tile + 1 - 2 * core
    far_tile = tile - 1 + 2 * core
    has_far = jnp.logical_and(far_tile >= 0, far_tile < n_tile)
    turn = jnp.logical_and(has_far, (far_tile + X_RUN) // X_RUN != (tile + X_RUN) // X_RUN)
    straight = jnp.logical_and(has_far, jnp.logical_not(turn))

    def member(step):
        return lax.rem(step, 2) * 4 + step // 2

    def peer(j):
        return member(j + jnp.where(my_step <= j, 1, 0))

    loads = [
        pltpu.make_async_copy(src, dst, load_sem.at[i])
        for i, (src, dst) in enumerate(
            [(x_hbm, x_v), (val_hbm, val_v), (rows_hbm, rows_s), (cnt_hbm, cnt_s),
             (mask_hbm, mask_v), (basis_hbm, basis_ref)]
        )
    ]
    dft_loads = [
        pltpu.make_async_copy(dft_hbm.at[a:b], dft_v.at[a:b], dft_sem.at[i])
        for i, (a, b) in enumerate(DFT_PARTS)
    ]
    loads[0].start()
    loads[1].start()
    for load in dft_loads:
        load.start()
    for load in loads[2:5]:
        load.start()

    barrier = pltpu.get_barrier_semaphore()
    for j in range(NGRP - 1):
        pl.semaphore_signal(barrier, inc=1, device_id=(tile, peer(j)), device_id_type=MESH)
    for direction in range(2):

        @pl.when(exists[direction])
        def _():
            pl.semaphore_signal(
                barrier, inc=1, device_id=(neighbour[direction], me), device_id_type=MESH
            )

    row64, col64 = iota((ROWS, ROWS), 0), iota((ROWS, ROWS), 1)
    order = (col64 == lax.rem(row64, SG) * SEG + row64 // SG).astype(F32).astype(BF)
    weights = power_weights()
    loads[1].wait()
    same_group = iota((ROWS, 128), 1) // 32 == iota((ROWS, 128), 0) // 16
    lane128 = iota((ROWS, 128), 1)
    valid_parts = []
    for s in range(SG):
        row = jnp.broadcast_to(val_v[s : s + 1, :].astype(F32), (SEG, SEG))
        diag = jnp.where(iota((SEG, SEG), 0) == iota((SEG, SEG), 1), row, 0.0)
        valid_parts.append(jnp.sum(diag, axis=1, keepdims=True))
    valid = jnp.broadcast_to(jnp.concatenate(valid_parts, axis=0), (ROWS, 128))
    valid = dot(order, valid.astype(BF))
    valid_group = jnp.where(same_group, valid, 0.0)
    loads[2].wait()
    loads[3].wait()

    def stack_group(a):
        packed = (a[0:16] + a[16:32]) + (a[32:48] + a[48:64])
        return jnp.concatenate([packed[0:8], packed[8:16]], axis=1)

    tail = stack_group(valid_group)
    tail_row, tail_lane = iota((8, 256), 0), iota((8, 256), 1)
    tail = jnp.where(lax.rem(tail_lane, 32) == 31, 0.0, tail)
    for direction in range(2):
        for h in range(SG):
            code = jnp.where(
                h < cnt_s[0, direction], rows_s[0, direction, h].astype(F32), DEAD
            )
            here = (tail_row == h) & (tail_lane == 31 + 32 * direction)
            tail = jnp.where(here, code, tail)

    loads[0].wait()
    x = x_v[...].reshape(ROWS, SAMP)
    x_high = x.astype(BF)
    x_low = (x - x_high.astype(F32)).astype(BF)
    x_both = jnp.concatenate(
        [dot(order, x_high).astype(BF), dot(order, x_low).astype(BF)], axis=0
    )
    both = None
    for load, (a, b) in zip(dft_loads, DFT_PARTS):
        load.wait()
        part = dot(x_both[:, a:b], dft_v[a:b, :])
        both = part if both is None else both + part
    loads[5].start()
    main = both[:ROWS, :256] + (both[ROWS:, :256] + both[:ROWS, 256:512])
    rest = both[:ROWS, 512:640] + jnp.where(lane128 < 32, both[ROWS:, 512:640], 0.0)
    rest = jnp.where(lane128 < 32, rest + pltpu.roll(rest, 96, 1), 0.0)
    rest = rest + pltpu.roll(rest, 32, 1)
    rest = rest + pltpu.roll(rest, 64, 1)
    real, imag = main[:, :MAIN], main[:, MAIN:]
    power = jnp.concatenate([real * real + imag * imag, rest * rest], axis=1)
    power_high = power.astype(BF)
    power_low = (power - power_high.astype(F32)).astype(BF)
    level = dot(jnp.concatenate([power_high, power_low], axis=0), weights)
    level = (level[:ROWS] + level[ROWS:]) * (1.0 / 288.0) + 1e-06
    factor = lax.rsqrt(level)
    factor_main = factor[:, :MAIN] * valid
    factor_rest = factor[:, MAIN:] * valid_group
    white = jnp.concatenate([real * factor_main, imag * factor_main], axis=1)
    own = jnp.concatenate([white, stack_group(rest * factor_rest), tail], axis=0).astype(BF)
    blk[...] = own
    gath[me] = own

    edges = jnp.where(exists[0], 1, 0) + jnp.where(exists[1], 1, 0)
    pl.semaphore_wait(barrier, NGRP - 1 + edges)

    def send(src, dst, send_sem, recv_sem, to_tile, to_member):
        return pltpu.make_async_remote_copy(
            src_ref=src, dst_ref=dst, send_sem=send_sem, recv_sem=recv_sem,
            device_id=(to_tile, to_member), device_id_type=MESH,
        )

    def gather_copy(j):
        return send(blk, gath.at[me], send_g.at[j], recv_g.at[me], tile, peer(j))

    def side_copy(g, src):
        return send(src, side.at[g], send_s.at[g], recv_s.at[g], side_tile, me)

    def far_copy(g, src):
        return send(src, far.at[g], send_x.at[g], recv_x.at[g], far_tile, me)

    def spread_copy(j):
        return send(far.at[me], far.at[me], send_b.at[j], recv_x.at[me], tile, peer(j))

    @pl.when(has_far)
    def _():
        far_copy(me, blk).start()

    for j in range(NGRP - 1):
        gather_copy(j).start()
    side_copy(me, blk).start()

    row, col = iota((BLK, BLK), 0), iota((BLK, BLK), 1)
    first_half = lax.rem(iota((8, 256), 1), 32) < 16

    def set_role(first, block):
        for s in range(SG):
            spread = (col == row // SG * SG + s).astype(F32).astype(BF)
            wide = dot(spread, block)
            role[first + s] = wide
            tail = wide[ROWS : ROWS + 8]
            ahead = jnp.concatenate(
                [pltpu.roll(tail[:, 0:128], 112, 1), pltpu.roll(tail[:, 128:], 112, 1)], axis=1
            )
            behind = jnp.concatenate(
                [pltpu.roll(tail[:, 0:128], 16, 1), pltpu.roll(tail[:, 128:], 16, 1)], axis=1
            )
            turned[first + s] = jnp.where(first_half, ahead, -behind)

    set_role(0, own)
    loads[4].wait()
    column, line = iota((96, 96), 0), iota((96, 96), 1)
    on_diagonal = column == line
    for s in range(SG):
        wanted = jnp.broadcast_to(mask_v[s : s + 1, :].astype(F32), (96, 96))
        kept = jnp.sum(jnp.where(on_diagonal, wanted, 0.0), axis=1, keepdims=True)
        keep_v[s] = jnp.broadcast_to(kept, (96, 128))

    lane = iota((8, 128), 1)
    last_lane = lax.rem(lane, 32) == 31
    low_half = iota((8, 128), 0) < 4
    rest_real = lax.rem(lane, 32) < 16

    def products(j, block):
        w_re, w_im = role[j, 0:ROWS, 0:128], role[j, 0:ROWS, 128:256]
        v_re, v_im = block[0:ROWS, 0:128], block[0:ROWS, 128:256]
        w_rest, v_rest = role[j, ROWS : ROWS + 8, :], block[ROWS : ROWS + 8]
        count = role[j, ROWS + 8 : BLK, :] * block[ROWS + 8 : BLK]
        rest_re = w_rest * v_rest
        rest_im = turned[j] * v_rest
        return [
            jnp.sum((w_re * v_re + w_im * v_im).reshape(-1, 8, 128), axis=0),
            jnp.sum((w_im * v_re - w_re * v_im).reshape(-1, 8, 128), axis=0),
            rest_re[:, 0:128] + rest_re[:, 128:],
            rest_im[:, 0:128] + rest_im[:, 128:],
            count[:, 0:128] + count[:, 128:],
        ]

    def finish(sums):
        re, im, rest_re, rest_im, count = sums
        count = lane_fold(count, (64, 32))
        count = jnp.where(last_lane, pltpu.roll(count, 1, 1), count)
        inverse = 1.0 / jnp.maximum(count, 1.0)
        rest_re = lane_fold(rest_re, (64, 32, 16))
        rest_im = lane_fold(rest_im, (64, 32, 16))
        return re * inverse, im * inverse, jnp.where(rest_real, rest_re, rest_im) * inverse

    def recv_wait(buffer, sems, g):
        pltpu.make_async_copy(buffer.at[g], buffer.at[g], sems.at[g]).wait()

    def columns(g, block, kind):
        block = block.astype(F32)
        rows = pl.ds(pl.multiple_of(g * 8, 8), 8)
        for s in range(SG):
            for i, part in enumerate(products(s, block)):
                raw[s, kind, i, rows, :] = part

    def settle(kind):
        for s in range(SG):
            for pair in range(NGRP // 2):
                parts = []
                for i in range(5):
                    a = raw[s, kind, i, 16 * pair : 16 * pair + 8, :]
                    b = raw[s, kind, i, 16 * pair + 8 : 16 * pair + 16, :]
                    crossed = pltpu.roll(jnp.where(low_half, b, a), 4, 0)
                    parts.append(jnp.where(low_half, a, b) + crossed)
                start = kind * 32 + 8 * pair
                for i, part in enumerate(finish(parts)):
                    f_ref[s, start : start + 8, 128 * i : 128 * i + 128] = part

    @pl.when(jnp.logical_not(has_far))
    def _():
        far[...] = jnp.zeros(far.shape, BF)

    @pl.when(turn)
    def _():
        recv_wait(far, recv_x, me)
        for j in range(NGRP - 1):
            spread_copy(j).start()

    def own_columns(step, carry):
        g = member(step)

        @pl.when(g != me)
        def _():
            recv_wait(gath, recv_g, g)
            side_copy(g, gath.at[g]).start()

            @pl.when(straight)
            def _():
                far_copy(g, gath.at[g]).start()

        columns(g, gath[g], 0)
        return carry

    lax.fori_loop(0, NGRP, own_columns, 0)
    settle(0)

    def side_columns(step, carry):
        g = member(step)
        recv_wait(side, recv_s, g)
        columns(g, side[g], 1)
        return carry

    lax.fori_loop(0, NGRP, side_columns, 0)
    settle(1)

    def far_columns(step, carry):
        g = member(step)

        @pl.when(jnp.logical_or(straight, jnp.logical_and(turn, g != me)))
        def _():
            recv_wait(far, recv_x, g)

        columns(g, far[g], 2)
        return carry

    lax.fori_loop(0, NGRP, far_columns, 0)

    def codes(buffer, g, direction):
        rows = buffer[g, ROWS + 8 : BLK, 0:128].astype(F32)
        picked = jnp.where(lane == 31 + 32 * direction, rows, 0.0)
        return jnp.broadcast_to(jnp.sum(picked, axis=1, keepdims=True), (8, 128))

    even = core == 0
    for g in range(NGRP):
        side_code = codes(side, g, 1 - core) + (32.0 + 4 * g)
        far_code = jnp.where(has_far, codes(far, g, core), DEAD) + (64.0 + 4 * g)
        code_v[g * 12 : g * 12 + 4, :] = iota((4, 128), 0).astype(F32) + 4.0 * g
        code_v[g * 12 + 4 : g * 12 + 8, :] = jnp.where(even, far_code, side_code)[0:4]
        code_v[g * 12 + 8 : g * 12 + 12, :] = jnp.where(even, side_code, far_code)[0:4]
    chosen = jnp.where(line.astype(F32) == code_v[:, 0:96], 1.0, 0.0)
    settle(2)
    for s in range(SG):
        pick = (chosen * keep_v[s][:, 0:96]).astype(BF)
        left_ref[s * 96 : (s + 1) * 96, :] = dot(pick, f_ref[s].astype(BF)).astype(BF)

    for j in range(NGRP - 1):
        gather_copy(j).wait_send()
    side_copy(me, blk).wait_send()

    @pl.when(has_far)
    def _():
        far_copy(me, blk).wait_send()

    @pl.when(turn)
    def _():
        for j in range(NGRP - 1):
            spread_copy(j).wait_send()

    for j in range(NGRP - 1):
        g = peer(j)
        side_copy(g, gath.at[g]).wait_send()

        @pl.when(straight)
        def _():
            far_copy(g, gath.at[g]).wait_send()

    loads[5].wait()


def lag_kernel(left_ref, basis_ref, out_hbm, out_v, sems):
    copies = []
    for i, start in enumerate(range(0, LAGS, CHUNK)):
        series = dot(left_ref[:, 0 : 2 * NBIN], basis_ref[:, start : start + CHUNK])
        stop = min(start + CHUNK, LAGS)
        series = series[:, : stop - start].reshape(SG, 96, stop - start)
        out_v[:, :, start:stop] = series.astype(BF)
        copies.append(
            pltpu.make_async_copy(
                out_v.at[:, :, start:stop], out_hbm.at[:, :, start:stop], sems.at[i]
            )
        )
        copies[-1].start()
    for copy in copies:
        copy.wait()


def on_device(n_tile, traces, validity, boundary_rows, boundary_count, pair_mask):
    dft = jnp.asarray(dft_table())
    anywhere = pl.BlockSpec(memory_space=pltpu.MemorySpace.HBM)
    dma = pltpu.SemaphoreType.DMA
    vmem = pl.BlockSpec(memory_space=pltpu.VMEM)
    basis = jnp.asarray(lag_table())
    left, basis = pl.pallas_call(
        functools.partial(cross_kernel, n_tile),
        out_shape=(
            jax.ShapeDtypeStruct((SG * 96, 384), BF),
            jax.ShapeDtypeStruct(basis.shape, BF),
        ),
        in_specs=[anywhere] * 7,
        out_specs=(vmem, vmem),
        scratch_shapes=[
            pltpu.VMEM((SG, SEG, SAMP), F32),
            pltpu.VMEM((SG, SEG), jnp.int32),
            pltpu.SMEM((1, 2, SG), jnp.int32),
            pltpu.SMEM((1, 2), jnp.int32),
            pltpu.VMEM((SG, 96), jnp.int32),
            pltpu.VMEM(dft.shape, BF),
            pltpu.VMEM((BLK, 256), BF),
            pltpu.VMEM((NGRP, BLK, 256), BF),
            pltpu.VMEM((NGRP, BLK, 256), BF),
            pltpu.VMEM((NGRP, BLK, 256), BF),
            pltpu.VMEM((SG, BLK, 256), F32),
            pltpu.VMEM((SG, 8, 256), F32),
            pltpu.VMEM((SG, 96, 128), F32),
            pltpu.VMEM((96, 128), F32),
            pltpu.VMEM((SG, 3, 5, 64, 128), F32),
            pltpu.VMEM((SG, 96, 384), F32),
            dma((6,)), dma((len(DFT_PARTS),)),
            dma((7,)), dma((8,)), dma((8,)), dma((7,)), dma((8,)), dma((8,)), dma((8,)),
        ],
        compiler_params=pltpu.CompilerParams(
            collective_id=0, has_side_effects=True, vmem_limit_bytes=24 << 20
        ),
        name="cross",
    )(*[
        pltpu.with_memory_space_constraint(array, pltpu.MemorySpace.HBM)
        for array in (
            traces, validity, boundary_rows, boundary_count, pair_mask, dft, basis
        )
    ])
    return pl.pallas_call(
        lag_kernel,
        out_shape=jax.ShapeDtypeStruct((SG, 96, LAGS), BF),
        in_specs=[vmem, vmem],
        out_specs=pl.BlockSpec(memory_space=pl.ANY),
        scratch_shapes=[
            pltpu.VMEM((SG, 96, LAGS), BF),
            pltpu.SemaphoreType.DMA((pl.cdiv(LAGS, CHUNK),)),
        ],
        compiler_params=pltpu.CompilerParams(vmem_limit_bytes=24 << 20),
        name="lags",
    )(left, basis)


def solution(mesh):
    three = P(("tile", "grp"), None, None)
    two = P(("tile", "grp"), None)
    return jax.shard_map(
        functools.partial(on_device, mesh.shape["tile"]),
        mesh=mesh,
        in_specs=(three, two, three, two, two),
        out_specs=three,
        check_vma=False,
    )
```

```python
import functools
import math

import jax
import jax.numpy as jnp
import ml_dtypes
import numpy as np
from jax import lax
from jax.experimental import pallas as pl
from jax.experimental.pallas import tpu as pltpu
from jax.sharding import PartitionSpec as P

SG = 4
SEG = 16
SAMP = 1500
NBIN = 144
MAXLAG = 1000
LAGS = 2001
NGRP = 8
MAIN = 128
ROWS = SG * SEG
BLK = ROWS + 16
CHUNK = 512
X_RUN = 8
DEAD = 128.0
DFT_PARTS = ((0, 512), (512, 1024), (1024, SAMP))
BF = jnp.bfloat16
F32 = jnp.float32
MESH = pl.DeviceIdType.MESH


def split_halves(table):
    high = table.astype(ml_dtypes.bfloat16)
    low = (table - high.astype(np.float64)).astype(ml_dtypes.bfloat16)
    return high, low


def dft_table():
    n = np.arange(SAMP, dtype=np.int64)[:, None]
    k = np.arange(1, NBIN + 1, dtype=np.int64)[None, :]
    angle = ((n * k) % (2 * SAMP)).astype(np.float64) * (2.0 * np.pi / (2 * SAMP))
    taper = 0.5 - 0.5 * np.cos(2.0 * np.pi * n / SAMP)
    cos, sin = taper * np.cos(angle), -taper * np.sin(angle)
    main = np.concatenate([cos[:, :MAIN], sin[:, :MAIN]], axis=1)
    rest = np.concatenate([cos[:, MAIN:], sin[:, MAIN:]], axis=1)
    main_high, main_low = split_halves(main)
    rest_high, rest_low = split_halves(rest)
    unused = np.zeros((SAMP, 64), ml_dtypes.bfloat16)
    return np.concatenate([main_high, main_low, rest_high, rest_low, unused], axis=1)


def lag_table():
    k = np.arange(1, NBIN + 1, dtype=np.int64)[:, None]
    lag = np.arange(LAGS, dtype=np.int64)[None, :] - MAXLAG
    angle = ((k * lag) % (2 * SAMP)).astype(np.float64) * (2.0 * np.pi / (2 * SAMP))
    cos = np.cos(angle) / math.sqrt(NBIN)
    sin = -np.sin(angle) / math.sqrt(NBIN)
    table = np.concatenate([cos[:MAIN], sin[:MAIN], cos[MAIN:], sin[MAIN:]], axis=0)
    table = np.pad(table, ((0, 0), (0, -LAGS % CHUNK)))
    return table.astype(ml_dtypes.bfloat16)


def iota(shape, axis):
    return lax.broadcasted_iota(jnp.int32, shape, axis)


def dot(a, b):
    return jnp.dot(a, b, preferred_element_type=F32)


def lane_fold(a, shifts):
    for shift in shifts:
        a = a + pltpu.roll(a, shift, 1)
    return a


def bin_of(lane):
    return jnp.where(lane < MAIN, lane, MAIN + lax.rem(lane, 16))


def power_weights():
    shape = (256, 256)
    source, target = iota(shape, 0), iota(shape, 1)
    near = jnp.abs(bin_of(source) - bin_of(target)) <= 4
    return jnp.where(source < MAIN + 32, jnp.where(near, 17.0, 1.0), 0.0).astype(BF)


def cross_kernel(
    n_tile, x_hbm, val_hbm, rows_hbm, cnt_hbm, mask_hbm, dft_hbm, basis_hbm,
    left_ref, basis_ref,
    x_v, val_v, rows_s, cnt_s, mask_v, dft_v, blk, edge, gath, side, far, nbin, role, turned,
    keep_v, code_v, raw, f_ref, far_f, out2, in2, load_sem, dft_sem,
    send_g, send_s, send_x, send_n, send_p, recv_g, recv_s, recv_x, recv_n, recv_p,
):
    tile, me = lax.axis_index("tile"), lax.axis_index("grp")
    my_step = lax.rem(me, 4) * 2 + me // 4
    neighbour = (tile + 1, tile - 1)
    exists = (tile < n_tile - 1, tile > 0)
    core = lax.rem(tile, 2)
    side_tile = tile + 1 - 2 * core
    far_tile = tile - 1 + 2 * core
    has_far = jnp.logical_and(far_tile >= 0, far_tile < n_tile)
    even = core == 0
    odd = core == 1
    turn = (far_tile + X_RUN) // X_RUN != (tile + X_RUN) // X_RUN
    takes_blocks = jnp.logical_and(even, jnp.logical_and(has_far, jnp.logical_not(turn)))
    gives_blocks = jnp.logical_and(odd, jnp.logical_and(has_far, jnp.logical_not(turn)))
    takes_results = jnp.logical_and(has_far, jnp.logical_or(odd, turn))
    gives_edge = jnp.logical_and(has_far, jnp.logical_or(even, turn))

    def member(step):
        return lax.rem(step, 2) * 4 + step // 2

    def near(step):
        d = jnp.where(step < 2, 4 * step, jnp.where(step < 6, 2 * step - 3, 4 * step - 22))
        return lax.rem(me // 4 + d // 4, 2) * 4 + lax.rem(lax.rem(me, 4) + lax.rem(d, 4), 4)

    def peer(j):
        return member(j + jnp.where(my_step <= j, 1, 0))

    loads = [
        pltpu.make_async_copy(src, dst, load_sem.at[i])
        for i, (src, dst) in enumerate(
            [(x_hbm, x_v), (val_hbm, val_v), (rows_hbm, rows_s), (cnt_hbm, cnt_s),
             (mask_hbm, mask_v), (basis_hbm, basis_ref)]
        )
    ]
    dft_loads = [
        pltpu.make_async_copy(dft_hbm.at[a:b], dft_v.at[a:b], dft_sem.at[i])
        for i, (a, b) in enumerate(DFT_PARTS)
    ]
    loads[0].start()
    loads[1].start()
    for load in dft_loads:
        load.start()
    for load in loads[2:5]:
        load.start()

    barrier = pltpu.get_barrier_semaphore()
    for j in range(NGRP - 1):
        pl.semaphore_signal(barrier, inc=1, device_id=(tile, peer(j)), device_id_type=MESH)
    for direction in range(2):

        @pl.when(exists[direction])
        def _():
            pl.semaphore_signal(
                barrier, inc=1, device_id=(neighbour[direction], me), device_id_type=MESH
            )

    row64, col64 = iota((ROWS, ROWS), 0), iota((ROWS, ROWS), 1)
    order = (col64 == lax.rem(row64, SG) * SEG + row64 // SG).astype(F32).astype(BF)
    weights = power_weights()
    loads[1].wait()
    same_group = iota((ROWS, 128), 1) // 32 == iota((ROWS, 128), 0) // 16
    lane128 = iota((ROWS, 128), 1)
    valid_parts = []
    for s in range(SG):
        row = jnp.broadcast_to(val_v[s : s + 1, :].astype(F32), (SEG, SEG))
        diag = jnp.where(iota((SEG, SEG), 0) == iota((SEG, SEG), 1), row, 0.0)
        valid_parts.append(jnp.sum(diag, axis=1, keepdims=True))
    valid = jnp.broadcast_to(jnp.concatenate(valid_parts, axis=0), (ROWS, 128))
    valid = dot(order, valid.astype(BF))
    valid_group = jnp.where(same_group, valid, 0.0)
    loads[2].wait()
    loads[3].wait()

    def stack_group(a):
        packed = (a[0:16] + a[16:32]) + (a[32:48] + a[48:64])
        return jnp.concatenate([packed[0:8], packed[8:16]], axis=1)

    tail = stack_group(valid_group)
    tail_row, tail_lane = iota((8, 256), 0), iota((8, 256), 1)
    tail = jnp.where(lax.rem(tail_lane, 32) == 31, 0.0, tail)
    for direction in range(2):
        for h in range(SG):
            code = jnp.where(
                h < cnt_s[0, direction], rows_s[0, direction, h].astype(F32), DEAD
            )
            here = (tail_row == h) & (tail_lane == 31 + 32 * direction)
            tail = jnp.where(here, code, tail)

    r80, c80 = iota((BLK, BLK), 0), iota((BLK, BLK), 1)
    within = lax.rem(r80, SG)
    wanted = jnp.zeros((BLK, BLK), jnp.int32)
    for h in range(SG):
        chosen = jnp.where(even, rows_s[0, 1, h], rows_s[0, 0, h])
        live = h < jnp.where(even, cnt_s[0, 1], cnt_s[0, 0])
        wanted = jnp.where(within == h, jnp.where(live, chosen, SG), wanted)
    pick_far = (r80 // SG == c80 // SG) & (lax.rem(c80, SG) == wanted)
    pick_far = jnp.where(pick_far, 1.0, 0.0).astype(BF)

    loads[0].wait()
    x = x_v[...].reshape(ROWS, SAMP)
    x_high = x.astype(BF)
    x_low = (x - x_high.astype(F32)).astype(BF)
    x_both = jnp.concatenate(
        [dot(order, x_high).astype(BF), dot(order, x_low).astype(BF)], axis=0
    )
    both = None
    for load, (a, b) in zip(dft_loads, DFT_PARTS):
        load.wait()
        part = dot(x_both[:, a:b], dft_v[a:b, :])
        both = part if both is None else both + part
    loads[5].start()
    main = both[:ROWS, :256] + (both[ROWS:, :256] + both[:ROWS, 256:512])
    rest = both[:ROWS, 512:640] + jnp.where(lane128 < 32, both[ROWS:, 512:640], 0.0)
    rest = jnp.where(lane128 < 32, rest + pltpu.roll(rest, 96, 1), 0.0)
    rest = rest + pltpu.roll(rest, 32, 1)
    rest = rest + pltpu.roll(rest, 64, 1)
    real, imag = main[:, :MAIN], main[:, MAIN:]
    power = jnp.concatenate([real * real + imag * imag, rest * rest], axis=1)
    power_high = power.astype(BF)
    power_low = (power - power_high.astype(F32)).astype(BF)
    level = dot(jnp.concatenate([power_high, power_low], axis=0), weights)
    level = (level[:ROWS] + level[ROWS:]) * (1.0 / 288.0) + 1e-06
    factor = lax.rsqrt(level)
    factor_main = factor[:, :MAIN] * valid
    factor_rest = factor[:, MAIN:] * valid_group
    white = jnp.concatenate([real * factor_main, imag * factor_main], axis=1)
    own = jnp.concatenate([white, stack_group(rest * factor_rest), tail], axis=0).astype(BF)
    blk[...] = own
    gath[me] = own

    edges = jnp.where(exists[0], 1, 0) + jnp.where(exists[1], 1, 0)
    pl.semaphore_wait(barrier, NGRP - 1 + edges)

    def send(src, dst, send_sem, recv_sem, to_tile, to_member):
        return pltpu.make_async_remote_copy(
            src_ref=src, dst_ref=dst, send_sem=send_sem, recv_sem=recv_sem,
            device_id=(to_tile, to_member), device_id_type=MESH,
        )

    def gather_copy(j):
        return send(blk, gath.at[me], send_g.at[j], recv_g.at[me], tile, peer(j))

    def side_copy(g, src):
        return send(src, side.at[g], send_s.at[g], recv_s.at[g], side_tile, me)

    def far_copy(g, src):
        return send(src, far.at[g], send_x.at[g], recv_x.at[g], far_tile, me)

    def edge_copy():
        return send(edge, nbin, send_n, recv_n, far_tile, me)

    def result_copy(g):
        return send(out2.at[g], in2.at[me], send_p.at[g], recv_p.at[me], tile, g)

    row, col = iota((BLK, BLK), 0), iota((BLK, BLK), 1)
    edge[...] = dot(pick_far, own).astype(BF)

    @pl.when(gives_edge)
    def _():
        edge_copy().start()

    @pl.when(gives_blocks)
    def _():
        far_copy(me, blk).start()

    for j in range(NGRP - 1):
        gather_copy(j).start()
    side_copy(me, blk).start()

    first_half = lax.rem(iota((8, 256), 1), 32) < 16

    def set_role(first, block):
        for s in range(SG):
            spread = (col == row // SG * SG + s).astype(F32).astype(BF)
            wide = dot(spread, block)
            role[first + s] = wide
            tail = wide[ROWS : ROWS + 8]
            ahead = jnp.concatenate(
                [pltpu.roll(tail[:, 0:128], 112, 1), pltpu.roll(tail[:, 128:], 112, 1)], axis=1
            )
            behind = jnp.concatenate(
                [pltpu.roll(tail[:, 0:128], 16, 1), pltpu.roll(tail[:, 128:], 16, 1)], axis=1
            )
            turned[first + s] = jnp.where(first_half, ahead, -behind)

    set_role(0, own)
    loads[4].wait()
    column, line = iota((96, 96), 0), iota((96, 96), 1)
    on_diagonal = column == line
    for s in range(SG):
        wanted = jnp.broadcast_to(mask_v[s : s + 1, :].astype(F32), (96, 96))
        kept = jnp.sum(jnp.where(on_diagonal, wanted, 0.0), axis=1, keepdims=True)
        keep_v[s] = jnp.broadcast_to(kept, (96, 128))

    lane = iota((8, 128), 1)
    last_lane = lax.rem(lane, 32) == 31
    low_half = iota((8, 128), 0) < 4
    rest_real = lax.rem(lane, 32) < 16

    def products(j, block):
        w_re, w_im = role[j, 0:ROWS, 0:128], role[j, 0:ROWS, 128:256]
        v_re, v_im = block[0:ROWS, 0:128], block[0:ROWS, 128:256]
        w_rest, v_rest = role[j, ROWS : ROWS + 8, :], block[ROWS : ROWS + 8]
        count = role[j, ROWS + 8 : BLK, :] * block[ROWS + 8 : BLK]
        rest_re = w_rest * v_rest
        rest_im = turned[j] * v_rest
        return [
            jnp.sum((w_re * v_re + w_im * v_im).reshape(-1, 8, 128), axis=0),
            jnp.sum((w_im * v_re - w_re * v_im).reshape(-1, 8, 128), axis=0),
            rest_re[:, 0:128] + rest_re[:, 128:],
            rest_im[:, 0:128] + rest_im[:, 128:],
            count[:, 0:128] + count[:, 128:],
        ]

    def finish(sums, sign=1.0):
        re, im, rest_re, rest_im, count = sums
        count = lane_fold(count, (64, 32))
        count = jnp.where(last_lane, pltpu.roll(count, 1, 1), count)
        inverse = 1.0 / jnp.maximum(count, 1.0)
        rest_re = lane_fold(rest_re, (64, 32, 16))
        rest_im = lane_fold(rest_im, (64, 32, 16)) * sign
        return re * inverse, im * (inverse * sign), jnp.where(rest_real, rest_re, rest_im) * inverse

    def recv_wait(buffer, sems, g):
        pltpu.make_async_copy(buffer.at[g], buffer.at[g], sems.at[g]).wait()

    def columns(g, block, kind):
        block = block.astype(F32)
        rows = pl.ds(pl.multiple_of(g * 8, 8), 8)
        for s in range(SG):
            for i, part in enumerate(products(s, block)):
                raw[s, kind, i, rows, :] = part

    def merge(first, second):
        return [
            jnp.where(low_half, a, b) + pltpu.roll(jnp.where(low_half, b, a), 4, 0)
            for a, b in zip(first, second)
        ]

    def settle(kind):
        for s in range(SG):
            for pair in range(NGRP // 2):
                parts = merge(
                    [raw[s, kind, i, 16 * pair : 16 * pair + 8, :] for i in range(5)],
                    [raw[s, kind, i, 16 * pair + 8 : 16 * pair + 16, :] for i in range(5)],
                )
                start = kind * 32 + 8 * pair
                for i, part in enumerate(finish(parts)):
                    f_ref[s, start : start + 8, 128 * i : 128 * i + 128] = part

    @pl.when(takes_results)
    def _():
        edge_copy().wait_recv()
        set_role(SG, nbin[...])

    def results(g):
        block = gath[g].astype(F32)
        packed = jnp.zeros((8, 128), F32)
        for pair in range(2):
            re, im, rest = finish(
                merge(products(SG + 2 * pair, block), products(SG + 2 * pair + 1, block)), -1.0
            )
            out2[g, 8 * pair : 8 * pair + 8, :] = jnp.concatenate([re, im], axis=1).astype(BF)
            packed = jnp.where(lane // 32 == pair, rest, packed)
        out2[g, 16:24, :] = jnp.concatenate([packed, packed], axis=1).astype(BF)

    def own_columns(step, carry):
        g = member(step)

        @pl.when(g != me)
        def _():
            recv_wait(gath, recv_g, g)
            side_copy(g, gath.at[g]).start()

            @pl.when(gives_blocks)
            def _():
                far_copy(g, gath.at[g]).start()

        @pl.when(takes_results)
        def _():
            results(g)

            @pl.when(g != me)
            def _():
                result_copy(g).start()

        columns(g, gath[g], 0)
        return carry

    lax.fori_loop(0, NGRP, own_columns, 0)
    settle(0)

    def side_columns(step, carry):
        g = member(step)
        recv_wait(side, recv_s, g)
        columns(g, side[g], 1)
        return carry

    lax.fori_loop(0, NGRP, side_columns, 0)
    settle(1)

    def unpack(g, block):
        rows = block.astype(F32)
        start = pl.multiple_of(g * 16, 8)
        for i in range(2):
            far_f[i, pl.ds(start, 16), :] = rows[0:16, 128 * i : 128 * i + 128]
        rest = rows[16:24, 0:128]
        far_f[2, pl.ds(start, 8), :] = rest
        far_f[2, pl.ds(pl.multiple_of(start + 8, 8), 8), :] = pltpu.roll(rest, 96, 1)

    def codes(buffer, g, direction):
        rows = buffer[g, ROWS + 8 : BLK, 0:128].astype(F32)
        picked = jnp.where(lane == 31 + 32 * direction, rows, 0.0)
        return jnp.broadcast_to(jnp.sum(picked, axis=1, keepdims=True), (8, 128))

    @pl.when(takes_results)
    def _():
        unpack(me, out2[me])

        def collect(step, carry):
            g = member(step)

            @pl.when(g != me)
            def _():
                recv_wait(in2, recv_p, g)
                unpack(g, in2[g])

            return carry

        lax.fori_loop(0, NGRP, collect, 0)
        for s in range(SG):
            for i in range(3):
                outer = far_f[i, pl.ds(s, 32, stride=4), :]
                f_ref[s, 64:96, 128 * i : 128 * i + 128] = outer

    @pl.when(takes_blocks)
    def _():
        def far_columns(step, carry):
            g = member(step)
            recv_wait(far, recv_x, g)
            columns(g, far[g], 2)
            return carry

        lax.fori_loop(0, NGRP, far_columns, 0)
        settle(2)

    @pl.when(jnp.logical_not(has_far))
    def _():
        f_ref[:, 64:96, :] = jnp.zeros((SG, 32, 384), F32)

    for g in range(NGRP):
        side_code = codes(side, g, 1 - core) + (32.0 + 4 * g)
        far_code = jnp.where(takes_blocks, codes(far, g, core), iota((8, 128), 0).astype(F32))
        far_code = far_code + (64.0 + 4 * g)
        code_v[g * 12 : g * 12 + 4, :] = iota((4, 128), 0).astype(F32) + 4.0 * g
        code_v[g * 12 + 4 : g * 12 + 8, :] = jnp.where(even, far_code, side_code)[0:4]
        code_v[g * 12 + 8 : g * 12 + 12, :] = jnp.where(even, side_code, far_code)[0:4]
    chosen = jnp.where(line.astype(F32) == code_v[:, 0:96], 1.0, 0.0)
    for s in range(SG):
        pick = (chosen * keep_v[s][:, 0:96]).astype(BF)
        rows = f_ref[s].astype(BF)
        left_ref[s * 96 : (s + 1) * 96, :] = dot(pick, rows).astype(BF)

    side_copy(me, blk).wait_send()

    @pl.when(gives_edge)
    def _():
        edge_copy().wait_send()

    @pl.when(gives_blocks)
    def _():
        far_copy(me, blk).wait_send()

    for j in range(NGRP - 1):
        g = peer(j)
        gather_copy(j).wait_send()
        side_copy(g, gath.at[g]).wait_send()

        @pl.when(gives_blocks)
        def _():
            far_copy(g, gath.at[g]).wait_send()

        @pl.when(takes_results)
        def _():
            result_copy(g).wait_send()

    loads[5].wait()


def lag_kernel(left_ref, basis_ref, out_hbm, out_v, sems):
    copies = []
    for i, start in enumerate(range(0, LAGS, CHUNK)):
        series = dot(left_ref[:, 0 : 2 * NBIN], basis_ref[:, start : start + CHUNK])
        stop = min(start + CHUNK, LAGS)
        series = series[:, : stop - start].reshape(SG, 96, stop - start)
        out_v[:, :, start:stop] = series.astype(BF)
        copies.append(
            pltpu.make_async_copy(
                out_v.at[:, :, start:stop], out_hbm.at[:, :, start:stop], sems.at[i]
            )
        )
        copies[-1].start()
    for copy in copies:
        copy.wait()


def on_device(n_tile, traces, validity, boundary_rows, boundary_count, pair_mask):
    dft = jnp.asarray(dft_table())
    anywhere = pl.BlockSpec(memory_space=pltpu.MemorySpace.HBM)
    dma = pltpu.SemaphoreType.DMA
    vmem = pl.BlockSpec(memory_space=pltpu.VMEM)
    basis = jnp.asarray(lag_table())
    left, basis = pl.pallas_call(
        functools.partial(cross_kernel, n_tile),
        out_shape=(
            jax.ShapeDtypeStruct((SG * 96, 384), BF),
            jax.ShapeDtypeStruct(basis.shape, BF),
        ),
        in_specs=[anywhere] * 7,
        out_specs=(vmem, vmem),
        scratch_shapes=[
            pltpu.VMEM((SG, SEG, SAMP), F32),
            pltpu.VMEM((SG, SEG), jnp.int32),
            pltpu.SMEM((1, 2, SG), jnp.int32),
            pltpu.SMEM((1, 2), jnp.int32),
            pltpu.VMEM((SG, 96), jnp.int32),
            pltpu.VMEM(dft.shape, BF),
            pltpu.VMEM((BLK, 256), BF),
            pltpu.VMEM((BLK, 256), BF),
            pltpu.VMEM((NGRP, BLK, 256), BF),
            pltpu.VMEM((NGRP, BLK, 256), BF),
            pltpu.VMEM((NGRP, BLK, 256), BF),
            pltpu.VMEM((BLK, 256), BF),
            pltpu.VMEM((2 * SG, BLK, 256), F32),
            pltpu.VMEM((2 * SG, 8, 256), F32),
            pltpu.VMEM((SG, 96, 128), F32),
            pltpu.VMEM((96, 128), F32),
            pltpu.VMEM((SG, 3, 5, 64, 128), F32),
            pltpu.VMEM((SG, 96, 384), F32),
            pltpu.VMEM((3, 128, 128), F32),
            pltpu.VMEM((NGRP, 24, 256), BF),
            pltpu.VMEM((NGRP, 24, 256), BF),
            dma((6,)), dma((len(DFT_PARTS),)),
            dma((7,)), dma((8,)), dma((8,)), dma(()), dma((8,)),
            dma((8,)), dma((8,)), dma((8,)), dma(()), dma((8,)),
        ],
        compiler_params=pltpu.CompilerParams(
            collective_id=0, has_side_effects=True, vmem_limit_bytes=24 << 20
        ),
        name="cross",
    )(*[
        pltpu.with_memory_space_constraint(array, pltpu.MemorySpace.HBM)
        for array in (
            traces, validity, boundary_rows, boundary_count, pair_mask, dft, basis
        )
    ])
    return pl.pallas_call(
        lag_kernel,
        out_shape=jax.ShapeDtypeStruct((SG, 96, LAGS), BF),
        in_specs=[vmem, vmem],
        out_specs=pl.BlockSpec(memory_space=pl.ANY),
        scratch_shapes=[
            pltpu.VMEM((SG, 96, LAGS), BF),
            pltpu.SemaphoreType.DMA((pl.cdiv(LAGS, CHUNK),)),
        ],
        compiler_params=pltpu.CompilerParams(vmem_limit_bytes=24 << 20),
        name="lags",
    )(left, basis)


def solution(mesh):
    three = P(("tile", "grp"), None, None)
    two = P(("tile", "grp"), None)
    return jax.shard_map(
        functools.partial(on_device, mesh.shape["tile"]),
        mesh=mesh,
        in_specs=(three, two, three, two, two),
        out_specs=three,
        check_vma=False,
    )
```

```python
import functools
import math

import jax
import jax.numpy as jnp
import ml_dtypes
import numpy as np
from jax import lax
from jax.experimental import pallas as pl
from jax.experimental.pallas import tpu as pltpu
from jax.sharding import PartitionSpec as P

SG = 4
SEG = 16
SAMP = 1500
NBIN = 144
MAXLAG = 1000
LAGS = 2001
NGRP = 8
MAIN = 128
ROWS = SG * SEG
BLK = ROWS + 16
CHUNK = 512
X_RUN = 8
DFT_PARTS = tuple((a, min(a + 768, SAMP)) for a in range(0, SAMP, 768))
DEAD = 128.0
BF = jnp.bfloat16
F32 = jnp.float32
MESH = pl.DeviceIdType.MESH


def split_halves(table):
    high = table.astype(ml_dtypes.bfloat16)
    low = (table - high.astype(np.float64)).astype(ml_dtypes.bfloat16)
    return high, low


def dft_table():
    n = np.arange(SAMP, dtype=np.int64)[:, None]
    k = np.arange(1, NBIN + 1, dtype=np.int64)[None, :]
    angle = ((n * k) % (2 * SAMP)).astype(np.float64) * (2.0 * np.pi / (2 * SAMP))
    taper = 0.5 - 0.5 * np.cos(2.0 * np.pi * n / SAMP)
    cos, sin = taper * np.cos(angle), -taper * np.sin(angle)
    main = np.concatenate([cos[:, :MAIN], sin[:, :MAIN]], axis=1)
    rest = np.concatenate([cos[:, MAIN:], sin[:, MAIN:]], axis=1)
    main_high, main_low = split_halves(main)
    rest_high, rest_low = split_halves(rest)
    unused = np.zeros((SAMP, 64), ml_dtypes.bfloat16)
    return np.concatenate([main_high, main_low, rest_high, rest_low, unused], axis=1)


def lag_table():
    k = np.arange(1, NBIN + 1, dtype=np.int64)[:, None]
    lag = np.arange(LAGS, dtype=np.int64)[None, :] - MAXLAG
    angle = ((k * lag) % (2 * SAMP)).astype(np.float64) * (2.0 * np.pi / (2 * SAMP))
    cos = np.cos(angle) / math.sqrt(NBIN)
    sin = -np.sin(angle) / math.sqrt(NBIN)
    table = np.concatenate([cos[:MAIN], sin[:MAIN], cos[MAIN:], sin[MAIN:]], axis=0)
    table = np.pad(table, ((0, 0), (0, -LAGS % CHUNK)))
    return table.astype(ml_dtypes.bfloat16)


def iota(shape, axis):
    return lax.broadcasted_iota(jnp.int32, shape, axis)


def dot(a, b):
    return jnp.dot(a, b, preferred_element_type=F32)


def lane_fold(a, shifts):
    for shift in shifts:
        a = a + pltpu.roll(a, shift, 1)
    return a


def bin_of(lane):
    return jnp.where(lane < MAIN, lane, MAIN + (lane & 15))


def power_weights():
    shape = (256, 256)
    source, target = iota(shape, 0), iota(shape, 1)
    near = jnp.abs(bin_of(source) - bin_of(target)) <= 4
    return jnp.where(source < MAIN + 32, jnp.where(near, 17.0, 1.0), 0.0).astype(BF)


def cross_kernel(
    n_tile, x_hbm, val_hbm, rows_hbm, cnt_hbm, mask_hbm, dft_hbm, basis_hbm,
    left_ref, basis_ref,
    x_v, val_v, rows_s, cnt_s, mask_v, dft_v, blk, edge, gath, side, far, nbin, role, turned,
    keep_v, code_v, raw, f_ref, far_f, out2, in2, load_sem, dft_sem,
    send_g, send_s, send_x, send_n, send_p, recv_g, recv_s, recv_x, recv_n, recv_p,
):
    tile, me = lax.axis_index("tile"), lax.axis_index("grp")
    my_step = lax.rem(me, 4) * 2 + me // 4
    neighbour = (tile + 1, tile - 1)
    exists = (tile < n_tile - 1, tile > 0)
    core = lax.rem(tile, 2)
    side_tile = tile + 1 - 2 * core
    far_tile = tile - 1 + 2 * core
    has_far = jnp.logical_and(far_tile >= 0, far_tile < n_tile)
    even = core == 0
    odd = core == 1
    turn = (far_tile + X_RUN) // X_RUN != (tile + X_RUN) // X_RUN
    takes_blocks = jnp.logical_and(even, jnp.logical_and(has_far, jnp.logical_not(turn)))
    gives_blocks = jnp.logical_and(odd, jnp.logical_and(has_far, jnp.logical_not(turn)))
    takes_results = jnp.logical_and(has_far, jnp.logical_or(odd, turn))
    gives_edge = jnp.logical_and(has_far, jnp.logical_or(even, turn))

    def member(step):
        return lax.rem(step, 2) * 4 + step // 2

    def near(step):
        d = jnp.where(step < 2, 4 * step, jnp.where(step < 6, 2 * step - 3, 4 * step - 22))
        return lax.rem(me // 4 + d // 4, 2) * 4 + lax.rem(lax.rem(me, 4) + lax.rem(d, 4), 4)

    def peer(j):
        return member(j + jnp.where(my_step <= j, 1, 0))

    loads = [
        pltpu.make_async_copy(src, dst, load_sem.at[i])
        for i, (src, dst) in enumerate(
            [(x_hbm, x_v), (val_hbm, val_v), (rows_hbm, rows_s), (cnt_hbm, cnt_s),
             (mask_hbm, mask_v), (basis_hbm, basis_ref)]
        )
    ]
    dft_loads = [
        pltpu.make_async_copy(dft_hbm.at[a:b], dft_v.at[a:b], dft_sem.at[i])
        for i, (a, b) in enumerate(DFT_PARTS)
    ]
    for load in loads[1:5]:
        load.start()
    loads[0].start()
    for load in dft_loads:
        load.start()

    barrier = pltpu.get_barrier_semaphore()
    for j in range(NGRP - 1):
        pl.semaphore_signal(barrier, inc=1, device_id=(tile, peer(j)), device_id_type=MESH)
    for direction in range(2):

        @pl.when(exists[direction])
        def _():
            pl.semaphore_signal(
                barrier, inc=1, device_id=(neighbour[direction], me), device_id_type=MESH
            )

    row80, col64 = iota((BLK, ROWS), 0), iota((BLK, ROWS), 1)
    head = row80 < ROWS
    same_station = (row80 & 3) == (col64 >> 4)
    segment = col64 & 15
    source = jnp.where(head, row80 >> 2, (row80 - ROWS) >> 2)
    order = same_station & (jnp.where(head, segment, segment & 3) == source)
    order = order.astype(F32).astype(BF)
    weights = power_weights()
    loads[1].wait()
    same_group = (iota((ROWS, 128), 1) >> 5) == ((iota((ROWS, 128), 0) & 15) >> 2)
    lane128 = iota((ROWS, 128), 1)
    valid_parts = []
    for s in range(SG):
        row = jnp.broadcast_to(val_v[s : s + 1, :].astype(F32), (SEG, SEG))
        diag = jnp.where(iota((SEG, SEG), 0) == iota((SEG, SEG), 1), row, 0.0)
        valid_parts.append(jnp.sum(diag, axis=1, keepdims=True))
    valid = jnp.broadcast_to(jnp.concatenate(valid_parts, axis=0), (ROWS, 128))
    valid_group = jnp.where(same_group, valid, 0.0)
    loads[2].wait()
    loads[3].wait()

    def fold_rows(a):
        return jnp.concatenate([a[0:8], a[8:16]], axis=1)

    tail = fold_rows(dot(order[ROWS:], valid_group.astype(BF)))
    tail_row, tail_lane = iota((8, 256), 0), iota((8, 256), 1)
    tail = jnp.where((tail_lane & 31) == 31, 0.0, tail)
    for direction in range(2):
        for h in range(SG):
            code = jnp.where(
                h < cnt_s[0, direction], rows_s[0, direction, h].astype(F32), DEAD
            )
            here = (tail_row == h) & (tail_lane == 31 + 32 * direction)
            tail = jnp.where(here, code, tail)

    r80, c80 = iota((BLK, BLK), 0), iota((BLK, BLK), 1)
    within = r80 & 3
    wanted = jnp.zeros((BLK, BLK), jnp.int32)
    for h in range(SG):
        chosen = jnp.where(even, rows_s[0, 1, h], rows_s[0, 0, h])
        live = h < jnp.where(even, cnt_s[0, 1], cnt_s[0, 0])
        wanted = jnp.where(within == h, jnp.where(live, chosen, SG), wanted)
    pick_far = ((r80 >> 2) == (c80 >> 2)) & ((c80 & 3) == wanted)
    pick_far = jnp.where(pick_far, 1.0, 0.0).astype(BF)

    loads[0].wait()
    x = x_v[...].reshape(ROWS, SAMP)
    x_high = x.astype(BF)
    x_low = (x - x_high.astype(F32)).astype(BF)
    x_both = jnp.concatenate([x_high, x_low], axis=0)
    for load in dft_loads:
        load.wait()
    both = dot(x_both, dft_v[...])
    loads[5].start()
    main = both[:ROWS, :256] + (both[ROWS:, :256] + both[:ROWS, 256:512])
    rest = both[:ROWS, 512:640] + jnp.where(lane128 < 32, both[ROWS:, 512:640], 0.0)
    rest = jnp.where(lane128 < 32, rest + pltpu.roll(rest, 96, 1), 0.0)
    rest = rest + pltpu.roll(rest, 32, 1)
    rest = rest + pltpu.roll(rest, 64, 1)
    real, imag = main[:, :MAIN], main[:, MAIN:]
    power = jnp.concatenate([real * real + imag * imag, rest * rest], axis=1)
    power_high = power.astype(BF)
    power_low = (power - power_high.astype(F32)).astype(BF)
    level = dot(jnp.concatenate([power_high, power_low], axis=0), weights)
    level = (level[:ROWS] + level[ROWS:]) * (1.0 / 288.0) + 1e-06
    factor = lax.rsqrt(level)
    factor_main = factor[:, :MAIN] * valid
    factor_rest = factor[:, MAIN:] * valid_group
    white = jnp.concatenate([real * factor_main, imag * factor_main], axis=1)
    white = dot(order[:ROWS], white.astype(BF))
    white_rest = fold_rows(dot(order[ROWS:], (rest * factor_rest).astype(BF)))
    own = jnp.concatenate([white, white_rest, tail], axis=0).astype(BF)
    blk[...] = own
    gath[me] = own

    edges = jnp.where(exists[0], 1, 0) + jnp.where(exists[1], 1, 0)
    pl.semaphore_wait(barrier, NGRP - 1 + edges)

    def send(src, dst, send_sem, recv_sem, to_tile, to_member):
        return pltpu.make_async_remote_copy(
            src_ref=src, dst_ref=dst, send_sem=send_sem, recv_sem=recv_sem,
            device_id=(to_tile, to_member), device_id_type=MESH,
        )

    def gather_copy(j):
        return send(blk, gath.at[me], send_g.at[j], recv_g.at[me], tile, peer(j))

    def side_copy(g, src):
        return send(src, side.at[g], send_s.at[g], recv_s.at[g], side_tile, me)

    def far_copy(g, src):
        return send(src, far.at[g], send_x.at[g], recv_x.at[g], far_tile, me)

    def edge_copy():
        return send(edge, nbin, send_n, recv_n, far_tile, me)

    def result_copy(g):
        return send(out2.at[g], in2.at[me], send_p.at[g], recv_p.at[me], tile, g)

    on_turn = jnp.logical_and(has_far, turn)

    @pl.when(on_turn)
    def _():
        edge[...] = dot(pick_far, own).astype(BF)
        edge_copy().start()

    @pl.when(gives_blocks)
    def _():
        far_copy(me, blk).start()

    for j in range(NGRP - 1):
        gather_copy(j).start()

    @pl.when(jnp.logical_and(gives_edge, jnp.logical_not(turn)))
    def _():
        edge[...] = dot(pick_far, own).astype(BF)
        edge_copy().start()

    side_copy(me, blk).start()
    row, col = iota((BLK, BLK), 0), iota((BLK, BLK), 1)
    first_half = (iota((8, 256), 1) & 31) < 16

    def set_role(first, block):
        for s in range(SG):
            spread = (col == (row >> 2) * SG + s).astype(F32).astype(BF)
            wide = dot(spread, block)
            role[first + s] = wide
            tail = wide[ROWS : ROWS + 8]
            ahead = jnp.concatenate(
                [pltpu.roll(tail[:, 0:128], 112, 1), pltpu.roll(tail[:, 128:], 112, 1)], axis=1
            )
            behind = jnp.concatenate(
                [pltpu.roll(tail[:, 0:128], 16, 1), pltpu.roll(tail[:, 128:], 16, 1)], axis=1
            )
            turned[first + s] = jnp.where(first_half, ahead, -behind)

    set_role(0, own)
    loads[4].wait()
    column, line = iota((96, 96), 0), iota((96, 96), 1)
    on_diagonal = column == line
    for s in range(SG):
        wanted = jnp.broadcast_to(mask_v[s : s + 1, :].astype(F32), (96, 96))
        kept = jnp.sum(jnp.where(on_diagonal, wanted, 0.0), axis=1, keepdims=True)
        keep_v[s] = jnp.broadcast_to(kept, (96, 128))

    lane = iota((8, 128), 1)
    last_lane = (lane & 31) == 31
    low_half = iota((8, 128), 0) < 4
    rest_real = (lane & 31) < 16

    def products(j, block):
        w_re, w_im = role[j, 0:ROWS, 0:128], role[j, 0:ROWS, 128:256]
        v_re, v_im = block[0:ROWS, 0:128], block[0:ROWS, 128:256]
        w_rest, v_rest = role[j, ROWS : ROWS + 8, :], block[ROWS : ROWS + 8]
        count = role[j, ROWS + 8 : BLK, :] * block[ROWS + 8 : BLK]
        rest_re = w_rest * v_rest
        rest_im = turned[j] * v_rest
        return [
            jnp.sum((w_re * v_re + w_im * v_im).reshape(-1, 8, 128), axis=0),
            jnp.sum((w_im * v_re - w_re * v_im).reshape(-1, 8, 128), axis=0),
            rest_re[:, 0:128] + rest_re[:, 128:],
            rest_im[:, 0:128] + rest_im[:, 128:],
            count[:, 0:128] + count[:, 128:],
        ]

    def finish(sums, sign=1.0):
        re, im, rest_re, rest_im, count = sums
        count = lane_fold(count, (64, 32))
        count = jnp.where(last_lane, pltpu.roll(count, 1, 1), count)
        inverse = 1.0 / jnp.maximum(count, 1.0)
        rest_re = lane_fold(rest_re, (64, 32, 16))
        rest_im = lane_fold(rest_im, (64, 32, 16)) * sign
        return re * inverse, im * (inverse * sign), jnp.where(rest_real, rest_re, rest_im) * inverse

    def recv_wait(buffer, sems, g):
        pltpu.make_async_copy(buffer.at[g], buffer.at[g], sems.at[g]).wait()

    def columns(g, block, kind):
        block = block.astype(F32)
        rows = pl.ds(pl.multiple_of(g * 8, 8), 8)
        for s in range(SG):
            for i, part in enumerate(products(s, block)):
                raw[s, kind, i, rows, :] = part

    def merge(first, second):
        return [
            jnp.where(low_half, a, b) + pltpu.roll(jnp.where(low_half, b, a), 4, 0)
            for a, b in zip(first, second)
        ]

    def settle(kind):
        for s in range(SG):
            for pair in range(NGRP // 2):
                parts = merge(
                    [raw[s, kind, i, 16 * pair : 16 * pair + 8, :] for i in range(5)],
                    [raw[s, kind, i, 16 * pair + 8 : 16 * pair + 16, :] for i in range(5)],
                )
                start = kind * 32 + 8 * pair
                for i, part in enumerate(finish(parts)):
                    f_ref[s, start : start + 8, 128 * i : 128 * i + 128] = part

    @pl.when(takes_results)
    def _():
        edge_copy().wait_recv()
        set_role(SG, nbin[...])

    def results(g):
        block = gath[g].astype(F32)
        packed = jnp.zeros((8, 128), F32)
        for pair in range(2):
            re, im, rest = finish(
                merge(products(SG + 2 * pair, block), products(SG + 2 * pair + 1, block)), -1.0
            )
            out2[g, 8 * pair : 8 * pair + 8, :] = jnp.concatenate([re, im], axis=1).astype(BF)
            packed = jnp.where((lane >> 5) == pair, rest, packed)
        out2[g, 16:24, :] = jnp.concatenate([packed, packed], axis=1).astype(BF)

    def own_columns(step, carry):
        g = member(step)

        @pl.when(g != me)
        def _():
            recv_wait(gath, recv_g, g)
            side_copy(g, gath.at[g]).start()

            @pl.when(gives_blocks)
            def _():
                far_copy(g, gath.at[g]).start()

        @pl.when(takes_results)
        def _():
            results(g)

            @pl.when(g != me)
            def _():
                result_copy(g).start()

        columns(g, gath[g], 0)
        return carry

    lax.fori_loop(0, NGRP, own_columns, 0)
    settle(0)

    def side_columns(step, carry):
        g = member(step)
        recv_wait(side, recv_s, g)
        columns(g, side[g], 1)
        return carry

    lax.fori_loop(0, NGRP, side_columns, 0)
    settle(1)

    def unpack(g, block):
        rows = block.astype(F32)
        start = g * 16
        for i in range(2):
            far_f[i, pl.ds(start, 16), :] = rows[0:16, 128 * i : 128 * i + 128]
        rest = rows[16:24, 0:128]
        far_f[2, pl.ds(start, 8), :] = rest
        far_f[2, pl.ds(start + 8, 8), :] = pltpu.roll(rest, 96, 1)

    def codes(buffer, g, direction):
        rows = buffer[g, ROWS + 8 : BLK, 0:128].astype(F32)
        picked = jnp.where(lane == 31 + 32 * direction, rows, 0.0)
        return jnp.broadcast_to(jnp.sum(picked, axis=1, keepdims=True), (8, 128))

    station = iota((8, 128), 0).astype(F32)

    def place(g, first, second):
        code_v[g * 12 + 4 : g * 12 + 8, :] = jnp.where(even, first, second)[0:4]
        code_v[g * 12 + 8 : g * 12 + 12, :] = jnp.where(even, second, first)[0:4]

    for g in range(NGRP):
        code_v[g * 12 : g * 12 + 4, :] = station[0:4] + 4.0 * g
        place(g, station + (64.0 + 4 * g), codes(side, g, 1 - core) + (32.0 + 4 * g))

    @pl.when(takes_results)
    def _():
        in2[me] = out2[me]

        def collect(step, carry):
            g = member(step)

            @pl.when(g != me)
            def _():
                recv_wait(in2, recv_p, g)

            return carry

        lax.fori_loop(0, NGRP, collect, 0)
        for g in range(NGRP):
            unpack(g, in2[g])
        for s in range(SG):
            for i in range(3):
                outer = far_f[i, pl.ds(s, 32, stride=4), :]
                f_ref[s, 64:96, 128 * i : 128 * i + 128] = outer

    @pl.when(takes_blocks)
    def _():
        def far_columns(step, carry):
            g = member(step)
            recv_wait(far, recv_x, g)
            columns(g, far[g], 2)
            return carry

        lax.fori_loop(0, NGRP, far_columns, 0)
        for g in range(NGRP):
            far_code = codes(far, g, 0) + (64.0 + 4 * g)
            code_v[g * 12 + 4 : g * 12 + 8, :] = far_code[0:4]
        settle(2)

    @pl.when(jnp.logical_not(has_far))
    def _():
        f_ref[:, 64:96, :] = jnp.zeros((SG, 32, 384), F32)

    chosen = jnp.where(line.astype(F32) == code_v[:, 0:96], 1.0, 0.0)
    for s in range(SG):
        pick = (chosen * keep_v[s][:, 0:96]).astype(BF)
        rows = f_ref[s].astype(BF)
        left_ref[s * 96 : (s + 1) * 96, :] = dot(pick, rows).astype(BF)

    side_copy(me, blk).wait_send()

    @pl.when(gives_edge)
    def _():
        edge_copy().wait_send()

    @pl.when(gives_blocks)
    def _():
        far_copy(me, blk).wait_send()

    for j in range(NGRP - 1):
        g = peer(j)
        gather_copy(j).wait_send()
        side_copy(g, gath.at[g]).wait_send()

        @pl.when(gives_blocks)
        def _():
            far_copy(g, gath.at[g]).wait_send()

        @pl.when(takes_results)
        def _():
            result_copy(g).wait_send()

    loads[5].wait()


def lag_kernel(left_ref, basis_ref, out_hbm, out_v, sems):
    copies = []
    for i, start in enumerate(range(0, LAGS, CHUNK)):
        series = dot(left_ref[:, 0 : 2 * NBIN], basis_ref[:, start : start + CHUNK])
        stop = min(start + CHUNK, LAGS)
        series = series[:, : stop - start].reshape(SG, 96, stop - start)
        out_v[:, :, start:stop] = series.astype(BF)
        copies.append(
            pltpu.make_async_copy(
                out_v.at[:, :, start:stop], out_hbm.at[:, :, start:stop], sems.at[i]
            )
        )
        copies[-1].start()
    for copy in copies:
        copy.wait()


def on_device(n_tile, traces, validity, boundary_rows, boundary_count, pair_mask):
    dft = jnp.asarray(dft_table())
    anywhere = pl.BlockSpec(memory_space=pltpu.MemorySpace.HBM)
    dma = pltpu.SemaphoreType.DMA
    vmem = pl.BlockSpec(memory_space=pltpu.VMEM)
    basis = jnp.asarray(lag_table())
    left, basis = pl.pallas_call(
        functools.partial(cross_kernel, n_tile),
        out_shape=(
            jax.ShapeDtypeStruct((SG * 96, 384), BF),
            jax.ShapeDtypeStruct(basis.shape, BF),
        ),
        in_specs=[anywhere] * 7,
        out_specs=(vmem, vmem),
        scratch_shapes=[
            pltpu.VMEM((SG, SEG, SAMP), F32),
            pltpu.VMEM((SG, SEG), jnp.int32),
            pltpu.SMEM((1, 2, SG), jnp.int32),
            pltpu.SMEM((1, 2), jnp.int32),
            pltpu.VMEM((SG, 96), jnp.int32),
            pltpu.VMEM(dft.shape, BF),
            pltpu.VMEM((BLK, 256), BF),
            pltpu.VMEM((BLK, 256), BF),
            pltpu.VMEM((NGRP, BLK, 256), BF),
            pltpu.VMEM((NGRP, BLK, 256), BF),
            pltpu.VMEM((NGRP, BLK, 256), BF),
            pltpu.VMEM((BLK, 256), BF),
            pltpu.VMEM((2 * SG, BLK, 256), F32),
            pltpu.VMEM((2 * SG, 8, 256), F32),
            pltpu.VMEM((SG, 96, 128), F32),
            pltpu.VMEM((96, 128), F32),
            pltpu.VMEM((SG, 3, 5, 64, 128), F32),
            pltpu.VMEM((SG, 96, 384), F32),
            pltpu.VMEM((3, 128, 128), F32),
            pltpu.VMEM((NGRP, 24, 256), BF),
            pltpu.VMEM((NGRP, 24, 256), BF),
            dma((6,)), dma((len(DFT_PARTS),)),
            dma((7,)), dma((8,)), dma((8,)), dma(()), dma((8,)),
            dma((8,)), dma((8,)), dma((8,)), dma(()), dma((8,)),
        ],
        compiler_params=pltpu.CompilerParams(
            collective_id=0, has_side_effects=True, vmem_limit_bytes=24 << 20
        ),
        name="cross",
    )(*[
        pltpu.with_memory_space_constraint(array, pltpu.MemorySpace.HBM)
        for array in (
            traces, validity, boundary_rows, boundary_count, pair_mask, dft, basis
        )
    ])
    return pl.pallas_call(
        lag_kernel,
        out_shape=jax.ShapeDtypeStruct((SG, 96, LAGS), BF),
        in_specs=[vmem, vmem],
        out_specs=pl.BlockSpec(memory_space=pl.ANY),
        scratch_shapes=[
            pltpu.VMEM((SG, 96, LAGS), BF),
            pltpu.SemaphoreType.DMA((pl.cdiv(LAGS, CHUNK),)),
        ],
        compiler_params=pltpu.CompilerParams(vmem_limit_bytes=24 << 20),
        name="lags",
    )(left, basis)


def solution(mesh):
    three = P(("tile", "grp"), None, None)
    two = P(("tile", "grp"), None)
    return jax.shard_map(
        functools.partial(on_device, mesh.shape["tile"]),
        mesh=mesh,
        in_specs=(three, two, three, two, two),
        out_specs=three,
        check_vma=False,
    )
```

```python
import functools
import math

import jax
import jax.numpy as jnp
import ml_dtypes
import numpy as np
from jax import lax
from jax.experimental import pallas as pl
from jax.experimental.pallas import tpu as pltpu
from jax.sharding import PartitionSpec as P

SG = 4
SEG = 16
SAMP = 1500
NBIN = 144
MAXLAG = 1000
LAGS = 2001
NGRP = 8
MAIN = 128
ROWS = SG * SEG
BLK = ROWS + 16
CHUNK = 512
X_RUN = 8
DFT_PARTS = tuple((a, min(a + 768, SAMP)) for a in range(0, SAMP, 768))
DEAD = 128.0
BF = jnp.bfloat16
F32 = jnp.float32
MESH = pl.DeviceIdType.MESH


def split_halves(table):
    high = table.astype(ml_dtypes.bfloat16)
    low = (table - high.astype(np.float64)).astype(ml_dtypes.bfloat16)
    return high, low


def dft_table():
    n = np.arange(SAMP, dtype=np.int64)[:, None]
    k = np.arange(1, NBIN + 1, dtype=np.int64)[None, :]
    angle = ((n * k) % (2 * SAMP)).astype(np.float64) * (2.0 * np.pi / (2 * SAMP))
    taper = 0.5 - 0.5 * np.cos(2.0 * np.pi * n / SAMP)
    cos, sin = taper * np.cos(angle), -taper * np.sin(angle)
    main = np.concatenate([cos[:, :MAIN], sin[:, :MAIN]], axis=1)
    rest = np.concatenate([cos[:, MAIN:], sin[:, MAIN:]], axis=1)
    main_high, main_low = split_halves(main)
    rest_high, rest_low = split_halves(rest)
    unused = np.zeros((SAMP, 64), ml_dtypes.bfloat16)
    return np.concatenate([main_high, main_low, rest_high, rest_low, unused], axis=1)


def lag_table():
    k = np.arange(1, NBIN + 1, dtype=np.int64)[:, None]
    lag = np.arange(LAGS, dtype=np.int64)[None, :] - MAXLAG
    angle = ((k * lag) % (2 * SAMP)).astype(np.float64) * (2.0 * np.pi / (2 * SAMP))
    cos = np.cos(angle) / math.sqrt(NBIN)
    sin = -np.sin(angle) / math.sqrt(NBIN)
    table = np.concatenate([cos[:MAIN], sin[:MAIN], cos[MAIN:], sin[MAIN:]], axis=0)
    table = np.pad(table, ((0, 0), (0, -LAGS % CHUNK)))
    return table.astype(ml_dtypes.bfloat16)


def iota(shape, axis):
    return lax.broadcasted_iota(jnp.int32, shape, axis)


def dot(a, b):
    return jnp.dot(a, b, preferred_element_type=F32)


def lane_fold(a, shifts):
    for shift in shifts:
        a = a + pltpu.roll(a, shift, 1)
    return a


def bin_of(lane):
    return jnp.where(lane < MAIN, lane, MAIN + (lane & 15))


def power_weights():
    shape = (256, 256)
    source, target = iota(shape, 0), iota(shape, 1)
    near = jnp.abs(bin_of(source) - bin_of(target)) <= 4
    return jnp.where(source < MAIN + 32, jnp.where(near, 17.0, 1.0), 0.0).astype(BF)


def cross_kernel(
    n_tile, x_hbm, val_hbm, rows_hbm, cnt_hbm, mask_hbm, dft_hbm, basis_hbm,
    left_ref, basis_ref,
    x_v, val_v, rows_s, cnt_s, mask_v, dft_v, blk, edge, gath, side, far, nbin, role, turned,
    keep_v, code_v, raw, f_ref, far_f, out2, in2, load_sem, dft_sem,
    send_g, send_s, send_x, send_n, send_p, recv_g, recv_s, recv_x, recv_n, recv_p,
):
    tile, me = lax.axis_index("tile"), lax.axis_index("grp")
    my_step = lax.rem(me, 4) * 2 + me // 4
    neighbour = (tile + 1, tile - 1)
    exists = (tile < n_tile - 1, tile > 0)
    core = lax.rem(tile, 2)
    side_tile = tile + 1 - 2 * core
    far_tile = tile - 1 + 2 * core
    has_far = jnp.logical_and(far_tile >= 0, far_tile < n_tile)
    even = core == 0
    odd = core == 1
    turn = (far_tile + X_RUN) // X_RUN != (tile + X_RUN) // X_RUN
    takes_blocks = jnp.logical_and(even, jnp.logical_and(has_far, jnp.logical_not(turn)))
    gives_blocks = jnp.logical_and(odd, jnp.logical_and(has_far, jnp.logical_not(turn)))
    takes_results = jnp.logical_and(has_far, jnp.logical_or(odd, turn))
    gives_edge = jnp.logical_and(has_far, jnp.logical_or(even, turn))

    def member(step):
        return lax.rem(step, 2) * 4 + step // 2

    def near(step):
        d = jnp.where(step < 2, 4 * step, jnp.where(step < 6, 2 * step - 3, 4 * step - 22))
        return lax.rem(me // 4 + d // 4, 2) * 4 + lax.rem(lax.rem(me, 4) + lax.rem(d, 4), 4)

    def peer(j):
        return member(j + jnp.where(my_step <= j, 1, 0))

    loads = [
        pltpu.make_async_copy(src, dst, load_sem.at[i])
        for i, (src, dst) in enumerate(
            [(x_hbm, x_v), (val_hbm, val_v), (rows_hbm, rows_s), (cnt_hbm, cnt_s),
             (mask_hbm, mask_v), (basis_hbm, basis_ref)]
        )
    ]
    dft_loads = [
        pltpu.make_async_copy(dft_hbm.at[a:b], dft_v.at[a:b], dft_sem.at[i])
        for i, (a, b) in enumerate(DFT_PARTS)
    ]
    for load in loads[1:5]:
        load.start()
    loads[0].start()
    for load in dft_loads:
        load.start()

    barrier = pltpu.get_barrier_semaphore()
    for j in range(NGRP - 1):
        pl.semaphore_signal(barrier, inc=1, device_id=(tile, peer(j)), device_id_type=MESH)
    for direction in range(2):

        @pl.when(exists[direction])
        def _():
            pl.semaphore_signal(
                barrier, inc=1, device_id=(neighbour[direction], me), device_id_type=MESH
            )

    row80, col64 = iota((BLK, ROWS), 0), iota((BLK, ROWS), 1)
    head = row80 < ROWS
    same_station = (row80 & 3) == (col64 >> 4)
    segment = col64 & 15
    source = jnp.where(head, row80 >> 2, (row80 - ROWS) >> 2)
    order = same_station & (jnp.where(head, segment, segment & 3) == source)
    order = order.astype(F32).astype(BF)
    weights = power_weights()
    loads[1].wait()
    same_group = (iota((ROWS, 128), 1) >> 5) == ((iota((ROWS, 128), 0) & 15) >> 2)
    lane128 = iota((ROWS, 128), 1)
    valid_parts = []
    for s in range(SG):
        row = jnp.broadcast_to(val_v[s : s + 1, :].astype(F32), (SEG, SEG))
        diag = jnp.where(iota((SEG, SEG), 0) == iota((SEG, SEG), 1), row, 0.0)
        valid_parts.append(jnp.sum(diag, axis=1, keepdims=True))
    valid = jnp.broadcast_to(jnp.concatenate(valid_parts, axis=0), (ROWS, 128))
    valid_group = jnp.where(same_group, valid, 0.0)
    loads[2].wait()
    loads[3].wait()

    def fold_rows(a):
        return jnp.concatenate([a[0:8], a[8:16]], axis=1)

    tail = fold_rows(dot(order[ROWS:], valid_group.astype(BF)))
    tail_row, tail_lane = iota((8, 256), 0), iota((8, 256), 1)
    tail = jnp.where((tail_lane & 31) == 31, 0.0, tail)
    for direction in range(2):
        for h in range(SG):
            code = jnp.where(
                h < cnt_s[0, direction], rows_s[0, direction, h].astype(F32), DEAD
            )
            here = (tail_row == h) & (tail_lane == 31 + 32 * direction)
            tail = jnp.where(here, code, tail)

    r80, c80 = iota((BLK, BLK), 0), iota((BLK, BLK), 1)
    within = r80 & 3
    wanted = jnp.zeros((BLK, BLK), jnp.int32)
    for h in range(SG):
        chosen = jnp.where(even, rows_s[0, 1, h], rows_s[0, 0, h])
        live = h < jnp.where(even, cnt_s[0, 1], cnt_s[0, 0])
        wanted = jnp.where(within == h, jnp.where(live, chosen, SG), wanted)
    pick_far = ((r80 >> 2) == (c80 >> 2)) & ((c80 & 3) == wanted)
    pick_far = jnp.where(pick_far, 1.0, 0.0).astype(BF)

    loads[0].wait()
    x = x_v[...].reshape(ROWS, SAMP)
    x_high = x.astype(BF)
    x_low = (x - x_high.astype(F32)).astype(BF)
    x_both = jnp.concatenate([x_high, x_low], axis=0)
    for load in dft_loads:
        load.wait()
    both = dot(x_both, dft_v[...])
    loads[5].start()
    main = both[:ROWS, :256] + (both[ROWS:, :256] + both[:ROWS, 256:512])
    rest = both[:ROWS, 512:640] + jnp.where(lane128 < 32, both[ROWS:, 512:640], 0.0)
    rest = jnp.where(lane128 < 32, rest + pltpu.roll(rest, 96, 1), 0.0)
    rest = rest + pltpu.roll(rest, 32, 1)
    rest = rest + pltpu.roll(rest, 64, 1)
    real, imag = main[:, :MAIN], main[:, MAIN:]
    power = jnp.concatenate([real * real + imag * imag, rest * rest], axis=1)
    power_high = power.astype(BF)
    power_low = (power - power_high.astype(F32)).astype(BF)
    level = dot(jnp.concatenate([power_high, power_low], axis=0), weights)
    level = (level[:ROWS] + level[ROWS:]) * (1.0 / 288.0) + 1e-06
    factor = lax.rsqrt(level)
    factor_main = factor[:, :MAIN] * valid
    factor_rest = factor[:, MAIN:] * valid_group
    white = jnp.concatenate([real * factor_main, imag * factor_main], axis=1)
    white = dot(order[:ROWS], white.astype(BF))
    white_rest = fold_rows(dot(order[ROWS:], (rest * factor_rest).astype(BF)))
    own = jnp.concatenate([white, white_rest, tail], axis=0).astype(BF)
    blk[...] = own
    gath[me] = own

    edges = jnp.where(exists[0], 1, 0) + jnp.where(exists[1], 1, 0)
    pl.semaphore_wait(barrier, NGRP - 1 + edges)

    def send(src, dst, send_sem, recv_sem, to_tile, to_member):
        return pltpu.make_async_remote_copy(
            src_ref=src, dst_ref=dst, send_sem=send_sem, recv_sem=recv_sem,
            device_id=(to_tile, to_member), device_id_type=MESH,
        )

    def gather_copy(j):
        return send(blk, gath.at[me], send_g.at[j], recv_g.at[me], tile, peer(j))

    def side_copy(g, src):
        return send(src, side.at[g], send_s.at[g], recv_s.at[g], side_tile, me)

    def far_copy(g, src):
        return send(src, far.at[g], send_x.at[g], recv_x.at[g], far_tile, me)

    def edge_copy():
        return send(edge, nbin, send_n, recv_n, far_tile, me)

    def result_copy(g):
        return send(out2.at[g], in2.at[me], send_p.at[g], recv_p.at[me], tile, g)

    on_turn = jnp.logical_and(has_far, turn)

    @pl.when(on_turn)
    def _():
        edge[...] = dot(pick_far, own).astype(BF)
        edge_copy().start()

    @pl.when(gives_blocks)
    def _():
        far_copy(me, blk).start()

    for j in range(NGRP - 1):
        gather_copy(j).start()

    @pl.when(jnp.logical_and(gives_edge, jnp.logical_not(turn)))
    def _():
        edge[...] = dot(pick_far, own).astype(BF)
        edge_copy().start()

    side_copy(me, blk).start()
    row, col = iota((BLK, BLK), 0), iota((BLK, BLK), 1)
    first_half = (iota((8, 256), 1) & 31) < 16

    def set_role(first, block):
        for s in range(SG):
            spread = (col == (row >> 2) * SG + s).astype(F32).astype(BF)
            wide = dot(spread, block)
            role[first + s] = wide
            tail = wide[ROWS : ROWS + 8]
            ahead = jnp.concatenate(
                [pltpu.roll(tail[:, 0:128], 112, 1), pltpu.roll(tail[:, 128:], 112, 1)], axis=1
            )
            behind = jnp.concatenate(
                [pltpu.roll(tail[:, 0:128], 16, 1), pltpu.roll(tail[:, 128:], 16, 1)], axis=1
            )
            turned[first + s] = jnp.where(first_half, ahead, -behind)

    set_role(0, own)
    loads[4].wait()
    column, line = iota((96, 96), 0), iota((96, 96), 1)
    on_diagonal = column == line
    for s in range(SG):
        wanted = jnp.broadcast_to(mask_v[s : s + 1, :].astype(F32), (96, 96))
        kept = jnp.sum(jnp.where(on_diagonal, wanted, 0.0), axis=1, keepdims=True)
        keep_v[s] = jnp.broadcast_to(kept, (96, 128))

    lane = iota((8, 128), 1)
    last_lane = (lane & 31) == 31
    low_half = iota((8, 128), 0) < 4
    rest_real = (lane & 31) < 16

    def products(j, block):
        w_re, w_im = role[j, 0:ROWS, 0:128], role[j, 0:ROWS, 128:256]
        v_re, v_im = block[0:ROWS, 0:128], block[0:ROWS, 128:256]
        w_rest, v_rest = role[j, ROWS : ROWS + 8, :], block[ROWS : ROWS + 8]
        count = role[j, ROWS + 8 : BLK, :] * block[ROWS + 8 : BLK]
        rest_re = w_rest * v_rest
        rest_im = turned[j] * v_rest
        return [
            jnp.sum((w_re * v_re + w_im * v_im).reshape(-1, 8, 128), axis=0),
            jnp.sum((w_im * v_re - w_re * v_im).reshape(-1, 8, 128), axis=0),
            rest_re[:, 0:128] + rest_re[:, 128:],
            rest_im[:, 0:128] + rest_im[:, 128:],
            count[:, 0:128] + count[:, 128:],
        ]

    def finish(sums, sign=1.0):
        re, im, rest_re, rest_im, count = sums
        count = lane_fold(count, (64, 32))
        count = jnp.where(last_lane, pltpu.roll(count, 1, 1), count)
        inverse = 1.0 / jnp.maximum(count, 1.0)
        rest_re = lane_fold(rest_re, (64, 32, 16))
        rest_im = lane_fold(rest_im, (64, 32, 16)) * sign
        return re * inverse, im * (inverse * sign), jnp.where(rest_real, rest_re, rest_im) * inverse

    def recv_wait(buffer, sems, g):
        pltpu.make_async_copy(buffer.at[g], buffer.at[g], sems.at[g]).wait()

    def columns(g, block, kind):
        block = block.astype(F32)
        rows = pl.ds(pl.multiple_of(g * 8, 8), 8)
        for s in range(SG):
            for i, part in enumerate(products(s, block)):
                raw[s, kind, i, rows, :] = part

    def merge(first, second):
        return [
            jnp.where(low_half, a, b) + pltpu.roll(jnp.where(low_half, b, a), 4, 0)
            for a, b in zip(first, second)
        ]

    def settle(kind):
        for s in range(SG):
            for pair in range(NGRP // 2):
                parts = merge(
                    [raw[s, kind, i, 16 * pair : 16 * pair + 8, :] for i in range(5)],
                    [raw[s, kind, i, 16 * pair + 8 : 16 * pair + 16, :] for i in range(5)],
                )
                start = kind * 32 + 8 * pair
                for i, part in enumerate(finish(parts)):
                    f_ref[s, start : start + 8, 128 * i : 128 * i + 128] = part

    @pl.when(takes_results)
    def _():
        edge_copy().wait_recv()
        set_role(SG, nbin[...])

    def results(members):
        done = []
        for g in members:
            block = gath[g].astype(F32)
            done.append([
                finish(
                    merge(products(SG + 2 * pair, block), products(SG + 2 * pair + 1, block)),
                    -1.0,
                )
                for pair in range(2)
            ])
        for g, pairs in zip(members, done):
            for pair, (re, im, rest) in enumerate(pairs):
                out2[g, 8 * pair : 8 * pair + 8, :] = jnp.concatenate([re, im], axis=1).astype(BF)
            packed = jnp.where((lane >> 5) == 0, pairs[0][2], pairs[1][2])
            out2[g, 16:24, :] = jnp.concatenate([packed, packed], axis=1).astype(BF)

    def own_columns(step, carry):
        members = (step, step + 4)
        for g in members:

            @pl.when(g != me)
            def _():
                recv_wait(gath, recv_g, g)
                side_copy(g, gath.at[g]).start()

                @pl.when(gives_blocks)
                def _():
                    far_copy(g, gath.at[g]).start()

        @pl.when(takes_results)
        def _():
            results(members)
            for g in members:

                @pl.when(g != me)
                def _():
                    result_copy(g).start()

        for g in members:
            columns(g, gath[g], 0)
        return carry

    lax.fori_loop(0, NGRP // 2, own_columns, 0)
    settle(0)

    def side_columns(step, carry):
        g = member(step)
        recv_wait(side, recv_s, g)
        columns(g, side[g], 1)
        return carry

    lax.fori_loop(0, NGRP, side_columns, 0)
    settle(1)

    def unpack(g, block):
        rows = block.astype(F32)
        start = g * 16
        for i in range(2):
            far_f[i, pl.ds(start, 16), :] = rows[0:16, 128 * i : 128 * i + 128]
        rest = rows[16:24, 0:128]
        far_f[2, pl.ds(start, 8), :] = rest
        far_f[2, pl.ds(start + 8, 8), :] = pltpu.roll(rest, 96, 1)

    def codes(buffer, g, direction):
        rows = buffer[g, ROWS + 8 : BLK, 0:128].astype(F32)
        picked = jnp.where(lane == 31 + 32 * direction, rows, 0.0)
        return jnp.broadcast_to(jnp.sum(picked, axis=1, keepdims=True), (8, 128))

    station = iota((8, 128), 0).astype(F32)

    def place(g, first, second):
        code_v[g * 12 + 4 : g * 12 + 8, :] = jnp.where(even, first, second)[0:4]
        code_v[g * 12 + 8 : g * 12 + 12, :] = jnp.where(even, second, first)[0:4]

    for g in range(NGRP):
        code_v[g * 12 : g * 12 + 4, :] = station[0:4] + 4.0 * g
        place(g, station + (64.0 + 4 * g), codes(side, g, 1 - core) + (32.0 + 4 * g))

    @pl.when(takes_results)
    def _():
        in2[me] = out2[me]

        def collect(step, carry):
            g = member(step)

            @pl.when(g != me)
            def _():
                recv_wait(in2, recv_p, g)

            return carry

        lax.fori_loop(0, NGRP, collect, 0)
        for g in range(NGRP):
            unpack(g, in2[g])
        for s in range(SG):
            for i in range(3):
                outer = far_f[i, pl.ds(s, 32, stride=4), :]
                f_ref[s, 64:96, 128 * i : 128 * i + 128] = outer

    @pl.when(takes_blocks)
    def _():
        def far_columns(step, carry):
            g = member(step)
            recv_wait(far, recv_x, g)
            columns(g, far[g], 2)
            return carry

        lax.fori_loop(0, NGRP, far_columns, 0)
        for g in range(NGRP):
            far_code = codes(far, g, 0) + (64.0 + 4 * g)
            code_v[g * 12 + 4 : g * 12 + 8, :] = far_code[0:4]
        settle(2)

    @pl.when(jnp.logical_not(has_far))
    def _():
        f_ref[:, 64:96, :] = jnp.zeros((SG, 32, 384), F32)

    chosen = jnp.where(line.astype(F32) == code_v[:, 0:96], 1.0, 0.0)
    for s in range(SG):
        pick = (chosen * keep_v[s][:, 0:96]).astype(BF)
        rows = f_ref[s].astype(BF)
        left_ref[s * 96 : (s + 1) * 96, :] = dot(pick, rows).astype(BF)

    side_copy(me, blk).wait_send()

    @pl.when(gives_edge)
    def _():
        edge_copy().wait_send()

    @pl.when(gives_blocks)
    def _():
        far_copy(me, blk).wait_send()

    for j in range(NGRP - 1):
        g = peer(j)
        gather_copy(j).wait_send()
        side_copy(g, gath.at[g]).wait_send()

        @pl.when(gives_blocks)
        def _():
            far_copy(g, gath.at[g]).wait_send()

        @pl.when(takes_results)
        def _():
            result_copy(g).wait_send()

    loads[5].wait()


def lag_kernel(left_ref, basis_ref, out_hbm, out_v, sems):
    copies = []
    for i, start in enumerate(range(0, LAGS, CHUNK)):
        series = dot(left_ref[:, 0 : 2 * NBIN], basis_ref[:, start : start + CHUNK])
        stop = min(start + CHUNK, LAGS)
        series = series[:, : stop - start].reshape(SG, 96, stop - start)
        out_v[:, :, start:stop] = series.astype(BF)
        copies.append(
            pltpu.make_async_copy(
                out_v.at[:, :, start:stop], out_hbm.at[:, :, start:stop], sems.at[i]
            )
        )
        copies[-1].start()
    for copy in copies:
        copy.wait()


def on_device(n_tile, traces, validity, boundary_rows, boundary_count, pair_mask):
    dft = jnp.asarray(dft_table())
    anywhere = pl.BlockSpec(memory_space=pltpu.MemorySpace.HBM)
    dma = pltpu.SemaphoreType.DMA
    vmem = pl.BlockSpec(memory_space=pltpu.VMEM)
    basis = jnp.asarray(lag_table())
    left, basis = pl.pallas_call(
        functools.partial(cross_kernel, n_tile),
        out_shape=(
            jax.ShapeDtypeStruct((SG * 96, 384), BF),
            jax.ShapeDtypeStruct(basis.shape, BF),
        ),
        in_specs=[anywhere] * 7,
        out_specs=(vmem, vmem),
        scratch_shapes=[
            pltpu.VMEM((SG, SEG, SAMP), F32),
            pltpu.VMEM((SG, SEG), jnp.int32),
            pltpu.SMEM((1, 2, SG), jnp.int32),
            pltpu.SMEM((1, 2), jnp.int32),
            pltpu.VMEM((SG, 96), jnp.int32),
            pltpu.VMEM(dft.shape, BF),
            pltpu.VMEM((BLK, 256), BF),
            pltpu.VMEM((BLK, 256), BF),
            pltpu.VMEM((NGRP, BLK, 256), BF),
            pltpu.VMEM((NGRP, BLK, 256), BF),
            pltpu.VMEM((NGRP, BLK, 256), BF),
            pltpu.VMEM((BLK, 256), BF),
            pltpu.VMEM((2 * SG, BLK, 256), F32),
            pltpu.VMEM((2 * SG, 8, 256), F32),
            pltpu.VMEM((SG, 96, 128), F32),
            pltpu.VMEM((96, 128), F32),
            pltpu.VMEM((SG, 3, 5, 64, 128), F32),
            pltpu.VMEM((SG, 96, 384), F32),
            pltpu.VMEM((3, 128, 128), F32),
            pltpu.VMEM((NGRP, 24, 256), BF),
            pltpu.VMEM((NGRP, 24, 256), BF),
            dma((6,)), dma((len(DFT_PARTS),)),
            dma((7,)), dma((8,)), dma((8,)), dma(()), dma((8,)),
            dma((8,)), dma((8,)), dma((8,)), dma(()), dma((8,)),
        ],
        compiler_params=pltpu.CompilerParams(
            collective_id=0, has_side_effects=True, vmem_limit_bytes=24 << 20
        ),
        name="cross",
    )(*[
        pltpu.with_memory_space_constraint(array, pltpu.MemorySpace.HBM)
        for array in (
            traces, validity, boundary_rows, boundary_count, pair_mask, dft, basis
        )
    ])
    return pl.pallas_call(
        lag_kernel,
        out_shape=jax.ShapeDtypeStruct((SG, 96, LAGS), BF),
        in_specs=[vmem, vmem],
        out_specs=pl.BlockSpec(memory_space=pl.ANY),
        scratch_shapes=[
            pltpu.VMEM((SG, 96, LAGS), BF),
            pltpu.SemaphoreType.DMA((pl.cdiv(LAGS, CHUNK),)),
        ],
        compiler_params=pltpu.CompilerParams(vmem_limit_bytes=24 << 20),
        name="lags",
    )(left, basis)


def solution(mesh):
    three = P(("tile", "grp"), None, None)
    two = P(("tile", "grp"), None)
    return jax.shard_map(
        functools.partial(on_device, mesh.shape["tile"]),
        mesh=mesh,
        in_specs=(three, two, three, two, two),
        out_specs=three,
        check_vma=False,
    )
```

```python
import functools
import math

import jax
import jax.numpy as jnp
import ml_dtypes
import numpy as np
from jax import lax
from jax.experimental import pallas as pl
from jax.experimental.pallas import tpu as pltpu
from jax.sharding import PartitionSpec as P

SG = 4
SEG = 16
SAMP = 1500
NBIN = 144
MAXLAG = 1000
LAGS = 2001
NGRP = 8
MAIN = 128
ROWS = SG * SEG
BLK = ROWS + 16
CHUNK = 512
X_RUN = 8
DFT_PARTS = tuple((a, min(a + 768, SAMP)) for a in range(0, SAMP, 768))
DEAD = 128.0
BF = jnp.bfloat16
F32 = jnp.float32
MESH = pl.DeviceIdType.MESH


def split_halves(table):
    high = table.astype(ml_dtypes.bfloat16)
    low = (table - high.astype(np.float64)).astype(ml_dtypes.bfloat16)
    return high, low


def dft_table():
    n = np.arange(SAMP, dtype=np.int64)[:, None]
    k = np.arange(1, NBIN + 1, dtype=np.int64)[None, :]
    angle = ((n * k) % (2 * SAMP)).astype(np.float64) * (2.0 * np.pi / (2 * SAMP))
    taper = 0.5 - 0.5 * np.cos(2.0 * np.pi * n / SAMP)
    cos, sin = taper * np.cos(angle), -taper * np.sin(angle)
    main = np.concatenate([cos[:, :MAIN], sin[:, :MAIN]], axis=1)
    rest = np.concatenate([cos[:, MAIN:], sin[:, MAIN:]], axis=1)
    main_high, main_low = split_halves(main)
    rest_high, rest_low = split_halves(rest)
    unused = np.zeros((SAMP, 64), ml_dtypes.bfloat16)
    return np.concatenate([main_high, main_low, rest_high, rest_low, unused], axis=1)


def lag_table():
    k = np.arange(1, NBIN + 1, dtype=np.int64)[:, None]
    lag = np.arange(LAGS, dtype=np.int64)[None, :] - MAXLAG
    angle = ((k * lag) % (2 * SAMP)).astype(np.float64) * (2.0 * np.pi / (2 * SAMP))
    cos = np.cos(angle) / math.sqrt(NBIN)
    sin = -np.sin(angle) / math.sqrt(NBIN)
    table = np.concatenate([cos[:MAIN], sin[:MAIN], cos[MAIN:], sin[MAIN:]], axis=0)
    table = np.pad(table, ((0, 0), (0, -LAGS % CHUNK)))
    return table.astype(ml_dtypes.bfloat16)


def iota(shape, axis):
    return lax.broadcasted_iota(jnp.int32, shape, axis)


def dot(a, b):
    return jnp.dot(a, b, preferred_element_type=F32)


def lane_fold(a, shifts):
    for shift in shifts:
        a = a + pltpu.roll(a, shift, 1)
    return a


def bin_of(lane):
    return jnp.where(lane < MAIN, lane, MAIN + (lane & 15))


def power_weights():
    shape = (256, 256)
    source, target = iota(shape, 0), iota(shape, 1)
    near = jnp.abs(bin_of(source) - bin_of(target)) <= 4
    return jnp.where(source < MAIN + 32, jnp.where(near, 17.0, 1.0), 0.0).astype(BF)


def cross_kernel(
    n_tile, x_hbm, val_hbm, rows_hbm, cnt_hbm, mask_hbm, dft_hbm, basis_hbm,
    left_ref, basis_ref,
    x_v, val_v, rows_s, cnt_s, mask_v, dft_v, blk, edge, gath, side, far, nbin, role, turned,
    keep_v, code_v, raw, f_ref, far_f, out2, in2, load_sem, dft_sem,
    send_g, send_s, send_x, send_n, send_p, recv_g, recv_s, recv_x, recv_n, recv_p,
):
    tile, me = lax.axis_index("tile"), lax.axis_index("grp")
    my_step = lax.rem(me, 4) * 2 + me // 4
    neighbour = (tile + 1, tile - 1)
    exists = (tile < n_tile - 1, tile > 0)
    core = lax.rem(tile, 2)
    side_tile = tile + 1 - 2 * core
    far_tile = tile - 1 + 2 * core
    has_far = jnp.logical_and(far_tile >= 0, far_tile < n_tile)
    even = core == 0
    odd = core == 1
    turn = (far_tile + X_RUN) // X_RUN != (tile + X_RUN) // X_RUN
    takes_blocks = jnp.logical_and(even, jnp.logical_and(has_far, jnp.logical_not(turn)))
    gives_blocks = jnp.logical_and(odd, jnp.logical_and(has_far, jnp.logical_not(turn)))
    takes_results = jnp.logical_and(has_far, jnp.logical_or(odd, turn))
    gives_edge = jnp.logical_and(has_far, jnp.logical_or(even, turn))

    def member(step):
        return lax.rem(step, 2) * 4 + step // 2

    def near(step):
        d = jnp.where(step < 2, 4 * step, jnp.where(step < 6, 2 * step - 3, 4 * step - 22))
        return lax.rem(me // 4 + d // 4, 2) * 4 + lax.rem(lax.rem(me, 4) + lax.rem(d, 4), 4)

    def peer(j):
        return member(j + jnp.where(my_step <= j, 1, 0))

    loads = [
        pltpu.make_async_copy(src, dst, load_sem.at[i])
        for i, (src, dst) in enumerate(
            [(x_hbm, x_v), (val_hbm, val_v), (rows_hbm, rows_s), (cnt_hbm, cnt_s),
             (mask_hbm, mask_v), (basis_hbm, basis_ref)]
        )
    ]
    dft_loads = [
        pltpu.make_async_copy(dft_hbm.at[a:b], dft_v.at[a:b], dft_sem.at[i])
        for i, (a, b) in enumerate(DFT_PARTS)
    ]
    for load in loads[1:5]:
        load.start()
    loads[0].start()
    for load in dft_loads:
        load.start()

    barrier = pltpu.get_barrier_semaphore()
    for j in range(NGRP - 1):
        pl.semaphore_signal(barrier, inc=1, device_id=(tile, peer(j)), device_id_type=MESH)
    for direction in range(2):

        @pl.when(exists[direction])
        def _():
            pl.semaphore_signal(
                barrier, inc=1, device_id=(neighbour[direction], me), device_id_type=MESH
            )

    row80, col64 = iota((BLK, ROWS), 0), iota((BLK, ROWS), 1)
    head = row80 < ROWS
    same_station = (row80 & 3) == (col64 >> 4)
    segment = col64 & 15
    source = jnp.where(head, row80 >> 2, (row80 - ROWS) >> 2)
    order = same_station & (jnp.where(head, segment, segment & 3) == source)
    order = order.astype(F32).astype(BF)
    weights = power_weights()
    loads[1].wait()
    same_group = (iota((ROWS, 128), 1) >> 5) == ((iota((ROWS, 128), 0) & 15) >> 2)
    lane128 = iota((ROWS, 128), 1)
    valid_parts = []
    for s in range(SG):
        row = jnp.broadcast_to(val_v[s : s + 1, :].astype(F32), (SEG, SEG))
        diag = jnp.where(iota((SEG, SEG), 0) == iota((SEG, SEG), 1), row, 0.0)
        valid_parts.append(jnp.sum(diag, axis=1, keepdims=True))
    valid = jnp.broadcast_to(jnp.concatenate(valid_parts, axis=0), (ROWS, 128))
    valid_group = jnp.where(same_group, valid, 0.0)
    loads[2].wait()
    loads[3].wait()

    def fold_rows(a):
        return jnp.concatenate([a[0:8], a[8:16]], axis=1)

    tail = fold_rows(dot(order[ROWS:], valid_group.astype(BF)))
    tail_row, tail_lane = iota((8, 256), 0), iota((8, 256), 1)
    tail = jnp.where((tail_lane & 31) == 31, 0.0, tail)
    for direction in range(2):
        for h in range(SG):
            code = jnp.where(
                h < cnt_s[0, direction], rows_s[0, direction, h].astype(F32), DEAD
            )
            here = (tail_row == h) & (tail_lane == 31 + 32 * direction)
            tail = jnp.where(here, code, tail)

    r80, c80 = iota((BLK, BLK), 0), iota((BLK, BLK), 1)
    within = r80 & 3
    wanted = jnp.zeros((BLK, BLK), jnp.int32)
    for h in range(SG):
        chosen = jnp.where(even, rows_s[0, 1, h], rows_s[0, 0, h])
        live = h < jnp.where(even, cnt_s[0, 1], cnt_s[0, 0])
        wanted = jnp.where(within == h, jnp.where(live, chosen, SG), wanted)
    pick_far = ((r80 >> 2) == (c80 >> 2)) & ((c80 & 3) == wanted)
    pick_far = jnp.where(pick_far, 1.0, 0.0).astype(BF)

    loads[0].wait()
    x = x_v[...].reshape(ROWS, SAMP)
    x_high = x.astype(BF)
    x_low = (x - x_high.astype(F32)).astype(BF)
    x_both = jnp.concatenate([x_high, x_low], axis=0)
    for load in dft_loads:
        load.wait()
    both = dot(x_both, dft_v[...])
    loads[5].start()
    main = both[:ROWS, :256] + (both[ROWS:, :256] + both[:ROWS, 256:512])
    rest = both[:ROWS, 512:640] + jnp.where(lane128 < 32, both[ROWS:, 512:640], 0.0)
    rest = jnp.where(lane128 < 32, rest + pltpu.roll(rest, 96, 1), 0.0)
    rest = rest + pltpu.roll(rest, 32, 1)
    rest = rest + pltpu.roll(rest, 64, 1)
    real, imag = main[:, :MAIN], main[:, MAIN:]
    power = jnp.concatenate([real * real + imag * imag, rest * rest], axis=1)
    power_high = power.astype(BF)
    power_low = (power - power_high.astype(F32)).astype(BF)
    level = dot(jnp.concatenate([power_high, power_low], axis=0), weights)
    level = (level[:ROWS] + level[ROWS:]) * (1.0 / 288.0) + 1e-06
    factor = lax.rsqrt(level)
    factor_main = factor[:, :MAIN] * valid
    factor_rest = factor[:, MAIN:] * valid_group
    white = jnp.concatenate([real * factor_main, imag * factor_main], axis=1)
    white = dot(order[:ROWS], white.astype(BF))
    white_rest = fold_rows(dot(order[ROWS:], (rest * factor_rest).astype(BF)))
    own = jnp.concatenate([white, white_rest, tail], axis=0).astype(BF)
    blk[...] = own
    gath[me] = own

    edges = jnp.where(exists[0], 1, 0) + jnp.where(exists[1], 1, 0)
    pl.semaphore_wait(barrier, NGRP - 1 + edges)

    def send(src, dst, send_sem, recv_sem, to_tile, to_member):
        return pltpu.make_async_remote_copy(
            src_ref=src, dst_ref=dst, send_sem=send_sem, recv_sem=recv_sem,
            device_id=(to_tile, to_member), device_id_type=MESH,
        )

    def gather_copy(j):
        return send(blk, gath.at[me], send_g.at[j], recv_g.at[me], tile, peer(j))

    def side_copy(g, src):
        return send(src, side.at[g], send_s.at[g], recv_s.at[g], side_tile, me)

    def far_copy(g, src):
        return send(src, far.at[g], send_x.at[g], recv_x.at[g], far_tile, me)

    def edge_copy():
        return send(edge, nbin, send_n, recv_n, far_tile, me)

    def result_copy(g):
        return send(out2.at[g], in2.at[me], send_p.at[g], recv_p.at[me], tile, g)

    on_turn = jnp.logical_and(has_far, turn)

    @pl.when(gives_edge)
    def _():
        edge[...] = dot(pick_far, own).astype(BF)
        edge_copy().start()

    @pl.when(gives_blocks)
    def _():
        far_copy(me, blk).start()

    for j in range(NGRP - 1):
        gather_copy(j).start()

    side_copy(me, blk).start()
    row, col = iota((BLK, BLK), 0), iota((BLK, BLK), 1)
    first_half = (iota((8, 256), 1) & 31) < 16

    def set_role(first, block):
        for s in range(SG):
            spread = (col == (row >> 2) * SG + s).astype(F32).astype(BF)
            wide = dot(spread, block)
            role[first + s] = wide
            tail = wide[ROWS : ROWS + 8]
            ahead = jnp.concatenate(
                [pltpu.roll(tail[:, 0:128], 112, 1), pltpu.roll(tail[:, 128:], 112, 1)], axis=1
            )
            behind = jnp.concatenate(
                [pltpu.roll(tail[:, 0:128], 16, 1), pltpu.roll(tail[:, 128:], 16, 1)], axis=1
            )
            turned[first + s] = jnp.where(first_half, ahead, -behind)

    set_role(0, own)
    loads[4].wait()
    column, line = iota((96, 96), 0), iota((96, 96), 1)
    on_diagonal = column == line
    for s in range(SG):
        wanted = jnp.broadcast_to(mask_v[s : s + 1, :].astype(F32), (96, 96))
        kept = jnp.sum(jnp.where(on_diagonal, wanted, 0.0), axis=1, keepdims=True)
        keep_v[s] = jnp.broadcast_to(kept, (96, 128))

    lane = iota((8, 128), 1)
    last_lane = (lane & 31) == 31
    low_half = iota((8, 128), 0) < 4
    rest_real = (lane & 31) < 16

    def products(j, block):
        w_re, w_im = role[j, 0:ROWS, 0:128], role[j, 0:ROWS, 128:256]
        v_re, v_im = block[0:ROWS, 0:128], block[0:ROWS, 128:256]
        w_rest, v_rest = role[j, ROWS : ROWS + 8, :], block[ROWS : ROWS + 8]
        count = role[j, ROWS + 8 : BLK, :] * block[ROWS + 8 : BLK]
        rest_re = w_rest * v_rest
        rest_im = turned[j] * v_rest
        return [
            jnp.sum((w_re * v_re + w_im * v_im).reshape(-1, 8, 128), axis=0),
            jnp.sum((w_im * v_re - w_re * v_im).reshape(-1, 8, 128), axis=0),
            rest_re[:, 0:128] + rest_re[:, 128:],
            rest_im[:, 0:128] + rest_im[:, 128:],
            count[:, 0:128] + count[:, 128:],
        ]

    def finish(sums, sign=1.0):
        re, im, rest_re, rest_im, count = sums
        count = lane_fold(count, (64, 32))
        count = jnp.where(last_lane, pltpu.roll(count, 1, 1), count)
        inverse = 1.0 / jnp.maximum(count, 1.0)
        rest_re = lane_fold(rest_re, (64, 32, 16))
        rest_im = lane_fold(rest_im, (64, 32, 16)) * sign
        return re * inverse, im * (inverse * sign), jnp.where(rest_real, rest_re, rest_im) * inverse

    def recv_wait(buffer, sems, g):
        pltpu.make_async_copy(buffer.at[g], buffer.at[g], sems.at[g]).wait()

    def columns(g, block, kind):
        block = block.astype(F32)
        rows = pl.ds(pl.multiple_of(g * 8, 8), 8)
        for s in range(SG):
            for i, part in enumerate(products(s, block)):
                raw[s, kind, i, rows, :] = part

    def merge(first, second):
        return [
            jnp.where(low_half, a, b) + pltpu.roll(jnp.where(low_half, b, a), 4, 0)
            for a, b in zip(first, second)
        ]

    def settle(kind):
        for s in range(SG):
            for pair in range(NGRP // 2):
                parts = merge(
                    [raw[s, kind, i, 16 * pair : 16 * pair + 8, :] for i in range(5)],
                    [raw[s, kind, i, 16 * pair + 8 : 16 * pair + 16, :] for i in range(5)],
                )
                start = kind * 32 + 8 * pair
                for i, part in enumerate(finish(parts)):
                    f_ref[s, start : start + 8, 128 * i : 128 * i + 128] = part

    @pl.when(takes_results)
    def _():
        edge_copy().wait_recv()
        set_role(SG, nbin[...])

    def results(g):
        block = gath[g].astype(F32)
        packed = jnp.zeros((8, 128), F32)
        for pair in range(2):
            re, im, rest = finish(
                merge(products(SG + 2 * pair, block), products(SG + 2 * pair + 1, block)), -1.0
            )
            out2[g, 8 * pair : 8 * pair + 8, :] = jnp.concatenate([re, im], axis=1).astype(BF)
            packed = jnp.where((lane >> 5) == pair, rest, packed)
        out2[g, 16:24, :] = jnp.concatenate([packed, packed], axis=1).astype(BF)

    def own_columns(step, carry):
        g = member(step)

        @pl.when(g != me)
        def _():
            recv_wait(gath, recv_g, g)
            side_copy(g, gath.at[g]).start()

            @pl.when(gives_blocks)
            def _():
                far_copy(g, gath.at[g]).start()

        @pl.when(takes_results)
        def _():
            results(g)

            @pl.when(g != me)
            def _():
                result_copy(g).start()

        columns(g, gath[g], 0)
        return carry

    lax.fori_loop(0, NGRP, own_columns, 0)
    settle(0)

    def side_columns(step, carry):
        g = member(step)
        recv_wait(side, recv_s, g)
        columns(g, side[g], 1)
        return carry

    lax.fori_loop(0, NGRP, side_columns, 0)
    settle(1)

    def unpack(g, block):
        rows = block.astype(F32)
        start = g * 16
        for i in range(2):
            far_f[i, pl.ds(start, 16), :] = rows[0:16, 128 * i : 128 * i + 128]
        rest = rows[16:24, 0:128]
        far_f[2, pl.ds(start, 8), :] = rest
        far_f[2, pl.ds(start + 8, 8), :] = pltpu.roll(rest, 96, 1)

    def codes(buffer, g, direction):
        rows = buffer[g, ROWS + 8 : BLK, 0:128].astype(F32)
        picked = jnp.where(lane == 31 + 32 * direction, rows, 0.0)
        return jnp.broadcast_to(jnp.sum(picked, axis=1, keepdims=True), (8, 128))

    station = iota((8, 128), 0).astype(F32)

    def place(g, first, second):
        code_v[g * 12 + 4 : g * 12 + 8, :] = jnp.where(even, first, second)[0:4]
        code_v[g * 12 + 8 : g * 12 + 12, :] = jnp.where(even, second, first)[0:4]

    for g in range(NGRP):
        code_v[g * 12 : g * 12 + 4, :] = station[0:4] + 4.0 * g
        place(g, station + (64.0 + 4 * g), codes(side, g, 1 - core) + (32.0 + 4 * g))

    @pl.when(takes_results)
    def _():
        in2[me] = out2[me]

        def collect(step, carry):
            g = member(step)

            @pl.when(g != me)
            def _():
                recv_wait(in2, recv_p, g)

            return carry

        lax.fori_loop(0, NGRP, collect, 0)
        for g in range(NGRP):
            unpack(g, in2[g])
        for s in range(SG):
            for i in range(3):
                outer = far_f[i, pl.ds(s, 32, stride=4), :]
                f_ref[s, 64:96, 128 * i : 128 * i + 128] = outer

    @pl.when(takes_blocks)
    def _():
        def far_columns(step, carry):
            g = member(step)
            recv_wait(far, recv_x, g)
            columns(g, far[g], 2)
            return carry

        lax.fori_loop(0, NGRP, far_columns, 0)
        for g in range(NGRP):
            far_code = codes(far, g, 0) + (64.0 + 4 * g)
            code_v[g * 12 + 4 : g * 12 + 8, :] = far_code[0:4]
        settle(2)

    @pl.when(jnp.logical_not(has_far))
    def _():
        f_ref[:, 64:96, :] = jnp.zeros((SG, 32, 384), F32)

    chosen = jnp.where(line.astype(F32) == code_v[:, 0:96], 1.0, 0.0)
    for s in range(SG):
        pick = (chosen * keep_v[s][:, 0:96]).astype(BF)
        rows = f_ref[s].astype(BF)
        left_ref[s * 96 : (s + 1) * 96, :] = dot(pick, rows).astype(BF)

    side_copy(me, blk).wait_send()

    @pl.when(gives_edge)
    def _():
        edge_copy().wait_send()

    @pl.when(gives_blocks)
    def _():
        far_copy(me, blk).wait_send()

    for j in range(NGRP - 1):
        g = peer(j)
        gather_copy(j).wait_send()
        side_copy(g, gath.at[g]).wait_send()

        @pl.when(gives_blocks)
        def _():
            far_copy(g, gath.at[g]).wait_send()

        @pl.when(takes_results)
        def _():
            result_copy(g).wait_send()

    loads[5].wait()


def lag_kernel(left_ref, basis_ref, out_hbm, out_v, sems):
    copies = []
    for i, start in enumerate(range(0, LAGS, CHUNK)):
        series = dot(left_ref[:, 0 : 2 * NBIN], basis_ref[:, start : start + CHUNK])
        stop = min(start + CHUNK, LAGS)
        series = series[:, : stop - start].reshape(SG, 96, stop - start)
        out_v[:, :, start:stop] = series.astype(BF)
        copies.append(
            pltpu.make_async_copy(
                out_v.at[:, :, start:stop], out_hbm.at[:, :, start:stop], sems.at[i]
            )
        )
        copies[-1].start()
    for copy in copies:
        copy.wait()


def on_device(n_tile, traces, validity, boundary_rows, boundary_count, pair_mask):
    dft = jnp.asarray(dft_table())
    anywhere = pl.BlockSpec(memory_space=pltpu.MemorySpace.HBM)
    dma = pltpu.SemaphoreType.DMA
    vmem = pl.BlockSpec(memory_space=pltpu.VMEM)
    basis = jnp.asarray(lag_table())
    left, basis = pl.pallas_call(
        functools.partial(cross_kernel, n_tile),
        out_shape=(
            jax.ShapeDtypeStruct((SG * 96, 384), BF),
            jax.ShapeDtypeStruct(basis.shape, BF),
        ),
        in_specs=[anywhere] * 7,
        out_specs=(vmem, vmem),
        scratch_shapes=[
            pltpu.VMEM((SG, SEG, SAMP), F32),
            pltpu.VMEM((SG, SEG), jnp.int32),
            pltpu.SMEM((1, 2, SG), jnp.int32),
            pltpu.SMEM((1, 2), jnp.int32),
            pltpu.VMEM((SG, 96), jnp.int32),
            pltpu.VMEM(dft.shape, BF),
            pltpu.VMEM((BLK, 256), BF),
            pltpu.VMEM((BLK, 256), BF),
            pltpu.VMEM((NGRP, BLK, 256), BF),
            pltpu.VMEM((NGRP, BLK, 256), BF),
            pltpu.VMEM((NGRP, BLK, 256), BF),
            pltpu.VMEM((BLK, 256), BF),
            pltpu.VMEM((2 * SG, BLK, 256), F32),
            pltpu.VMEM((2 * SG, 8, 256), F32),
            pltpu.VMEM((SG, 96, 128), F32),
            pltpu.VMEM((96, 128), F32),
            pltpu.VMEM((SG, 3, 5, 64, 128), F32),
            pltpu.VMEM((SG, 96, 384), F32),
            pltpu.VMEM((3, 128, 128), F32),
            pltpu.VMEM((NGRP, 24, 256), BF),
            pltpu.VMEM((NGRP, 24, 256), BF),
            dma((6,)), dma((len(DFT_PARTS),)),
            dma((7,)), dma((8,)), dma((8,)), dma(()), dma((8,)),
            dma((8,)), dma((8,)), dma((8,)), dma(()), dma((8,)),
        ],
        compiler_params=pltpu.CompilerParams(
            collective_id=0, has_side_effects=True, vmem_limit_bytes=24 << 20
        ),
        name="cross",
    )(*[
        pltpu.with_memory_space_constraint(array, pltpu.MemorySpace.HBM)
        for array in (
            traces, validity, boundary_rows, boundary_count, pair_mask, dft, basis
        )
    ])
    return pl.pallas_call(
        lag_kernel,
        out_shape=jax.ShapeDtypeStruct((SG, 96, LAGS), BF),
        in_specs=[vmem, vmem],
        out_specs=pl.BlockSpec(memory_space=pl.ANY),
        scratch_shapes=[
            pltpu.VMEM((SG, 96, LAGS), BF),
            pltpu.SemaphoreType.DMA((pl.cdiv(LAGS, CHUNK),)),
        ],
        compiler_params=pltpu.CompilerParams(vmem_limit_bytes=24 << 20),
        name="lags",
    )(left, basis)


def solution(mesh):
    three = P(("tile", "grp"), None, None)
    two = P(("tile", "grp"), None)
    return jax.shard_map(
        functools.partial(on_device, mesh.shape["tile"]),
        mesh=mesh,
        in_specs=(three, two, three, two, two),
        out_specs=three,
        check_vma=False,
    )
```
